32 devices in a mesh: section: 2 (over x), dp: 4 (over z), mp: 4 (over y, core).
Axes of the slice: x: 2, y: 2, z: 4, core: 2. Of those that a mesh axis runs over, the one named last changes fastest.
Arguments:
- w_query: bfloat16 [2, 4096, 4096], P('section', None, 'mp'), may hold values from -0.09375 to 0.09375
- w_key: bfloat16 [2, 4096, 1024], P('section', None, 'mp'), may hold values from -0.09375 to 0.09375
- w_value: bfloat16 [2, 4096, 1024], P('section', None, 'mp'), may hold values from -0.09375 to 0.09375
- w_out: bfloat16 [2, 4096, 4096], P('section', 'mp'), may hold values from -0.09375 to 0.09375
- norm_gain: bfloat16 [2, 4096], P('section', 'mp'), may hold values from 0.099609375 to 1.8984375
- saved_input: bfloat16 [2, 2, 4, 64, 4096], P('section', None, 'dp', None, 'mp'), may hold values from -6 to 6
- saved_query: bfloat16 [2, 2, 4, 64, 4096], P('section', None, 'dp', None, 'mp'), may hold values from -5 to 5
- saved_key: bfloat16 [2, 2, 4, 64, 1024], P('section', None, 'dp', None, 'mp'), may hold values from -5 to 5
- saved_value: bfloat16 [2, 2, 4, 64, 1024], P('section', None, 'dp', None, 'mp'), may hold values from -6 to 6
- grad_in: bfloat16 [2, 4, 64, 4096], P('section', 'dp', None, 'mp'), may hold values from -0.29882812 to 0.29882812
- fresh_grad: bfloat16 [1, 4, 64, 4096], P(None, 'dp', None, 'mp'), may hold values from -0.29882812 to 0.29882812
- features: bfloat16 [2, 4, 16, 7680], P(None, 'dp', None, 'section'), may hold values from -6 to 6
- image_pos: int32 [2, 4, 16], P(None, 'dp'), may hold values from 0 to 63, as said below
Outputs:
- proj_grad: bfloat16 [7680, 4096], P(('section', 'dp'), 'mp')
- pending: bfloat16 [2, 4, 64, 4096], P('section', 'dp', None, 'mp')
The draws below stay inside these ranges and needn't reach their ends.
Inputs may be any that keep to these rules, and one draw needn't show every extreme that they name: `image_pos`: each row holds 16 consecutive ascending positions; the first row starts at 0 and the last ends at 63.
All inputs are finite; a program needn't handle non-finite values.
Results may differ from the reference program's by a relative error of at most 0.017.
Values may be sent and summed in bfloat16 or wider, within the bound.
A program may use at most 64 MiB of HBM per device.

```python
import jax
import jax.numpy as jnp
from jax import lax

D = 4096
HEADS = 32
KVH = 8
HD = 128
VF = 7680
L = 64
IMG = 16
TICKS = 2
QW = 4096
KW = 1024
NSEQ = 4
N_SECTION = 2
N_MP = 4


def score_pair(key):
    keys = jax.random.split(jax.random.fold_in(key, 7), 2)
    group = HEADS // KVH
    key_arr = jnp.clip(jax.random.normal(keys[0], (N_SECTION, TICKS, NSEQ, L, KVH, HD), jnp.float32), -5.0, 5.0)
    query_arr = jnp.clip(jax.random.normal(keys[1], (N_SECTION, TICKS, NSEQ, L, KVH, group, HD), jnp.float32), -5.0, 5.0)
    return (query_arr.reshape(N_SECTION, TICKS, NSEQ, L, HEADS * HD), key_arr.reshape(N_SECTION, TICKS, NSEQ, L, KVH * HD))


def draw_saved_query(key, part):
    return score_pair(key)[0].astype(jnp.bfloat16)


def draw_saved_key(key, part):
    return score_pair(key)[1].astype(jnp.bfloat16)


def draw_image_pos(key, part):
    count = TICKS * NSEQ
    starts = jax.random.randint(jax.random.fold_in(key, 3), (count,), 0, L - IMG + 1)
    starts = starts.at[0].set(0).at[count - 1].set(L - IMG)
    starts = starts.reshape(TICKS, NSEQ)
    return (starts[:, :, None] + jnp.arange(IMG)[None, None, :]).astype(jnp.int32)


def levels(key, extent, shards, low, top_value):
    def one(axis_at, blocks):
        draws = jax.random.uniform(jax.random.fold_in(jax.random.fold_in(key, 6), axis_at), (blocks,), jnp.float32, low / len(shards), top_value / len(shards))
        return jnp.repeat(jnp.exp(draws), extent[axis_at] // blocks).reshape((-1,) + (1,) * (len(extent) - axis_at - 1))

    factor_of = one(*shards[0])
    for cut in shards[1:]:
        factor_of = factor_of * one(*cut)
    return factor_of


def centred(own_key, dims, deviation, bound, pieces=(), held_as=jnp.bfloat16):
    level = levels(own_key, dims, pieces, -0.22, 0.18) if pieces else 1.0
    entries = jax.random.normal(own_key, dims, jnp.float32) * deviation * level
    return jnp.minimum(jnp.maximum(entries, -bound), bound).astype(held_as)


def setup_inputs(seed: int = 0) -> dict:
    key_of = jax.random.split(jax.random.key(seed), 14)
    w_query = centred(key_of[0], (N_SECTION, D, QW), D ** -0.5, 0.09375, ((0, 2), (2, 4)))
    w_key = centred(key_of[1], (N_SECTION, D, KW), D ** -0.5, 0.09375, ((0, 2), (2, 4)))
    w_value = centred(key_of[2], (N_SECTION, D, KW), D ** -0.5, 0.09375, ((0, 2), (2, 4)))
    w_out = centred(key_of[3], (N_SECTION, QW, D), QW ** -0.5, 0.09375, ((0, 2), (1, 4)))
    norm_gain = jnp.clip(1.0 + 0.18 * jax.random.normal(key_of[4], (N_SECTION, D), jnp.float32), 0.099609375, 1.8984375).astype(jnp.bfloat16)
    saved_input = centred(key_of[5], (N_SECTION, TICKS, NSEQ, L, D), 1.0, 6.0, ((0, 2), (2, 4), (4, 4)))
    saved_query = draw_saved_query(jax.random.fold_in(key_of[13], 71), 0)
    saved_key = draw_saved_key(jax.random.fold_in(key_of[13], 71), 0)
    saved_value = centred(key_of[8], (N_SECTION, TICKS, NSEQ, L, KW), 1.0, 6.0, ((0, 2), (2, 4), (4, 4)))
    grad_in = centred(key_of[9], (N_SECTION, NSEQ, L, D), 0.05, 0.29882812, ((0, 2), (1, 4), (3, 4)))
    fresh_grad = centred(key_of[10], (TICKS - 1, NSEQ, L, D), 0.05, 0.29882812, ((1, 4), (3, 4)))
    features = centred(key_of[11], (TICKS, NSEQ, IMG, VF), 1.0, 6.0, ((1, 4), (3, 2)))
    image_pos = draw_image_pos(jax.random.fold_in(key_of[13], 71), 0)
    return {"w_query": w_query, "w_key": w_key, "w_value": w_value, "w_out": w_out, "norm_gain": norm_gain, "saved_input": saved_input, "saved_query": saved_query, "saved_key": saved_key, "saved_value": saved_value, "grad_in": grad_in, "fresh_grad": fresh_grad, "features": features, "image_pos": image_pos}


def to_half(value):
    return lax.optimization_barrier(value.astype(jnp.bfloat16)).astype(jnp.float32)

def segment_back(grad, x_saved, gain, w_q, w_k, w_v, w_o, query, key_in, value):
    seq_len = grad.shape[0]
    group = HEADS // KVH
    scale = HD ** (-0.5)
    d_attn = jnp.dot(grad, w_o.T, preferred_element_type=jnp.float32).astype(jnp.bfloat16)
    q_four = query.astype(jnp.float32).reshape(seq_len, KVH, group, HD)
    k_three = key_in.astype(jnp.float32).reshape(seq_len, KVH, HD)
    v_three = value.astype(jnp.float32).reshape(seq_len, KVH, HD)
    a_four = d_attn.astype(jnp.float32).reshape(seq_len, KVH, group, HD)
    scores = jnp.einsum('lgjd,mgd->gjlm', q_four, k_three) * scale
    rows = jnp.arange(seq_len)[:, None]
    cols = jnp.arange(seq_len)[None, :]
    scores = jnp.where(cols <= rows, scores, -1e+30)
    top = lax.optimization_barrier(jnp.max(scores, -1, keepdims=True))
    expo = jnp.exp(scores - top)
    probs = expo / lax.optimization_barrier(jnp.sum(expo, -1, keepdims=True))
    d_probs = jnp.einsum('lgjd,mgd->gjlm', a_four, v_three)
    inner = lax.optimization_barrier(jnp.sum(probs * d_probs, -1, keepdims=True))
    d_scores = to_half(probs * (d_probs - inner) * scale)
    probs_half = to_half(probs)
    d_query = jnp.einsum('gjlm,mgd->lgjd', d_scores, k_three).astype(jnp.bfloat16).reshape(seq_len, QW)
    d_key = jnp.einsum('gjlm,lgjd->mgd', d_scores, q_four).astype(jnp.bfloat16).reshape(seq_len, KW)
    d_value = jnp.einsum('gjlm,lgjd->mgd', probs_half, a_four).astype(jnp.bfloat16).reshape(seq_len, KW)
    parts = N_MP
    term = jnp.einsum('lnc,dnc->nld', d_query.astype(jnp.float32).reshape(seq_len, parts, QW // parts), w_q.astype(jnp.float32).reshape(D, parts, QW // parts))
    term = term + jnp.einsum('lnc,dnc->nld', d_key.astype(jnp.float32).reshape(seq_len, parts, KW // parts), w_k.astype(jnp.float32).reshape(D, parts, KW // parts))
    term = term + jnp.einsum('lnc,dnc->nld', d_value.astype(jnp.float32).reshape(seq_len, parts, KW // parts), w_v.astype(jnp.float32).reshape(D, parts, KW // parts))
    d_normed = lax.optimization_barrier(jnp.sum(to_half(term), axis=0))
    x_float = x_saved.astype(jnp.float32)
    rstd = lax.rsqrt(lax.optimization_barrier(jnp.mean(x_float * x_float, -1, keepdims=True)) + 1e-05)
    weighted = gain.astype(jnp.float32) * d_normed
    cross = lax.optimization_barrier(jnp.mean(x_float * weighted, -1, keepdims=True))
    d_input = rstd * weighted - x_float * rstd ** 3 * cross
    return (grad.astype(jnp.float32) + d_input).astype(jnp.bfloat16)

def reference(w_query, w_key, w_value, w_out, norm_gain, saved_input, saved_query, saved_key, saved_value, grad_in, fresh_grad, features, image_pos):
    per_seq = jax.vmap(segment_back, in_axes=(0, 0, None, None, None, None, None, 0, 0, 0))

    def one_layer(layer):
        grad, x_saved, gain, w_q, w_k, w_v, w_o, query, key_in, value = layer
        return per_seq(grad, x_saved, gain, w_q, w_k, w_v, w_o, query, key_in, value)

    def run_tick(grads, tick):
        return lax.map(one_layer, (grads, saved_input[:, tick], norm_gain, w_query, w_key, w_value, w_out, saved_query[:, tick], saved_key[:, tick], saved_value[:, tick]))
    produced = run_tick(grad_in, 0)
    total = jnp.zeros((VF, D), jnp.float32)
    for tick in range(TICKS):
        if tick > 0:
            incoming = jnp.concatenate([produced[1:], fresh_grad[tick - 1][None]], axis=0)
            produced = run_tick(incoming, tick)
        picked = jnp.take_along_axis(produced[0], image_pos[tick].astype(jnp.int32)[:, :, None], axis=1)
        total = total + jnp.einsum('nif,nid->fd', features[tick].astype(jnp.float32), picked.astype(jnp.float32))
    return (total.astype(jnp.bfloat16), produced)
```

```python
import functools

import jax
import jax.numpy as jnp
from jax import lax
from jax.experimental import pallas as pl
from jax.experimental.pallas import tpu as pltpu
from jax.sharding import PartitionSpec as P

HD = 128
LANES = 128
TICKS = 2
MESH = pl.DeviceIdType.MESH
LAST = (((1,), (1,)), ((), ()))
FIRST = (((0,), (0,)), ((), ()))
PLAIN = (((1,), (0,)), ((), ()))


def mul(a, b, dims):
    return lax.dot_general(a, b, dims, preferred_element_type=jnp.float32)


def lane_sum(a):
    parts = [a[:, i : i + LANES] for i in range(0, a.shape[1], LANES)]
    return functools.reduce(lambda p, q: p + q, parts)


def kernel(
    n_section, n_dp, n_mp, chunks, direct, groups,
    wq, wk, wv, wo, gain, x, q, k, v, g_in, fresh, feat, pos,
    feat_all, picks, pending,
    wq_s, wk_s, wv_s, wo_s, gain_s, x_s, q_s, k_s, v_s, g_s, feat_s, cut_s, pos_s,
    probs_s, attn_s, dq_s, dk_s, dv_s, out_s, send_s, recv_s, term_s,
    scaled_s, upper_s, proj_s, fix_s, cross_s, cross_r, square_s, square_r, factor_s, factor_r,
    load_sem, g_sem, fresh_sem, wo_sem, wq_sem, wk_sem, wv_sem,
    ag_send, ag_recv, xg_send, xg_recv, up_send, up_recv, rs_send, rs_recv, cr_send, cr_recv,
    sq_send, sq_recv, fc_send, fc_recv,
    held_send, held_recv, far_send, ft_send, ft_recv, px_send, px_recv, pz_send, pz_recv,
):
    section = lax.axis_index("section")
    seq = lax.axis_index("dp")
    me = lax.axis_index("mp")
    y, core = me // 2, me % 2
    partner = 2 * y + (1 - core)
    across = 2 * (1 - y) + core
    diag = 2 * (1 - y) + (1 - core)
    length = g_in.shape[2]
    width = g_in.shape[3]
    depth = width * n_mp
    kw = k.shape[4]
    kv_local = kw // HD
    group = q.shape[4] // kw
    scale = HD ** (-0.5)
    f32, bf16 = jnp.float32, jnp.bfloat16
    last = n_section - 1

    def remote(src, dst, ssem, rsem, where):
        return pltpu.make_async_remote_copy(
            src_ref=src, dst_ref=dst, send_sem=ssem, recv_sem=rsem,
            device_id=where, device_id_type=MESH,
        )

    loads = {}

    def load(name, src, dst, sem):
        loads[name] = pltpu.make_async_copy(src, dst, sem)
        loads[name].start()

    cw = width // chunks
    spans = [pl.ds(c * cw, cw) for c in range(chunks)]
    for c in range(chunks):
        load(f"g{c}", g_in.at[0, 0, :, spans[c]], g_s.at[0, me, c], g_sem.at[c])
    load("x1", x.at[0, 1, 0], x_s.at[1], load_sem.at[3])
    load("gain", gain, gain_s, load_sem.at[2])
    load("x0", x.at[0, 0, 0], x_s.at[0], load_sem.at[1])
    load("q", q.at[0, :, 0], q_s, load_sem.at[4])
    load("k", k.at[0, :, 0], k_s, load_sem.at[5])
    load("v", v.at[0, :, 0], v_s, load_sem.at[6])
    load("feat", feat.at[:, 0], feat_s, load_sem.at[7])
    load("pos", pos.at[:, 0], pos_s, load_sem.at[8])

    def fresh_copy(c):
        return pltpu.make_async_copy(
            fresh.at[0, 0, :, spans[c]], g_s.at[1, me, c], fresh_sem.at[c]
        )

    @pl.when(section == last)
    def _():
        for c in range(chunks):
            fresh_copy(c).start()

    order = (me, partner, across, diag)
    for i, b in enumerate(order):
        columns = pl.ds(pl.multiple_of(b * width, width), width)
        load(f"wo{i}", wo.at[0, :, columns], wo_s.at[b], wo_sem.at[i])
    barrier = pltpu.get_barrier_semaphore()
    for b in (partner, across, diag):
        pl.semaphore_signal(barrier, inc=1, device_id={"mp": b}, device_id_type=MESH)
    for o in range(1, n_dp):
        pl.semaphore_signal(
            barrier, inc=1, device_id={"dp": (seq + o) % n_dp}, device_id_type=MESH
        )
    greets = n_mp - 1 + n_dp - 1 + n_section - 1
    for o in range(1, n_section):
        other = (section + o) % n_section
        pl.semaphore_signal(
            barrier, inc=1, device_id={"section": other}, device_id_type=MESH
        )
        pl.semaphore_signal(
            barrier, inc=1, device_id={"section": other, "mp": across}, device_id_type=MESH
        )
        greets += 1
    pl.semaphore_wait(barrier, greets)

    def block_copy(ref, ssem, rsem, where):
        return remote(ref, ref, ssem, rsem, {"mp": where})

    def chunk_copy(t, slot, c, which, where):
        return block_copy(g_s.at[t, slot, c], ag_send.at[t, c, which], ag_recv.at[t, c, which], where)

    def scaled_copy(slot, which, where):
        return block_copy(scaled_s.at[slot], xg_send.at[which], xg_recv.at[which], where)

    def upper_copy(far):
        where = {"section": section - 1}
        if far:
            where["mp"] = across
        return remote(
            x_s.at[0], upper_s.at[me], up_send.at[far], up_recv.at[far], where
        )

    def upper_near(slot, which):
        return block_copy(upper_s.at[slot], up_send.at[2 + which], up_recv.at[2 + which], partner)

    for c in range(chunks):
        loads[f"g{c}"].wait()
        chunk_copy(0, me, c, 1, across).start()
        chunk_copy(0, me, c, 0, partner).start()
    for i, b in enumerate((diag, across, partner, me)):
        rows = pl.ds(pl.multiple_of(b * width, width), width)
        load(f"wk{i}", wk.at[0, rows], wk_s.at[b], wk_sem.at[i])
        load(f"wv{i}", wv.at[0, rows], wv_s.at[b], wv_sem.at[i])
        load(f"wq{i}", wq.at[0, rows], wq_s.at[b], wq_sem.at[i])

    loads["x0"].wait()
    loads["x1"].wait()
    loads["gain"].wait()
    gains = gain_s[...].astype(f32)
    scaled_s[me] = (x_s[1].astype(f32) * gains).astype(bf16)

    def inputs_start():
        @pl.when(section > 0)
        def _():
            upper_copy(1).start()
            upper_copy(0).start()

        scaled_copy(me, 1, across).start()
        scaled_copy(me, 0, partner).start()

    def row_lanes(total):
        padded = jnp.concatenate([total, jnp.zeros((LANES - length, LANES), f32)], axis=0)
        return jnp.broadcast_to(jnp.sum(padded.T, axis=0, keepdims=True), (8, LANES))

    def as_column(lanes):
        return jnp.broadcast_to(lanes[0:1], (LANES, LANES)).T[:length, 0:1]

    def square_copy(i, where):
        return remote(
            square_s, square_r.at[i], sq_send.at[i], sq_recv.at[i], {"mp": where}
        )

    for t in range(TICKS):
        own = x_s[t].astype(f32)
        square_s[t] = row_lanes(lane_sum(own * own))
    for i, b in enumerate((partner, across, diag)):
        square_copy(i, b).start()

    own_rows = feat_s.shape[2] // n_dp
    feat_own = pltpu.make_async_copy(cut_s.at[seq], feat_all.at[seq], load_sem.at[9])

    def feat_copy(o):
        to = (seq + o) % n_dp
        return remote(
            cut_s.at[to], feat_all.at[seq], ft_send.at[o], ft_recv.at[o], {"dp": to}
        )

    @pl.when(section == last)
    def _():
        upper_s[me] = jnp.zeros((length, width), bf16)
        fix_s[...] = jnp.zeros(fix_s.shape, f32)
        factor_r[...] = jnp.zeros(factor_r.shape, f32)

    loads["q"].wait()
    loads["k"].wait()
    loads["v"].wait()

    def stack(a, g):
        return jnp.concatenate(
            [a[:, (g * group + j) * HD : (g * group + j + 1) * HD] for j in range(group)], axis=0
        )

    rows_at = lax.rem(
        lax.broadcasted_iota(jnp.int32, (group * length, length), 0), jnp.int32(length)
    )
    cols_at = lax.broadcasted_iota(jnp.int32, (group * length, length), 1)
    causal = cols_at <= rows_at

    def softmax(t):
        for g in range(kv_local):
            kg = k_s[t, :, g * HD : (g + 1) * HD]
            scores = mul(stack(q_s[t], g), kg, LAST) * scale
            scores = jnp.where(causal, scores, -1e30)
            expo = jnp.exp(scores - jnp.max(scores, -1, keepdims=True))
            probs_s[t, g] = expo / jnp.sum(expo, -1, keepdims=True)

    for t in range(TICKS):
        softmax(t)

    def picks_second(t):
        @pl.when(section > 0)
        def _():
            remote(
                picks.at[seq, t], picks.at[seq, t], px_send.at[t, 0], px_recv.at[t],
                {"section": section},
            ).wait_recv()

        for o in range(1, n_dp):
            pick_copy(t, o).start()

    def pick_copy(t, o):
        to = (seq + o) % n_dp
        ref = picks.at[seq, t]
        return remote(ref, ref, pz_send.at[t, o], pz_recv.at[t, o], {"dp": to})

    def pick_spread(t, o):
        ref = picks.at[seq, t]
        return remote(ref, ref, px_send.at[t, o], px_recv.at[t], {"section": o})

    def rs_copy(t, i, h, where):
        part = pl.ds(*groups[h])
        return remote(
            send_s.at[t, i, part], recv_s.at[t, i, part],
            rs_send.at[t, i, h], rs_recv.at[t, i, h], {"mp": where},
        )

    def cross_copy(t, i, where):
        return remote(
            cross_s.at[t], cross_r.at[t, i], cr_send.at[t, i], cr_recv.at[t, i], {"mp": where}
        )

    def cross_start(t, total):
        cross_s[t] = row_lanes(total)
        for i, b in enumerate((across, diag, partner)):
            cross_copy(t, i, b).start()

    def cross_wait(t):
        cross = cross_s[t]
        for i in range(n_mp - 1):
            cross_copy(t, i, partner).wait_recv()
            cross += cross_r[t, i]
        return cross

    def held_copy(c):
        return remote(
            out_s.at[0, c], g_s.at[1, me, c], held_send.at[c], held_recv.at[c],
            {"section": section - 1},
        )

    def held_far(c):
        return remote(
            out_s.at[0, c], g_s.at[1, me, c], far_send.at[c], ag_recv.at[1, c, 1],
            {"section": section - 1, "mp": across},
        )

    factor_copy = remote(
        factor_s, factor_r, fc_send, fc_recv, {"section": section - 1}
    )

    def wo_part(t, b, c, n=1):
        rows = [g_s[t, b, c + i] for i in range(n)]
        lhs = rows[0] if n == 1 else jnp.concatenate(rows, axis=1)
        return mul(lhs, wo_s[b, :, c * cw : (c + n) * cw], LAST)

    def arrived(t, slot, which, c):
        chunk_copy(t, slot, c, which, partner).wait_recv()

    def forward(t, c):
        arrived(t, across, 1, c)
        chunk_copy(t, across, c, 2, partner).start()

    def project():
        scaled_copy(across, 1, partner).wait_recv()
        scaled_copy(across, 2, partner).start()
        scaled_copy(partner, 0, partner).wait_recv()
        weights = ((0, wq_s), (width, wk_s), (width + kw, wv_s))
        for at, w in weights:
            total = mul(scaled_s[me], w[me], PLAIN)
            for b in (partner, across):
                total += mul(scaled_s[b], w[b], PLAIN)
            proj_s[:, at : at + w.shape[2]] = total
        scaled_copy(diag, 2, partner).wait_recv()
        for at, w in weights:
            proj_s[:, at : at + w.shape[2]] += mul(scaled_s[diag], w[diag], PLAIN)

    def correction_first():
        upper_copy(1).wait_recv()
        upper_near(across, 1).start()
        upper_copy(0).wait_recv()
        upper_near(me, 0).start()
        total = mul(upper_s[me], wo_s[me], LAST)
        fix_s[...] = total + mul(upper_s[across], wo_s[across], LAST)

    def correction_second():
        upper_near(partner, 0).wait_recv()
        total = mul(upper_s[partner], wo_s[partner], LAST)
        upper_near(diag, 1).wait_recv()
        fix_s[...] += total + mul(upper_s[diag], wo_s[diag], LAST)

    def attention(t):
        for g in range(kv_local):
            lanes = slice(g * HD, (g + 1) * HD)
            kg, vg = k_s[t, :, lanes], v_s[t, :, lanes]
            qg = stack(q_s[t], g)
            ag = stack(attn_s[...], g)
            probs = probs_s[t, g]
            d_probs = mul(ag, vg, LAST)
            inner = jnp.sum(probs * d_probs, -1, keepdims=True)
            d_scores = (probs * (d_probs - inner) * scale).astype(bf16)
            d_query = mul(d_scores, kg, PLAIN).astype(bf16)
            for j in range(group):
                dq_s[:, (g * group + j) * HD : (g * group + j + 1) * HD] = d_query[
                    j * length : (j + 1) * length
                ]
            dk_s[:, lanes] = mul(d_scores, qg, FIRST).astype(bf16)
            dv_s[:, lanes] = mul(probs.astype(bf16), ag, FIRST).astype(bf16)

    def partial(t, i, b, low, count):
        at = slice(low * cw, (low + count) * cw)
        term = mul(dq_s[...], wq_s[b, at], LAST)
        term += mul(dk_s[...], wk_s[b, at], LAST)
        term += mul(dv_s[...], wv_s[b, at], LAST)
        return [(low + j, term[:, j * cw : (j + 1) * cw]) for j in range(count)]

    def weights_wait(t, i):
        if t == 0:
            loads[f"wk{i}"].wait()
            loads[f"wv{i}"].wait()
            loads[f"wq{i}"].wait()

    def scatter(t):
        weights_wait(t, 0)
        for h in range(len(groups)):
            for c, term in partial(t, 0, diag, *groups[h]):
                send_s[t, 0, c] = term.astype(bf16)
            rs_copy(t, 0, h, partner).start()
        weights_wait(t, 1)
        for h in range(len(groups)):
            terms = partial(t, 1, across, *groups[h])
            rs_copy(t, 0, h, partner).wait_recv()
            for c, term in terms:
                send_s[t, 1, c] = (term + recv_s[t, 0, c].astype(f32)).astype(bf16)
            rs_copy(t, 1, h, across).start()
        weights_wait(t, 2)
        for c, term in partial(t, 2, partner, 0, chunks):
            send_s[t, 2, c] = term.astype(bf16)
        for h in range(len(groups)):
            rs_copy(t, 2, h, partner).start()
        weights_wait(t, 3)
        for c, term in partial(t, 3, me, 0, chunks):
            term_s[:, c * cw : (c + 1) * cw] = term

    def rstd_lanes(t):
        squares = square_s[t] + square_r[0, t] + square_r[1, t] + square_r[2, t]
        return lax.rsqrt(squares / depth + 1e-05)

    def d_normed(t, c):
        at = slice(c * cw, (c + 1) * cw)
        return term_s[:, at] + recv_s[t, 2, c].astype(f32) + recv_s[t, 1, c].astype(f32)

    def pick(t):
        rows = jnp.concatenate([out_s[t, c] for c in range(chunks)], axis=1)
        at = lax.broadcasted_iota(jnp.int32, (length, pos_s.shape[1]), 0)
        chosen = (at == pos_s[pl.ds(t, 1), :]).astype(f32).astype(bf16)
        picks[seq, t] = mul(chosen, rows, FIRST).astype(bf16)
        for o in range(1, n_section):
            pick_spread(t, o).start()

    loads["wo0"].wait()
    d_attn = wo_part(0, me, 0, chunks)
    for c in range(chunks):
        arrived(0, partner, 0, c)
    loads["wo1"].wait()
    d_attn += wo_part(0, partner, 0, chunks)
    for c in range(chunks):
        forward(0, c)
        if c == 0:
            inputs_start()
            loads["wo2"].wait()
        d_attn += wo_part(0, across, c)
        if c > 0:
            arrived(0, diag, 2, c - 1)
            if c == 1:
                loads["wo3"].wait()
            d_attn += wo_part(0, diag, c - 1)
    arrived(0, diag, 2, chunks - 1)
    d_attn += wo_part(0, diag, chunks - 1)
    attn_s[...] = d_attn.astype(bf16)
    attention(0)
    scatter(0)
    loads["feat"].wait()
    for j in range(n_dp):
        for t in range(TICKS):
            cut_s[j, pl.ds(t * feat_s.shape[1], feat_s.shape[1]), :] = feat_s[
                t, :, j * own_rows : (j + 1) * own_rows
            ]
    feat_own.start()
    for o in range(1, n_dp):
        feat_copy(o).start()

    @pl.when(section < last)
    def _():
        project()

    for i in range(n_mp - 1):
        square_copy(i, partner).wait_recv()
    rstd = as_column(rstd_lanes(0))
    total = jnp.zeros((length, LANES), f32)
    for h, (low, count) in enumerate(groups):
        rs_copy(0, 2, h, partner).wait_recv()
        rs_copy(0, 1, h, across).wait_recv()
        for c in range(low, low + count):
            at = slice(c * cw, (c + 1) * cw)
            weighted = gains[:, at] * d_normed(0, c)
            total += lane_sum(x_s[0, :, at].astype(f32) * weighted)
            passed = g_s[0, me, c].astype(f32) + rstd * weighted
            out_s[0, c] = passed.astype(bf16)
            term_s[:, at] = passed

        @pl.when(section > 0)
        def _():
            for c in range(low, low + count):
                if c in direct:
                    held_far(c).start()
            for c in range(low, low + count):
                held_copy(c).start()

    cross_start(0, total)

    @pl.when(section == last)
    def _():
        for c in range(chunks):
            fresh_copy(c).wait()
            chunk_copy(1, me, c, 1, across).start()
            chunk_copy(1, me, c, 0, partner).start()

    def factor_make():
        rstd = rstd_lanes(0)
        factor_s[...] = rstd * rstd * rstd * (cross_wait(0) / depth)

    @pl.when(section > 0)
    def _():
        factor_make()
        factor_copy.start()

    early = [c for c in range(chunks) if c not in direct]
    late = [c for c in range(chunks) if c in direct]

    def received(c):
        held_copy(c).wait_recv()
        if c not in direct:
            chunk_copy(1, me, c, 1, across).start()
        chunk_copy(1, me, c, 0, partner).start()

    @pl.when(section < last)
    def _():
        correction_first()
        for c in early:
            received(c)
        correction_second()

    loads["pos"].wait()

    @pl.when(section == 0)
    def _():
        factor_make()
        factor = as_column(factor_s[...])
        for c in range(chunks):
            at = slice(c * cw, (c + 1) * cw)
            out_s[0, c] = (term_s[:, at] - x_s[0, :, at].astype(f32) * factor).astype(bf16)
        pick(0)

    @pl.when(section == last)
    def _():
        project()

    d_attn = jnp.zeros((length, width), f32)
    for c in early:
        d_attn += wo_part(1, me, c)
    for c in early:
        arrived(1, partner, 0, c)
        d_attn += wo_part(1, partner, c)
    for c in late:
        forward(1, c)
        d_attn += wo_part(1, across, c)
    for c in late:

        @pl.when(section < last)
        def _():
            received(c)

        d_attn += wo_part(1, me, c)
    for c in early:
        forward(1, c)
        d_attn += wo_part(1, across, c)
    for c in late:
        arrived(1, diag, 2, c)
        d_attn += wo_part(1, diag, c)
    for c in late:
        arrived(1, partner, 0, c)
        d_attn += wo_part(1, partner, c)

    @pl.when(section < last)
    def _():
        factor_copy.wait_recv()

    handed = as_column(factor_r[...])
    d_attn -= handed * fix_s[...]
    for c in early:
        arrived(1, diag, 2, c)
        d_attn += wo_part(1, diag, c)
    attn_s[...] = d_attn.astype(bf16)
    picks_second(0)
    attention(1)
    total = lane_sum(dq_s[...].astype(f32) * proj_s[:, :width])
    total += lane_sum(dk_s[...].astype(f32) * proj_s[:, width : width + kw])
    total += lane_sum(dv_s[...].astype(f32) * proj_s[:, width + kw :])
    cross_start(1, total)
    scatter(1)
    rstd = rstd_lanes(1)
    factor = as_column(rstd * rstd * rstd * (cross_wait(1) / depth))
    rstd = as_column(rstd)
    for h, (low, count) in enumerate(groups):
        rs_copy(1, 2, h, partner).wait_recv()
        rs_copy(1, 1, h, across).wait_recv()
        for c in range(low, low + count):
            at = slice(c * cw, (c + 1) * cw)
            below = g_s[1, me, c].astype(f32) - handed * upper_s[me, :, at].astype(f32)
            change = rstd * (gains[:, at] * d_normed(1, c)) - x_s[1, :, at].astype(f32) * factor
            out_s[1, c] = (below + change).astype(bf16)

    @pl.when(section == 0)
    def _():
        pick(1)

    picks_second(1)
    for c in range(chunks):
        pending[0, 0, :, c * cw : (c + 1) * cw] = out_s[1, c]

    feat_own.wait()
    for c in range(chunks):
        for which in range(3):
            chunk_copy(0, me, c, which, partner).wait_send()
        for which in (0, 2):
            chunk_copy(1, me, c, which, partner).wait_send()
        if c not in direct:
            chunk_copy(1, me, c, 1, partner).wait_send()
    for i in range(3):
        scaled_copy(me, i, partner).wait_send()
        square_copy(i, partner).wait_send()
        for t in range(TICKS):
            for h in range(len(groups)):
                rs_copy(t, i, h, partner).wait_send()
            cross_copy(t, i, partner).wait_send()

    @pl.when(section == last)
    def _():
        for c in direct:
            chunk_copy(1, me, c, 1, partner).wait_send()

    @pl.when(section < last)
    def _():
        upper_near(me, 0).wait_send()
        upper_near(me, 1).wait_send()

    @pl.when(section > 0)
    def _():
        for c in range(chunks):
            held_copy(c).wait_send()
        for c in direct:
            held_far(c).wait_send()
        upper_copy(0).wait_send()
        upper_copy(1).wait_send()
        factor_copy.wait_send()

    @pl.when(section == 0)
    def _():
        for t in range(TICKS):
            for o in range(1, n_section):
                pick_spread(t, o).wait_send()

    for o in range(1, n_dp):
        feat_copy(o).wait_send()
        source = (seq + n_dp - o) % n_dp
        remote(
            cut_s.at[seq], feat_all.at[source], ft_send.at[o], ft_recv.at[o], {"dp": source}
        ).wait_recv()
        for t in range(TICKS):
            pick_copy(t, o).wait_send()
            ref = picks.at[source, t]
            remote(ref, ref, pz_send.at[t, o], pz_recv.at[t, o], {"dp": source}).wait_recv()


def shards(
    w_query, w_key, w_value, w_out, norm_gain, saved_input, saved_query, saved_key,
    saved_value, grad_in, fresh_grad, features, image_pos, chunks=4, direct=(2, 3), groups=((0, 2), (2, 2)),
):
    n_section, n_dp, n_mp = (lax.axis_size(a) for a in ("section", "dp", "mp"))
    assert n_mp == 4
    length, width = grad_in.shape[2:]
    kw = saved_key.shape[4]
    kv_local = kw // HD
    group = width // kw
    images = features.shape[2]
    own_rows = features.shape[3] // n_dp
    f32, bf16 = jnp.float32, jnp.bfloat16
    vmem, dma = pltpu.VMEM, pltpu.SemaphoreType.DMA
    feat_all, picks, pending = pl.pallas_call(
        functools.partial(kernel, n_section, n_dp, n_mp, chunks, direct, groups),
        out_shape=(
            jax.ShapeDtypeStruct((n_dp, TICKS * images, own_rows), bf16),
            jax.ShapeDtypeStruct((n_dp, TICKS, images, width), bf16),
            jax.ShapeDtypeStruct((1, 1, length, width), bf16),
        ),
        in_specs=[pl.BlockSpec(memory_space=pltpu.HBM)] * 13,
        out_specs=(pl.BlockSpec(memory_space=pltpu.VMEM),) * 3,
        scratch_shapes=[
            vmem((n_mp, width, width), bf16),
            vmem((n_mp, width, kw), bf16),
            vmem((n_mp, width, kw), bf16),
            vmem((n_mp, width, width), bf16),
            vmem((1, width), bf16),
            vmem((TICKS, length, width), bf16),
            vmem((TICKS, length, width), bf16),
            vmem((TICKS, length, kw), bf16),
            vmem((TICKS, length, kw), bf16),
            vmem((TICKS, n_mp, chunks, length, width // chunks), bf16),
            vmem((TICKS, images, features.shape[3]), bf16),
            vmem((n_dp, TICKS * images, own_rows), bf16),
            vmem((TICKS, images), jnp.int32),
            vmem((TICKS, kv_local, group * length, length), f32),
            vmem((length, width), bf16),
            vmem((length, width), bf16),
            vmem((length, kw), bf16),
            vmem((length, kw), bf16),
            vmem((TICKS, chunks, length, width // chunks), bf16),
            vmem((TICKS, 3, chunks, length, width // chunks), bf16),
            vmem((TICKS, 3, chunks, length, width // chunks), bf16),
            vmem((length, width), f32),
            vmem((n_mp, length, width), bf16),
            vmem((n_mp, length, width), bf16),
            vmem((length, width + 2 * kw), f32),
            vmem((length, width), f32),
            vmem((TICKS, 8, LANES), f32),
            vmem((TICKS, 3, 8, LANES), f32),
            vmem((TICKS, 8, LANES), f32),
            vmem((3, TICKS, 8, LANES), f32),
            vmem((8, LANES), f32),
            vmem((8, LANES), f32),
            dma((10,)), dma((chunks,)), dma((chunks,)),
            dma((n_mp,)), dma((n_mp,)), dma((n_mp,)), dma((n_mp,)),
            dma((TICKS, chunks, 3)), dma((TICKS, chunks, 3)),
            dma((3,)), dma((3,)), dma((4,)), dma((4,)),
            dma((TICKS, 3, len(groups))), dma((TICKS, 3, len(groups))),
            dma((TICKS, 3)), dma((TICKS, 3)),
            dma((3,)), dma((3,)), dma(()), dma(()),
            dma((chunks,)), dma((chunks,)), dma((chunks,)),
            dma((n_dp,)), dma((n_dp,)),
            dma((TICKS, n_section)), dma((TICKS,)),
            dma((TICKS, n_dp)), dma((TICKS, n_dp)),
        ],
        compiler_params=pltpu.CompilerParams(
            collective_id=0, has_side_effects=True, vmem_limit_bytes=48 * 2**20
        ),
    )(
        *[
            pltpu.with_memory_space_constraint(a, pltpu.HBM)
            for a in (
                w_query, w_key, w_value, w_out, norm_gain, saved_input, saved_query, saved_key,
                saved_value, grad_in, fresh_grad, features, image_pos,
            )
        ]
    )
    total = lax.dot_general(
        feat_all.reshape(-1, own_rows),
        picks.reshape(-1, width),
        FIRST,
        preferred_element_type=jnp.float32,
    )
    return total.astype(bf16), pending


def solution(mesh):
    in_specs = (
        P("section", None, "mp"),
        P("section", None, "mp"),
        P("section", None, "mp"),
        P("section", "mp", None),
        P("section", "mp"),
        P("section", None, "dp", None, "mp"),
        P("section", None, "dp", None, "mp"),
        P("section", None, "dp", None, "mp"),
        P("section", None, "dp", None, "mp"),
        P("section", "dp", None, "mp"),
        P(None, "dp", None, "mp"),
        P(None, "dp", None, "section"),
        P(None, "dp", None),
    )
    out_specs = (P(("section", "dp"), "mp"), P("section", "dp", None, "mp"))
    return jax.shard_map(shards, mesh=mesh, in_specs=in_specs, out_specs=out_specs, check_vma=False)
```

```python
import functools

import jax
import jax.numpy as jnp
from jax import lax
from jax.experimental import pallas as pl
from jax.experimental.pallas import tpu as pltpu
from jax.sharding import PartitionSpec as P

HD = 128
LANES = 128
TICKS = 2
MESH = pl.DeviceIdType.MESH
LAST = (((1,), (1,)), ((), ()))
FIRST = (((0,), (0,)), ((), ()))
PLAIN = (((1,), (0,)), ((), ()))


def mul(a, b, dims):
    return lax.dot_general(a, b, dims, preferred_element_type=jnp.float32)


def lane_sum(a):
    parts = [a[:, i : i + LANES] for i in range(0, a.shape[1], LANES)]
    return functools.reduce(lambda p, q: p + q, parts)


def kernel(
    n_section, n_dp, n_mp, chunks, direct, groups,
    wq, wk, wv, wo, gain, x, q, k, v, g_in, fresh, feat, pos,
    feat_all, picks, pending,
    wq_s, wk_s, wv_s, wo_s, gain_s, x_s, q_s, k_s, v_s, g_s, feat_s, cut_s, pos_s,
    probs_s, attn_s, dq_s, dk_s, dv_s, out_s, send_s, recv_s, term_s,
    scaled_s, upper_s, proj_s, cross_s, cross_r, square_s, square_r, factor_s, factor_r, gain_r, rows_s, rows_r,
    load_sem, g_sem, fresh_sem, wo_sem, wq_sem, wk_sem, wv_sem,
    ag_send, ag_recv, xg_send, xg_recv, up_send, up_recv, rs_send, rs_recv, cr_send, cr_recv,
    sq_send, sq_recv, fc_send, fc_recv,
    gn_send, gn_recv, far_rows_send, far_rows_recv, own_rows_send, own_rows_recv,
    held_send, held_recv, far_send, ft_send, ft_recv, px_send, px_recv, pz_send, pz_recv,
):
    section = lax.axis_index("section")
    seq = lax.axis_index("dp")
    me = lax.axis_index("mp")
    y, core = me // 2, me % 2
    partner = 2 * y + (1 - core)
    across = 2 * (1 - y) + core
    diag = 2 * (1 - y) + (1 - core)
    length = g_in.shape[2]
    width = g_in.shape[3]
    depth = width * n_mp
    kw = k.shape[4]
    kv_local = kw // HD
    group = q.shape[4] // kw
    scale = HD ** (-0.5)
    f32, bf16 = jnp.float32, jnp.bfloat16
    last = n_section - 1

    def remote(src, dst, ssem, rsem, where):
        return pltpu.make_async_remote_copy(
            src_ref=src, dst_ref=dst, send_sem=ssem, recv_sem=rsem,
            device_id=where, device_id_type=MESH,
        )

    loads = {}

    def load(name, src, dst, sem):
        loads[name] = pltpu.make_async_copy(src, dst, sem)
        loads[name].start()

    cw = width // chunks
    spans = [pl.ds(c * cw, cw) for c in range(chunks)]
    for c in range(chunks):
        load(f"g{c}", g_in.at[0, 0, :, spans[c]], g_s.at[0, me, c], g_sem.at[c])
    load("x1", x.at[0, 1, 0], x_s.at[1], load_sem.at[3])
    load("gain", gain, gain_s, load_sem.at[2])
    load("x0", x.at[0, 0, 0], x_s.at[0], load_sem.at[1])
    load("q", q.at[0, :, 0], q_s, load_sem.at[4])
    load("k", k.at[0, :, 0], k_s, load_sem.at[5])
    load("v", v.at[0, :, 0], v_s, load_sem.at[6])
    load("feat", feat.at[:, 0], feat_s, load_sem.at[7])
    load("pos", pos.at[:, 0], pos_s, load_sem.at[8])

    def fresh_copy(c):
        return pltpu.make_async_copy(
            fresh.at[0, 0, :, spans[c]], g_s.at[1, me, c], fresh_sem.at[c]
        )

    @pl.when(section == last)
    def _():
        for c in range(chunks):
            fresh_copy(c).start()

    order = (me, partner, across, diag)
    for i, b in enumerate(order):
        columns = pl.ds(pl.multiple_of(b * width, width), width)
        load(f"wo{i}", wo.at[0, :, columns], wo_s.at[b], wo_sem.at[i])
    barrier = pltpu.get_barrier_semaphore()
    for b in (partner, across, diag):
        pl.semaphore_signal(barrier, inc=1, device_id={"mp": b}, device_id_type=MESH)
    for o in range(1, n_dp):
        pl.semaphore_signal(
            barrier, inc=1, device_id={"dp": (seq + o) % n_dp}, device_id_type=MESH
        )
    greets = n_mp - 1 + n_dp - 1 + n_section - 1
    for o in range(1, n_section):
        other = (section + o) % n_section
        pl.semaphore_signal(
            barrier, inc=1, device_id={"section": other}, device_id_type=MESH
        )
        pl.semaphore_signal(
            barrier, inc=1, device_id={"section": other, "mp": across}, device_id_type=MESH
        )
        greets += 1
    pl.semaphore_wait(barrier, greets)

    def block_copy(ref, ssem, rsem, where):
        return remote(ref, ref, ssem, rsem, {"mp": where})

    def chunk_copy(t, slot, c, which, where):
        return block_copy(g_s.at[t, slot, c], ag_send.at[t, c, which], ag_recv.at[t, c, which], where)

    def scaled_copy(slot, which, where):
        return block_copy(scaled_s.at[slot], xg_send.at[which], xg_recv.at[which], where)

    def upper_copy(far):
        where = {"section": section - 1}
        if far:
            where["mp"] = across
        return remote(
            x_s.at[0], upper_s.at[me], up_send.at[far], up_recv.at[far], where
        )

    def upper_near(slot, which):
        return block_copy(upper_s.at[slot], up_send.at[2 + which], up_recv.at[2 + which], partner)

    for c in range(chunks):
        loads[f"g{c}"].wait()
        chunk_copy(0, me, c, 1, across).start()
        chunk_copy(0, me, c, 0, partner).start()
    for i, b in enumerate((diag, across, partner, me)):
        rows = pl.ds(pl.multiple_of(b * width, width), width)
        load(f"wk{i}", wk.at[0, rows], wk_s.at[b], wk_sem.at[i])
        load(f"wv{i}", wv.at[0, rows], wv_s.at[b], wv_sem.at[i])
        load(f"wq{i}", wq.at[0, rows], wq_s.at[b], wq_sem.at[i])

    loads["x0"].wait()
    loads["x1"].wait()
    loads["gain"].wait()
    gains = gain_s[...].astype(f32)
    scaled_s[me] = (x_s[1].astype(f32) * gains).astype(bf16)

    def inputs_start():
        @pl.when(section > 0)
        def _():
            upper_copy(1).start()
            upper_copy(0).start()

        gain_copy.start()
        scaled_copy(me, 1, across).start()
        scaled_copy(me, 0, partner).start()

    def row_lanes(total):
        padded = jnp.concatenate([total, jnp.zeros((LANES - length, LANES), f32)], axis=0)
        return jnp.broadcast_to(jnp.sum(padded.T, axis=0, keepdims=True), (8, LANES))

    def as_column(lanes):
        return jnp.broadcast_to(lanes[0:1], (LANES, LANES)).T[:length, 0:1]

    def square_copy(i, where):
        return remote(
            square_s, square_r.at[i], sq_send.at[i], sq_recv.at[i], {"mp": where}
        )

    for t in range(TICKS):
        own = x_s[t].astype(f32)
        square_s[t] = row_lanes(lane_sum(own * own))
    for i, b in enumerate((partner, across, diag)):
        square_copy(i, b).start()

    own_rows = feat_s.shape[2] // n_dp
    feat_own = pltpu.make_async_copy(cut_s.at[seq], feat_all.at[seq], load_sem.at[9])

    def feat_copy(o):
        to = (seq + o) % n_dp
        return remote(
            cut_s.at[to], feat_all.at[seq], ft_send.at[o], ft_recv.at[o], {"dp": to}
        )

    @pl.when(section == last)
    def _():
        upper_s[...] = jnp.zeros(upper_s.shape, bf16)
        factor_r[...] = jnp.zeros(factor_r.shape, f32)

    loads["q"].wait()
    loads["k"].wait()
    loads["v"].wait()

    def stack(a, g):
        return jnp.concatenate(
            [a[:, (g * group + j) * HD : (g * group + j + 1) * HD] for j in range(group)], axis=0
        )

    rows_at = lax.rem(
        lax.broadcasted_iota(jnp.int32, (group * length, length), 0), jnp.int32(length)
    )
    cols_at = lax.broadcasted_iota(jnp.int32, (group * length, length), 1)
    causal = cols_at <= rows_at

    def softmax(t):
        for g in range(kv_local):
            kg = k_s[t, :, g * HD : (g + 1) * HD]
            scores = mul(stack(q_s[t], g), kg, LAST) * scale
            scores = jnp.where(causal, scores, -1e30)
            expo = jnp.exp(scores - jnp.max(scores, -1, keepdims=True))
            probs_s[t, g] = expo / jnp.sum(expo, -1, keepdims=True)

    for t in range(TICKS):
        softmax(t)

    def pick_copy(t, o):
        to = (seq + o) % n_dp
        ref = picks.at[seq, t]
        return remote(ref, ref, pz_send.at[t, o], pz_recv.at[t, o], {"dp": to})

    def pick_spread(o):
        ref = picks.at[seq, 0]
        return remote(ref, ref, px_send.at[o], px_recv, {"section": o})

    def far_rows(o):
        return remote(
            rows_s.at[0], rows_r.at[0], far_rows_send.at[o], far_rows_recv,
            {"section": o, "mp": across},
        )

    def own_rows_copy(o):
        return remote(
            rows_s.at[1], rows_r.at[1], own_rows_send.at[o], own_rows_recv, {"section": o}
        )

    gain_copy = remote(gain_s, gain_r, gn_send, gn_recv, {"mp": across})

    def chosen(t):
        at = lax.broadcasted_iota(jnp.int32, (length, pos_s.shape[1]), 0)
        return (at == pos_s[pl.ds(t, 1), :]).astype(f32).astype(bf16)

    def rs_copy(t, i, h, where):
        part = pl.ds(*groups[h])
        return remote(
            send_s.at[t, i, part], recv_s.at[t, i, part],
            rs_send.at[t, i, h], rs_recv.at[t, i, h], {"mp": where},
        )

    def cross_copy(t, i, where):
        return remote(
            cross_s.at[t], cross_r.at[t, i], cr_send.at[t, i], cr_recv.at[t, i], {"mp": where}
        )

    def cross_start(t, total):
        cross_s[t] = row_lanes(total)
        for i, b in enumerate((across, diag, partner)):
            cross_copy(t, i, b).start()

    def cross_wait(t):
        cross = cross_s[t]
        for i in range(n_mp - 1):
            cross_copy(t, i, partner).wait_recv()
            cross += cross_r[t, i]
        return cross

    def held_copy(c):
        return remote(
            out_s.at[0, c], g_s.at[1, me, c], held_send.at[c], held_recv.at[c],
            {"section": section - 1},
        )

    def held_far(c):
        return remote(
            out_s.at[0, c], g_s.at[1, me, c], far_send.at[c], ag_recv.at[1, c, 1],
            {"section": section - 1, "mp": across},
        )

    factor_copy = remote(
        factor_s, factor_r, fc_send, fc_recv, {"section": section - 1}
    )

    def wo_part(t, b, c, n=1):
        rows = [g_s[t, b, c + i] for i in range(n)]
        lhs = rows[0] if n == 1 else jnp.concatenate(rows, axis=1)
        return mul(lhs, wo_s[b, :, c * cw : (c + n) * cw], LAST)

    def arrived(t, slot, which, c):
        chunk_copy(t, slot, c, which, partner).wait_recv()

    def forward(t, c):
        arrived(t, across, 1, c)
        chunk_copy(t, across, c, 2, partner).start()

    def project():
        scaled_copy(across, 1, partner).wait_recv()
        scaled_copy(across, 2, partner).start()
        scaled_copy(partner, 0, partner).wait_recv()
        weights = ((0, wq_s), (width, wk_s), (width + kw, wv_s))
        for at, w in weights:
            total = mul(scaled_s[me], w[me], PLAIN)
            for b in (partner, across):
                total += mul(scaled_s[b], w[b], PLAIN)
            proj_s[:, at : at + w.shape[2]] = total
        scaled_copy(diag, 2, partner).wait_recv()
        for at, w in weights:
            proj_s[:, at : at + w.shape[2]] += mul(scaled_s[diag], w[diag], PLAIN)

    def uppers_forward():
        upper_copy(1).wait_recv()
        upper_near(across, 1).start()
        upper_copy(0).wait_recv()
        upper_near(me, 0).start()

    def uppers_wait():
        upper_near(partner, 0).wait_recv()
        upper_near(diag, 1).wait_recv()

    def stacked(b, c, n):
        lhs = jnp.concatenate([g_s[1, b, c + i] for i in range(n)], axis=1)
        at = slice(c * cw, (c + n) * cw)
        both = jnp.concatenate([lhs, upper_s[b, :, at]], axis=0)
        return mul(both, wo_s[b, :, at], LAST)

    def attention(t):
        for g in range(kv_local):
            lanes = slice(g * HD, (g + 1) * HD)
            kg, vg = k_s[t, :, lanes], v_s[t, :, lanes]
            qg = stack(q_s[t], g)
            ag = stack(attn_s[...], g)
            probs = probs_s[t, g]
            d_probs = mul(ag, vg, LAST)
            inner = jnp.sum(probs * d_probs, -1, keepdims=True)
            d_scores = (probs * (d_probs - inner) * scale).astype(bf16)
            d_query = mul(d_scores, kg, PLAIN).astype(bf16)
            for j in range(group):
                dq_s[:, (g * group + j) * HD : (g * group + j + 1) * HD] = d_query[
                    j * length : (j + 1) * length
                ]
            dk_s[:, lanes] = mul(d_scores, qg, FIRST).astype(bf16)
            dv_s[:, lanes] = mul(probs.astype(bf16), ag, FIRST).astype(bf16)

    def partial(t, i, b, low, count):
        at = slice(low * cw, (low + count) * cw)
        term = mul(dq_s[...], wq_s[b, at], LAST)
        term += mul(dk_s[...], wk_s[b, at], LAST)
        term += mul(dv_s[...], wv_s[b, at], LAST)
        return [(low + j, term[:, j * cw : (j + 1) * cw]) for j in range(count)]

    def weights_wait(t, i):
        if t == 0:
            loads[f"wk{i}"].wait()
            loads[f"wv{i}"].wait()
            loads[f"wq{i}"].wait()

    def scatter(t):
        weights_wait(t, 0)
        for h in range(len(groups)):
            for c, term in partial(t, 0, diag, *groups[h]):
                send_s[t, 0, c] = term.astype(bf16)
            rs_copy(t, 0, h, partner).start()
        weights_wait(t, 1)
        for h in range(len(groups)):
            terms = partial(t, 1, across, *groups[h])
            rs_copy(t, 0, h, partner).wait_recv()
            for c, term in terms:
                send_s[t, 1, c] = (term + recv_s[t, 0, c].astype(f32)).astype(bf16)
            if t == 0:
                rs_copy(t, 1, h, across).start()
        if t == 1:

            @pl.when(section == 0)
            def _():
                sums = jnp.concatenate([send_s[1, 1, c] for c in range(chunks)], axis=1)
                sums = as_column(rstd_lanes(1)) * (gain_r[...].astype(f32) * sums.astype(f32))
                rows_s[0] = mul(chosen(1), sums.astype(bf16), FIRST).astype(bf16)
                for o in range(n_section - 1, -1, -1):
                    far_rows(o).start()

            for h in range(len(groups)):
                rs_copy(t, 1, h, across).start()
        weights_wait(t, 2)
        for c, term in partial(t, 2, partner, 0, chunks):
            send_s[t, 2, c] = term.astype(bf16)
        for h in range(len(groups)):
            rs_copy(t, 2, h, partner).start()
        weights_wait(t, 3)
        for c, term in partial(t, 3, me, 0, chunks):
            term_s[:, c * cw : (c + 1) * cw] = term

    def rstd_lanes(t):
        squares = square_s[t] + square_r[0, t] + square_r[1, t] + square_r[2, t]
        return lax.rsqrt(squares / depth + 1e-05)

    def d_normed(t, c):
        at = slice(c * cw, (c + 1) * cw)
        return term_s[:, at] + recv_s[t, 2, c].astype(f32) + recv_s[t, 1, c].astype(f32)

    def pick_first():
        rows = jnp.concatenate([out_s[0, c] for c in range(chunks)], axis=1)
        picks[seq, 0] = mul(chosen(0), rows, FIRST).astype(bf16)
        for o in range(1, n_section):
            pick_spread(o).start()

    def picks_join(own):
        far_rows(0).wait_recv()
        picks[seq, 1] = (own.astype(f32) + rows_r[0].astype(f32)).astype(bf16)
        for o in range(1, n_dp):
            pick_copy(1, o).start()

    loads["wo0"].wait()
    d_attn = wo_part(0, me, 0, chunks)
    for c in range(chunks):
        arrived(0, partner, 0, c)
    loads["wo1"].wait()
    d_attn += wo_part(0, partner, 0, chunks)
    for c in range(chunks):
        forward(0, c)
        if c == 0:
            inputs_start()
            loads["wo2"].wait()
        d_attn += wo_part(0, across, c)
        if c > 0:
            arrived(0, diag, 2, c - 1)
            if c == 1:
                loads["wo3"].wait()
            d_attn += wo_part(0, diag, c - 1)
    arrived(0, diag, 2, chunks - 1)
    d_attn += wo_part(0, diag, chunks - 1)
    attn_s[...] = d_attn.astype(bf16)
    attention(0)
    scatter(0)
    loads["feat"].wait()
    for j in range(n_dp):
        for t in range(TICKS):
            cut_s[j, pl.ds(t * feat_s.shape[1], feat_s.shape[1]), :] = feat_s[
                t, :, j * own_rows : (j + 1) * own_rows
            ]
    feat_own.start()
    for o in range(1, n_dp):
        feat_copy(o).start()

    for i in range(n_mp - 1):
        square_copy(i, partner).wait_recv()
    rstd = as_column(rstd_lanes(0))
    total = jnp.zeros((length, LANES), f32)
    for h, (low, count) in enumerate(groups):
        rs_copy(0, 2, h, partner).wait_recv()
        rs_copy(0, 1, h, across).wait_recv()
        for c in range(low, low + count):
            at = slice(c * cw, (c + 1) * cw)
            weighted = gains[:, at] * d_normed(0, c)
            total += lane_sum(x_s[0, :, at].astype(f32) * weighted)
            passed = g_s[0, me, c].astype(f32) + rstd * weighted
            out_s[0, c] = passed.astype(bf16)
            term_s[:, at] = passed

        @pl.when(section > 0)
        def _():
            for c in range(low, low + count):
                if c in direct:
                    held_far(c).start()
            for c in range(low, low + count):
                held_copy(c).start()

    cross_start(0, total)

    @pl.when(section == last)
    def _():
        for c in range(chunks):
            fresh_copy(c).wait()
            chunk_copy(1, me, c, 1, across).start()
            chunk_copy(1, me, c, 0, partner).start()
        project()

    def factor_make():
        rstd = rstd_lanes(0)
        factor_s[...] = rstd * rstd * rstd * (cross_wait(0) / depth)

    @pl.when(section > 0)
    def _():
        factor_make()
        factor_copy.start()

    early = [c for c in range(chunks) if c not in direct]
    late = [c for c in range(chunks) if c in direct]

    def received(c):
        held_copy(c).wait_recv()
        if c not in direct:
            chunk_copy(1, me, c, 1, across).start()
        chunk_copy(1, me, c, 0, partner).start()

    @pl.when(section < last)
    def _():
        uppers_forward()
        project()
        uppers_wait()
        for c in early:
            received(c)

    loads["pos"].wait()

    pair = stacked(me, early[0], len(early))
    for c in early:
        arrived(1, partner, 0, c)
    pair += stacked(partner, early[0], len(early))
    for c in late:
        forward(1, c)
    pair += stacked(across, late[0], len(late))
    @pl.when(section == 0)
    def _():
        factor_make()
        factor = as_column(factor_s[...])
        for c in range(chunks):
            at = slice(c * cw, (c + 1) * cw)
            out_s[0, c] = (term_s[:, at] - x_s[0, :, at].astype(f32) * factor).astype(bf16)
        pick_first()

    for c in late:
        arrived(1, diag, 2, c)
    pair += stacked(diag, late[0], len(late))
    for c in late:

        @pl.when(section < last)
        def _():
            received(c)

    pair += stacked(me, late[0], len(late))
    for c in early:
        forward(1, c)
    pair += stacked(across, early[0], len(early))
    for c in late:
        arrived(1, partner, 0, c)
    pair += stacked(partner, late[0], len(late))

    @pl.when(section < last)
    def _():
        factor_copy.wait_recv()

    handed = as_column(factor_r[...])
    for c in early:
        arrived(1, diag, 2, c)
    pair += stacked(diag, early[0], len(early))
    d_attn = pair[:length] - handed * pair[length:]
    attn_s[...] = d_attn.astype(bf16)

    @pl.when(section > 0)
    def _():
        pick_spread(0).wait_recv()

    for o in range(1, n_dp):
        pick_copy(0, o).start()
    attention(1)
    gain_copy.wait_recv()
    total = lane_sum(dq_s[...].astype(f32) * proj_s[:, :width])
    total += lane_sum(dk_s[...].astype(f32) * proj_s[:, width : width + kw])
    total += lane_sum(dv_s[...].astype(f32) * proj_s[:, width + kw :])
    cross_start(1, total)
    scatter(1)
    rstd = rstd_lanes(1)
    factor = as_column(rstd * rstd * rstd * (cross_wait(1) / depth))
    rstd = as_column(rstd)
    for h in range(len(groups)):
        rs_copy(1, 2, h, partner).wait_recv()
    for c in range(chunks):
        at = slice(c * cw, (c + 1) * cw)
        below = g_s[1, me, c].astype(f32) - handed * upper_s[me, :, at].astype(f32)
        local = term_s[:, at] + recv_s[1, 2, c].astype(f32)
        change = rstd * (gains[:, at] * local) - x_s[1, :, at].astype(f32) * factor
        term_s[:, at] = below + change

    @pl.when(section == 0)
    def _():
        rows_s[1] = mul(chosen(1), term_s[...].astype(bf16), FIRST).astype(bf16)
        for o in range(1, n_section):
            own_rows_copy(o).start()
        picks_join(rows_s[1])

    for h, (low, count) in enumerate(groups):
        rs_copy(1, 1, h, across).wait_recv()
        for c in range(low, low + count):
            at = slice(c * cw, (c + 1) * cw)
            out_s[1, c] = (
                term_s[:, at] + rstd * (gains[:, at] * recv_s[1, 1, c].astype(f32))
            ).astype(bf16)

    @pl.when(section > 0)
    def _():
        own_rows_copy(0).wait_recv()
        picks_join(rows_r[1])

    for c in range(chunks):
        pending[0, 0, :, c * cw : (c + 1) * cw] = out_s[1, c]

    feat_own.wait()
    gain_copy.wait_send()
    for c in range(chunks):
        for which in range(3):
            chunk_copy(0, me, c, which, partner).wait_send()
        for which in (0, 2):
            chunk_copy(1, me, c, which, partner).wait_send()
        if c not in direct:
            chunk_copy(1, me, c, 1, partner).wait_send()
    for i in range(3):
        scaled_copy(me, i, partner).wait_send()
        square_copy(i, partner).wait_send()
        for t in range(TICKS):
            for h in range(len(groups)):
                rs_copy(t, i, h, partner).wait_send()
            cross_copy(t, i, partner).wait_send()

    @pl.when(section == last)
    def _():
        for c in direct:
            chunk_copy(1, me, c, 1, partner).wait_send()

    @pl.when(section < last)
    def _():
        upper_near(me, 0).wait_send()
        upper_near(me, 1).wait_send()

    @pl.when(section > 0)
    def _():
        for c in range(chunks):
            held_copy(c).wait_send()
        for c in direct:
            held_far(c).wait_send()
        upper_copy(0).wait_send()
        upper_copy(1).wait_send()
        factor_copy.wait_send()

    @pl.when(section == 0)
    def _():
        far_rows(0).wait_send()
        for o in range(1, n_section):
            pick_spread(o).wait_send()
            far_rows(o).wait_send()
            own_rows_copy(o).wait_send()

    for o in range(1, n_dp):
        feat_copy(o).wait_send()
        source = (seq + n_dp - o) % n_dp
        remote(
            cut_s.at[seq], feat_all.at[source], ft_send.at[o], ft_recv.at[o], {"dp": source}
        ).wait_recv()
        for t in range(TICKS):
            pick_copy(t, o).wait_send()
            ref = picks.at[source, t]
            remote(ref, ref, pz_send.at[t, o], pz_recv.at[t, o], {"dp": source}).wait_recv()


def project_kernel(bands, feat, picked, pending, out, pending_out, out_s, out_sem, pending_sem):
    handed = pltpu.make_async_copy(pending, pending_out, pending_sem)
    handed.start()
    band = out.shape[0] // bands
    lhs = feat[...].T
    copies = []
    for i in range(bands):
        rows = pl.ds(i * band, band)
        out_s[rows, :] = mul(lhs[i * band : (i + 1) * band], picked[...], PLAIN).astype(out_s.dtype)
        copies.append(pltpu.make_async_copy(out_s.at[rows], out.at[rows], out_sem.at[i]))
        copies[-1].start()
    for copy in copies:
        copy.wait()
    handed.wait()


def shards(
    w_query, w_key, w_value, w_out, norm_gain, saved_input, saved_query, saved_key,
    saved_value, grad_in, fresh_grad, features, image_pos, chunks=4, direct=(2, 3), groups=((0, 2), (2, 2)), bands=5,
):
    n_section, n_dp, n_mp = (lax.axis_size(a) for a in ("section", "dp", "mp"))
    assert n_mp == 4
    length, width = grad_in.shape[2:]
    kw = saved_key.shape[4]
    kv_local = kw // HD
    group = width // kw
    images = features.shape[2]
    own_rows = features.shape[3] // n_dp
    f32, bf16 = jnp.float32, jnp.bfloat16
    vmem, dma = pltpu.VMEM, pltpu.SemaphoreType.DMA
    feat_all, picks, pending = pl.pallas_call(
        functools.partial(kernel, n_section, n_dp, n_mp, chunks, direct, groups),
        out_shape=(
            jax.ShapeDtypeStruct((n_dp, TICKS * images, own_rows), bf16),
            jax.ShapeDtypeStruct((n_dp, TICKS, images, width), bf16),
            jax.ShapeDtypeStruct((1, 1, length, width), bf16),
        ),
        in_specs=[pl.BlockSpec(memory_space=pltpu.HBM)] * 13,
        out_specs=(pl.BlockSpec(memory_space=pltpu.VMEM),) * 3,
        scratch_shapes=[
            vmem((n_mp, width, width), bf16),
            vmem((n_mp, width, kw), bf16),
            vmem((n_mp, width, kw), bf16),
            vmem((n_mp, width, width), bf16),
            vmem((1, width), bf16),
            vmem((TICKS, length, width), bf16),
            vmem((TICKS, length, width), bf16),
            vmem((TICKS, length, kw), bf16),
            vmem((TICKS, length, kw), bf16),
            vmem((TICKS, n_mp, chunks, length, width // chunks), bf16),
            vmem((TICKS, images, features.shape[3]), bf16),
            vmem((n_dp, TICKS * images, own_rows), bf16),
            vmem((TICKS, images), jnp.int32),
            vmem((TICKS, kv_local, group * length, length), f32),
            vmem((length, width), bf16),
            vmem((length, width), bf16),
            vmem((length, kw), bf16),
            vmem((length, kw), bf16),
            vmem((TICKS, chunks, length, width // chunks), bf16),
            vmem((TICKS, 3, chunks, length, width // chunks), bf16),
            vmem((TICKS, 3, chunks, length, width // chunks), bf16),
            vmem((length, width), f32),
            vmem((n_mp, length, width), bf16),
            vmem((n_mp, length, width), bf16),
            vmem((length, width + 2 * kw), f32),
            vmem((TICKS, 8, LANES), f32),
            vmem((TICKS, 3, 8, LANES), f32),
            vmem((TICKS, 8, LANES), f32),
            vmem((3, TICKS, 8, LANES), f32),
            vmem((8, LANES), f32),
            vmem((8, LANES), f32),
            vmem((1, width), bf16),
            vmem((2, images, width), bf16),
            vmem((2, images, width), bf16),
            dma((10,)), dma((chunks,)), dma((chunks,)),
            dma((n_mp,)), dma((n_mp,)), dma((n_mp,)), dma((n_mp,)),
            dma((TICKS, chunks, 3)), dma((TICKS, chunks, 3)),
            dma((3,)), dma((3,)), dma((4,)), dma((4,)),
            dma((TICKS, 3, len(groups))), dma((TICKS, 3, len(groups))),
            dma((TICKS, 3)), dma((TICKS, 3)),
            dma((3,)), dma((3,)), dma(()), dma(()),
            dma(()), dma(()), dma((n_section,)), dma(()), dma((n_section,)), dma(()),
            dma((chunks,)), dma((chunks,)), dma((chunks,)),
            dma((n_dp,)), dma((n_dp,)),
            dma((n_section,)), dma(()),
            dma((TICKS, n_dp)), dma((TICKS, n_dp)),
        ],
        compiler_params=pltpu.CompilerParams(
            collective_id=0, has_side_effects=True, vmem_limit_bytes=48 * 2**20
        ),
    )(
        *[
            pltpu.with_memory_space_constraint(a, pltpu.HBM)
            for a in (
                w_query, w_key, w_value, w_out, norm_gain, saved_input, saved_query, saved_key,
                saved_value, grad_in, fresh_grad, features, image_pos,
            )
        ]
    )
    return pl.pallas_call(
        functools.partial(project_kernel, bands),
        out_shape=(
            jax.ShapeDtypeStruct((own_rows, width), bf16),
            jax.ShapeDtypeStruct(pending.shape, bf16),
        ),
        in_specs=[pl.BlockSpec(memory_space=pltpu.VMEM)] * 3,
        out_specs=(pl.BlockSpec(memory_space=pltpu.HBM),) * 2,
        scratch_shapes=[
            vmem((own_rows, width), bf16), dma((bands,)), dma(()),
        ],
        compiler_params=pltpu.CompilerParams(vmem_limit_bytes=8 * 2**20),
    )(feat_all.reshape(-1, own_rows), picks.reshape(-1, width), pending)


def solution(mesh):
    in_specs = (
        P("section", None, "mp"),
        P("section", None, "mp"),
        P("section", None, "mp"),
        P("section", "mp", None),
        P("section", "mp"),
        P("section", None, "dp", None, "mp"),
        P("section", None, "dp", None, "mp"),
        P("section", None, "dp", None, "mp"),
        P("section", None, "dp", None, "mp"),
        P("section", "dp", None, "mp"),
        P(None, "dp", None, "mp"),
        P(None, "dp", None, "section"),
        P(None, "dp", None),
    )
    out_specs = (P(("section", "dp"), "mp"), P("section", "dp", None, "mp"))
    return jax.shard_map(shards, mesh=mesh, in_specs=in_specs, out_specs=out_specs, check_vma=False)
```

```python
import functools

import jax
import jax.numpy as jnp
from jax import lax
from jax.experimental import pallas as pl
from jax.experimental.pallas import tpu as pltpu
from jax.sharding import PartitionSpec as P

HD = 128
LANES = 128
TICKS = 2
MESH = pl.DeviceIdType.MESH
LAST = (((1,), (1,)), ((), ()))
FIRST = (((0,), (0,)), ((), ()))
PLAIN = (((1,), (0,)), ((), ()))


def mul(a, b, dims):
    return lax.dot_general(a, b, dims, preferred_element_type=jnp.float32)


def lane_sum(a):
    parts = [a[:, i : i + LANES] for i in range(0, a.shape[1], LANES)]
    return functools.reduce(lambda p, q: p + q, parts)


def kernel(
    n_section, n_dp, n_mp, chunks, direct, groups,
    wq, wk, wv, wo, gain, x, q, k, v, g_in, fresh, feat, pos,
    feat_all, picks, pending,
    w_s, wo_s, gain_s, x_s, q_s, k_s, v_s, g_s, feat_s, cut_s, pos_s,
    probs_s, attn_s, grad_s, out_s, send_s, recv_s, term_s,
    scaled_s, upper_s, proj_s, cross_s, cross_r, square_s, square_r, factor_s, factor_r,
    gain_r, rows_s, rows_r,
    load_sem, wo_sem, w_sem, out_sem, across_recv, near_recv, diag_recv,
    xg_recv, up_recv, rs_recv, cr_recv, row_recv, held_recv,
):
    section = lax.axis_index("section")
    seq = lax.axis_index("dp")
    me = lax.axis_index("mp")
    y, core = me // 2, me % 2
    partner = 2 * y + (1 - core)
    across = 2 * (1 - y) + core
    diag = 2 * (1 - y) + (1 - core)
    length = g_in.shape[2]
    width = g_in.shape[3]
    depth = width * n_mp
    kw = k.shape[4]
    kv_local = kw // HD
    group = q.shape[4] // kw
    scale = HD ** (-0.5)
    f32, bf16 = jnp.float32, jnp.bfloat16
    last = n_section - 1
    (
        S_FIRST, S_NEAR, S_EARLY, S_LATE, S_SCALED, S_UPPER, S_UPPER_NEAR, S_SUMS, S_CROSS,
        S_SQUARE, S_HELD, S_FAR, S_FEAT, S_PICK, S_ROWS, S_GAIN, S_FACTOR,
    ) = (out_sem.at[i] for i in range(17))
    R_SQUARE, R_FACTOR, R_GAIN, R_FAR_ROWS, R_OWN_ROWS, R_SPREAD, R_FEAT, R_PICK = (
        row_recv.at[i] for i in range(8)
    )
    early = [c for c in range(chunks) if c not in direct]
    late = [c for c in range(chunks) if c in direct]
    first_span, later_span = pl.ds(early[0], len(early)), pl.ds(late[0], len(late))

    def remote(src, dst, ssem, rsem, where):
        return pltpu.make_async_remote_copy(
            src_ref=src, dst_ref=dst, send_sem=ssem, recv_sem=rsem,
            device_id=where, device_id_type=MESH,
        )

    loads = {}

    def load(name, src, dst, sem):
        loads[name] = pltpu.make_async_copy(src, dst, sem)
        loads[name].start()

    cw = width // chunks
    spans = [pl.ds(c * cw, cw) for c in range(chunks)]
    for c in range(chunks):
        load(f"g{c}", g_in.at[0, 0, :, spans[c]], g_s.at[0, me, c], load_sem.at[0])
    load("gain", gain, gain_s, load_sem.at[2])
    load("x", x.at[0, :, 0], x_s, load_sem.at[1])
    load("q", q.at[0, :, 0], q_s, load_sem.at[4])
    load("k", k.at[0, :, 0], k_s, load_sem.at[5])
    load("v", v.at[0, :, 0], v_s, load_sem.at[6])
    load("feat", feat.at[:, 0], feat_s, load_sem.at[7])
    load("pos", pos.at[:, 0], pos_s, load_sem.at[8])

    def fresh_copy(c):
        return pltpu.make_async_copy(
            fresh.at[0, 0, :, spans[c]], g_s.at[1, me, c], load_sem.at[3]
        )

    @pl.when(section == last)
    def _():
        for c in range(chunks):
            fresh_copy(c).start()

    order = (me, partner, across, diag)
    for i, b in enumerate(order):
        columns = pl.ds(pl.multiple_of(b * width, width), width)
        load(f"wo{i}", wo.at[0, :, columns], wo_s.at[b], wo_sem.at[i])
    barrier = pltpu.get_barrier_semaphore()
    for b in (partner, across, diag):
        pl.semaphore_signal(barrier, inc=1, device_id={"mp": b}, device_id_type=MESH)
    for o in range(1, n_dp):
        pl.semaphore_signal(
            barrier, inc=1, device_id={"dp": (seq + o) % n_dp}, device_id_type=MESH
        )
    greets = n_mp - 1 + n_dp - 1 + n_section - 1
    for o in range(1, n_section):
        other = (section + o) % n_section
        pl.semaphore_signal(
            barrier, inc=1, device_id={"section": other}, device_id_type=MESH
        )
        pl.semaphore_signal(
            barrier, inc=1, device_id={"section": other, "mp": across}, device_id_type=MESH
        )
        greets += 1
    pl.semaphore_wait(barrier, greets)

    def block_copy(ref, ssem, rsem, where):
        return remote(ref, ref, ssem, rsem, {"mp": where})

    def drain(ref, sem):
        remote(ref, ref, sem, sem, {"mp": partner}).wait_send()

    def landed(ref, sem):
        remote(ref, ref, sem, sem, {"mp": partner}).wait_recv()

    def near_sem(t, c):
        return near_recv.at[0] if t == 0 else near_recv.at[2 if c in late else 1]

    def diag_sem(t, c):
        return diag_recv.at[c] if t == 0 else diag_recv.at[chunks + (1 if c in late else 0)]

    def to_across(t, c):
        ssem = S_FIRST if t == 0 else S_LATE if c in late else S_EARLY
        return block_copy(g_s.at[t, me, c], ssem, across_recv.at[t, c], across)

    def to_partner(t, c):
        ssem = S_FIRST if t == 0 else S_NEAR
        return block_copy(g_s.at[t, me, c], ssem, near_sem(t, c), partner)

    def forward(t, c):
        landed(g_s.at[t, across, c], across_recv.at[t, c])
        ssem = S_FIRST if t == 0 else S_NEAR
        block_copy(g_s.at[t, across, c], ssem, diag_sem(t, c), partner).start()

    def scaled_copy(slot, which, where):
        return block_copy(scaled_s.at[slot], S_SCALED, xg_recv.at[which], where)

    def upper_copy(far):
        where = {"section": section - 1}
        if far:
            where["mp"] = across
        return remote(x_s.at[0], upper_s.at[me], S_UPPER, up_recv.at[far], where)

    def upper_near(slot, which):
        return block_copy(upper_s.at[slot], S_UPPER_NEAR, up_recv.at[2 + which], partner)

    def filled(ref, sem):
        pltpu.make_async_copy(ref, ref, sem).wait()

    filled(g_s.at[0, me], load_sem.at[0])
    for c in range(chunks):
        to_across(0, c).start()
        to_partner(0, c).start()
    for i, b in enumerate((diag, across, partner, me)):
        rows = pl.ds(pl.multiple_of(b * width, width), width)
        for name, src, low, size in (
            ("wq", wq, 0, width), ("wk", wk, width, kw), ("wv", wv, width + kw, kw)
        ):
            load(f"{name}{i}", src.at[0, rows], w_s.at[b, :, pl.ds(low, size)], w_sem.at[i])

    loads["x"].wait()
    loads["gain"].wait()
    gains = gain_s[...].astype(f32)
    scaled_s[me] = (x_s[1].astype(f32) * gains).astype(bf16)

    def inputs_start():
        @pl.when(section > 0)
        def _():
            upper_copy(1).start()
            upper_copy(0).start()

        gain_copy.start()
        scaled_copy(me, 1, across).start()
        scaled_copy(me, 0, partner).start()

    def row_lanes(total):
        padded = jnp.concatenate([total, jnp.zeros((LANES - length, LANES), f32)], axis=0)
        return jnp.broadcast_to(jnp.sum(padded.T, axis=0, keepdims=True), (8, LANES))

    def as_column(lanes):
        return jnp.broadcast_to(lanes[0:1], (LANES, LANES)).T[:length, 0:1]

    def square_copy(i, where):
        return remote(
            square_s, square_r.at[i], S_SQUARE, R_SQUARE, {"mp": where}
        )

    for t in range(TICKS):
        own = x_s[t].astype(f32)
        square_s[t] = row_lanes(lane_sum(own * own))
    for i, b in enumerate((partner, across, diag)):
        square_copy(i, b).start()

    own_rows = feat_s.shape[2] // n_dp
    def feat_copy(o):
        to = (seq + o) % n_dp
        return remote(
            cut_s.at[to], feat_all.at[seq], S_FEAT, R_FEAT, {"dp": to}
        )

    @pl.when(section == last)
    def _():
        upper_s[...] = jnp.zeros(upper_s.shape, bf16)
        factor_r[...] = jnp.zeros(factor_r.shape, f32)

    loads["q"].wait()
    loads["k"].wait()
    loads["v"].wait()

    def stack(a, g):
        return jnp.concatenate(
            [a[:, (g * group + j) * HD : (g * group + j + 1) * HD] for j in range(group)], axis=0
        )

    rows_at = lax.rem(
        lax.broadcasted_iota(jnp.int32, (group * length, length), 0), jnp.int32(length)
    )
    cols_at = lax.broadcasted_iota(jnp.int32, (group * length, length), 1)
    causal = cols_at <= rows_at

    def softmax(t):
        for g in range(kv_local):
            kg = k_s[t, :, g * HD : (g + 1) * HD]
            scores = mul(stack(q_s[t], g), kg, LAST) * scale
            scores = jnp.where(causal, scores, -1e30)
            expo = jnp.exp(scores - jnp.max(scores, -1, keepdims=True))
            probs_s[t, g] = expo / jnp.sum(expo, -1, keepdims=True)

    for t in range(TICKS):
        softmax(t)

    def pick_copy(t, o):
        to = (seq + o) % n_dp
        ref = picks.at[seq, t]
        return remote(ref, ref, S_PICK, R_PICK, {"dp": to})

    def pick_spread(o):
        ref = picks.at[seq, 0]
        return remote(ref, ref, S_ROWS, R_SPREAD, {"section": o})

    def far_rows(o):
        return remote(
            rows_s.at[0], rows_r.at[0], S_ROWS, R_FAR_ROWS,
            {"section": o, "mp": across},
        )

    def own_rows_copy(o):
        return remote(
            rows_s.at[1], rows_r.at[1], S_ROWS, R_OWN_ROWS, {"section": o}
        )

    gain_copy = remote(gain_s, gain_r, S_GAIN, R_GAIN, {"mp": across})

    def chosen(t):
        at = lax.broadcasted_iota(jnp.int32, (length, pos_s.shape[1]), 0)
        return (at == pos_s[pl.ds(t, 1), :]).astype(f32).astype(bf16)

    def rs_copy(t, i, h, where):
        part = pl.ds(*groups[h])
        rsem = rs_recv.at[t, 2 * len(groups)] if i == 2 else rs_recv.at[t, i * len(groups) + h]
        return remote(
            send_s.at[t, i, part], recv_s.at[t, i, part], S_SUMS, rsem, {"mp": where}
        )

    def cross_copy(t, i, where):
        return remote(
            cross_s.at[t], cross_r.at[t, i], S_CROSS, cr_recv.at[t], {"mp": where}
        )

    def cross_start(t, total):
        cross_s[t] = row_lanes(total)
        for i, b in enumerate((across, diag, partner)):
            cross_copy(t, i, b).start()

    def cross_wait(t):
        cross = cross_s[t]
        landed(cross_r.at[t], cr_recv.at[t])
        for i in range(n_mp - 1):
            cross += cross_r[t, i]
        return cross

    def held_copy(c):
        return remote(
            out_s.at[0, c], g_s.at[1, me, c], S_HELD, held_recv.at[c],
            {"section": section - 1},
        )

    def held_far(c):
        return remote(
            out_s.at[0, c], g_s.at[1, me, c], S_FAR, across_recv.at[1, c],
            {"section": section - 1, "mp": across},
        )

    factor_copy = remote(
        factor_s, factor_r, S_FACTOR, R_FACTOR, {"section": section - 1}
    )

    def wo_part(t, b, c, n=1):
        rows = [g_s[t, b, c + i] for i in range(n)]
        lhs = rows[0] if n == 1 else jnp.concatenate(rows, axis=1)
        return mul(lhs, wo_s[b, :, c * cw : (c + n) * cw], LAST)

    def project():
        scaled_copy(across, 1, partner).wait_recv()
        scaled_copy(across, 2, partner).start()
        scaled_copy(partner, 0, partner).wait_recv()
        total = mul(scaled_s[me], w_s[me], PLAIN)
        for b in (partner, across):
            total += mul(scaled_s[b], w_s[b], PLAIN)
        scaled_copy(diag, 2, partner).wait_recv()
        proj_s[...] = total + mul(scaled_s[diag], w_s[diag], PLAIN)

    def uppers_forward():
        upper_copy(1).wait_recv()
        upper_near(across, 1).start()
        upper_copy(0).wait_recv()
        upper_near(me, 0).start()

    def uppers_wait():
        upper_near(partner, 0).wait_recv()
        upper_near(diag, 1).wait_recv()

    def stacked(b, c, n):
        lhs = jnp.concatenate([g_s[1, b, c + i] for i in range(n)], axis=1)
        at = slice(c * cw, (c + n) * cw)
        both = jnp.concatenate([lhs, upper_s[b, :, at]], axis=0)
        return mul(both, wo_s[b, :, at], LAST)

    def attention(t):
        for g in range(kv_local):
            lanes = slice(g * HD, (g + 1) * HD)
            kg, vg = k_s[t, :, lanes], v_s[t, :, lanes]
            qg = stack(q_s[t], g)
            ag = stack(attn_s[...], g)
            probs = probs_s[t, g]
            d_probs = mul(ag, vg, LAST)
            inner = jnp.sum(probs * d_probs, -1, keepdims=True)
            d_scores = (probs * (d_probs - inner) * scale).astype(bf16)
            d_query = mul(d_scores, kg, PLAIN).astype(bf16)
            for j in range(group):
                grad_s[:, (g * group + j) * HD : (g * group + j + 1) * HD] = d_query[
                    j * length : (j + 1) * length
                ]
            low = width + g * HD
            grad_s[:, low : low + HD] = mul(d_scores, qg, FIRST).astype(bf16)
            grad_s[:, low + kw : low + kw + HD] = mul(
                probs.astype(bf16), ag, FIRST
            ).astype(bf16)

    def partial(b, low, count, rows):
        return mul(rows, w_s[b, low * cw : (low + count) * cw], LAST)

    def pieces(term, low, count):
        return [(low + j, term[:, j * cw : (j + 1) * cw]) for j in range(count)]

    def weights_wait(t, i, b):
        if t == 0:
            filled(w_s.at[b], w_sem.at[i])

    def scatter(t):
        weights_wait(t, 0, diag)
        for h in range(len(groups)):
            for c, term in pieces(partial(diag, *groups[h], grad_s[...]), *groups[h]):
                send_s[t, 0, c] = term.astype(bf16)
            rs_copy(t, 0, h, partner).start()
        if t == 1:
            cross_start(1, lane_sum(grad_s[...].astype(f32) * proj_s[...]))
        weights_wait(t, 1, across)
        for h in range(len(groups)):
            terms = pieces(partial(across, *groups[h], grad_s[...]), *groups[h])
            rs_copy(t, 0, h, partner).wait_recv()
            for c, term in terms:
                send_s[t, 1, c] = (term + recv_s[t, 0, c].astype(f32)).astype(bf16)
            if t == 0:
                rs_copy(t, 1, h, across).start()
        if t == 1:

            @pl.when(section == 0)
            def _():
                sums = jnp.concatenate([send_s[1, 1, c] for c in range(chunks)], axis=1)
                sums = as_column(rstd_lanes(1)) * (gain_r[...].astype(f32) * sums.astype(f32))
                rows_s[0] = mul(chosen(1), sums.astype(bf16), FIRST).astype(bf16)
                for o in range(n_section - 1, -1, -1):
                    far_rows(o).start()

            for h in range(len(groups)):
                rs_copy(t, 1, h, across).start()
        weights_wait(t, 2, partner)
        for c, term in pieces(partial(partner, 0, chunks, grad_s[...]), 0, chunks):
            send_s[t, 2, c] = term.astype(bf16)
        for h in range(len(groups)):
            rs_copy(t, 2, h, partner).start()
        weights_wait(t, 3, me)
        term_s[...] = partial(me, 0, chunks, grad_s[...])

    def rstd_lanes(t):
        squares = square_s[t] + square_r[0, t] + square_r[1, t] + square_r[2, t]
        return lax.rsqrt(squares / depth + 1e-05)

    def d_normed(t, c):
        at = slice(c * cw, (c + 1) * cw)
        return term_s[:, at] + recv_s[t, 2, c].astype(f32) + recv_s[t, 1, c].astype(f32)

    def pick_first():
        rows = jnp.concatenate([out_s[0, c] for c in range(chunks)], axis=1)
        picks[seq, 0] = mul(chosen(0), rows, FIRST).astype(bf16)
        for o in range(1, n_section):
            pick_spread(o).start()

    def picks_join(own):
        far_rows(0).wait_recv()
        picks[seq, 1] = (own.astype(f32) + rows_r[0].astype(f32)).astype(bf16)
        for o in range(1, n_dp):
            pick_copy(1, o).start()

    loads["wo0"].wait()
    d_attn = wo_part(0, me, 0, chunks)
    landed(g_s.at[0, partner], near_recv.at[0])
    loads["wo1"].wait()
    d_attn += wo_part(0, partner, 0, chunks)
    for c in range(chunks):
        forward(0, c)
        if c == 0:
            inputs_start()
            loads["wo2"].wait()
        d_attn += wo_part(0, across, c)
        if c > 0:
            landed(g_s.at[0, diag, c - 1], diag_recv.at[c - 1])
            if c == 1:
                loads["wo3"].wait()
            d_attn += wo_part(0, diag, c - 1)
    landed(g_s.at[0, diag, chunks - 1], diag_recv.at[chunks - 1])
    d_attn += wo_part(0, diag, chunks - 1)
    attn_s[...] = d_attn.astype(bf16)
    attention(0)
    scatter(0)
    loads["feat"].wait()
    for j in range(n_dp):
        for t in range(TICKS):
            cut_s[j, pl.ds(t * feat_s.shape[1], feat_s.shape[1]), :] = feat_s[
                t, :, j * own_rows : (j + 1) * own_rows
            ]
    feat_all[seq] = cut_s[seq]
    for o in range(1, n_dp):
        feat_copy(o).start()

    landed(square_r, R_SQUARE)
    rstd = as_column(rstd_lanes(0))
    total = jnp.zeros((length, LANES), f32)
    for h, (low, count) in enumerate(groups):
        if h == 0:
            landed(recv_s.at[0, 2], rs_recv.at[0, 2 * len(groups)])
        rs_copy(0, 1, h, across).wait_recv()
        for c in range(low, low + count):
            at = slice(c * cw, (c + 1) * cw)
            weighted = gains[:, at] * d_normed(0, c)
            total += lane_sum(x_s[0, :, at].astype(f32) * weighted)
            passed = g_s[0, me, c].astype(f32) + rstd * weighted
            out_s[0, c] = passed.astype(bf16)
            term_s[:, at] = passed

        @pl.when(section > 0)
        def _():
            for c in range(low, low + count):
                if c in direct:
                    held_far(c).start()
            for c in range(low, low + count):
                held_copy(c).start()

    cross_start(0, total)

    @pl.when(section == last)
    def _():
        filled(g_s.at[1, me], load_sem.at[3])
        for c in range(chunks):
            to_across(1, c).start()
            to_partner(1, c).start()
        project()

    def factor_make():
        rstd = rstd_lanes(0)
        factor_s[...] = rstd * rstd * rstd * (cross_wait(0) / depth)

    @pl.when(section > 0)
    def _():
        factor_make()
        factor_copy.start()

    def received(c):
        held_copy(c).wait_recv()
        if c not in direct:
            to_across(1, c).start()
        to_partner(1, c).start()

    @pl.when(section < last)
    def _():
        uppers_forward()
        project()
        uppers_wait()
        for c in early:
            received(c)

    loads["pos"].wait()

    pair = stacked(me, early[0], len(early))
    landed(g_s.at[1, partner, first_span], near_recv.at[1])
    pair += stacked(partner, early[0], len(early))

    @pl.when(section == 0)
    def _():
        factor_make()
        factor = as_column(factor_s[...])
        for c in range(chunks):
            at = slice(c * cw, (c + 1) * cw)
            out_s[0, c] = (term_s[:, at] - x_s[0, :, at].astype(f32) * factor).astype(bf16)
        pick_first()

    for c in late:
        forward(1, c)
    pair += stacked(across, late[0], len(late))
    landed(g_s.at[1, diag, later_span], diag_recv.at[chunks + 1])
    pair += stacked(diag, late[0], len(late))
    for c in late:

        @pl.when(section < last)
        def _():
            received(c)

    pair += stacked(me, late[0], len(late))
    for c in early:
        forward(1, c)
    pair += stacked(across, early[0], len(early))
    landed(g_s.at[1, partner, later_span], near_recv.at[2])
    pair += stacked(partner, late[0], len(late))

    @pl.when(section < last)
    def _():
        factor_copy.wait_recv()

    handed = as_column(factor_r[...])
    landed(g_s.at[1, diag, first_span], diag_recv.at[chunks])
    pair += stacked(diag, early[0], len(early))
    d_attn = pair[:length] - handed * pair[length:]
    attn_s[...] = d_attn.astype(bf16)

    @pl.when(section > 0)
    def _():
        pick_spread(0).wait_recv()

    for o in range(1, n_dp):
        pick_copy(0, o).start()
    attention(1)
    gain_copy.wait_recv()
    scatter(1)
    rstd = rstd_lanes(1)
    factor = as_column(rstd * rstd * rstd * (cross_wait(1) / depth))
    rstd = as_column(rstd)
    landed(recv_s.at[1, 2], rs_recv.at[1, 2 * len(groups)])
    for c in range(chunks):
        at = slice(c * cw, (c + 1) * cw)
        below = g_s[1, me, c].astype(f32) - handed * upper_s[me, :, at].astype(f32)
        local = term_s[:, at] + recv_s[1, 2, c].astype(f32)
        change = rstd * (gains[:, at] * local) - x_s[1, :, at].astype(f32) * factor
        term_s[:, at] = below + change

    @pl.when(section == 0)
    def _():
        rows_s[1] = mul(chosen(1), term_s[...].astype(bf16), FIRST).astype(bf16)
        for o in range(1, n_section):
            own_rows_copy(o).start()
        picks_join(rows_s[1])

    for h, (low, count) in enumerate(groups):
        rs_copy(1, 1, h, across).wait_recv()
        for c in range(low, low + count):
            at = slice(c * cw, (c + 1) * cw)
            out_s[1, c] = (
                term_s[:, at] + rstd * (gains[:, at] * recv_s[1, 1, c].astype(f32))
            ).astype(bf16)

    @pl.when(section > 0)
    def _():
        own_rows_copy(0).wait_recv()
        picks_join(rows_r[1])

    for c in range(chunks):
        pending[0, 0, :, c * cw : (c + 1) * cw] = out_s[1, c]

    drain(g_s.at[0, pl.ds(0, 3)], S_FIRST)
    drain(g_s.at[1, pl.ds(0, 2)], S_NEAR)
    drain(g_s.at[1, 0, first_span], S_EARLY)
    drain(scaled_s.at[pl.ds(0, 3)], S_SCALED)
    drain(send_s, S_SUMS)
    drain(cross_r, S_CROSS)
    drain(square_r, S_SQUARE)
    drain(gain_s, S_GAIN)

    @pl.when(section == last)
    def _():
        drain(g_s.at[1, 0, later_span], S_LATE)

    @pl.when(section < last)
    def _():
        drain(upper_s.at[pl.ds(0, 2)], S_UPPER_NEAR)

    @pl.when(section > 0)
    def _():
        drain(out_s.at[0], S_HELD)
        drain(g_s.at[1, 0, later_span], S_FAR)
        drain(upper_s.at[pl.ds(0, 2)], S_UPPER)
        drain(factor_s, S_FACTOR)

    @pl.when(section == 0)
    def _():
        sent = 3 * n_section - 2
        drain(picks.at[pl.ds(0, sent // 2)], S_ROWS)
        if sent % 2:
            drain(picks.at[0, 0], S_ROWS)

    others = pl.ds(0, n_dp - 1)
    drain(feat_all.at[others], S_FEAT)
    landed(feat_all.at[others], R_FEAT)
    drain(picks.at[others], S_PICK)
    landed(picks.at[others], R_PICK)


def project_kernel(bands, feat, picked, pending, out, pending_out, out_s, out_sem, pending_sem):
    handed = pltpu.make_async_copy(pending, pending_out, pending_sem)
    handed.start()
    band = out.shape[0] // bands
    lhs = feat[...].T
    copies = []
    for i in range(bands):
        rows = pl.ds(i * band, band)
        out_s[rows, :] = mul(lhs[i * band : (i + 1) * band], picked[...], PLAIN).astype(out_s.dtype)
        copies.append(pltpu.make_async_copy(out_s.at[rows], out.at[rows], out_sem.at[i]))
        copies[-1].start()
    for copy in copies:
        copy.wait()
    handed.wait()


def shards(
    w_query, w_key, w_value, w_out, norm_gain, saved_input, saved_query, saved_key,
    saved_value, grad_in, fresh_grad, features, image_pos, chunks=4, direct=(2, 3), groups=((0, 2), (2, 2)), bands=5,
):
    n_section, n_dp, n_mp = (lax.axis_size(a) for a in ("section", "dp", "mp"))
    assert n_mp == 4
    length, width = grad_in.shape[2:]
    kw = saved_key.shape[4]
    kv_local = kw // HD
    group = width // kw
    images = features.shape[2]
    own_rows = features.shape[3] // n_dp
    f32, bf16 = jnp.float32, jnp.bfloat16
    vmem, dma = pltpu.VMEM, pltpu.SemaphoreType.DMA
    feat_all, picks, pending = pl.pallas_call(
        functools.partial(kernel, n_section, n_dp, n_mp, chunks, direct, groups),
        out_shape=(
            jax.ShapeDtypeStruct((n_dp, TICKS * images, own_rows), bf16),
            jax.ShapeDtypeStruct((n_dp, TICKS, images, width), bf16),
            jax.ShapeDtypeStruct((1, 1, length, width), bf16),
        ),
        in_specs=[pl.BlockSpec(memory_space=pltpu.HBM)] * 13,
        out_specs=(pl.BlockSpec(memory_space=pltpu.VMEM),) * 3,
        scratch_shapes=[
            vmem((n_mp, width, width + 2 * kw), bf16),
            vmem((n_mp, width, width), bf16),
            vmem((1, width), bf16),
            vmem((TICKS, length, width), bf16),
            vmem((TICKS, length, width), bf16),
            vmem((TICKS, length, kw), bf16),
            vmem((TICKS, length, kw), bf16),
            vmem((TICKS, n_mp, chunks, length, width // chunks), bf16),
            vmem((TICKS, images, features.shape[3]), bf16),
            vmem((n_dp, TICKS * images, own_rows), bf16),
            vmem((TICKS, images), jnp.int32),
            vmem((TICKS, kv_local, group * length, length), f32),
            vmem((length, width), bf16),
            vmem((length, width + 2 * kw), bf16),
            vmem((TICKS, chunks, length, width // chunks), bf16),
            vmem((TICKS, 3, chunks, length, width // chunks), bf16),
            vmem((TICKS, 3, chunks, length, width // chunks), bf16),
            vmem((length, width), f32),
            vmem((n_mp, length, width), bf16),
            vmem((n_mp, length, width), bf16),
            vmem((length, width + 2 * kw), f32),
            vmem((TICKS, 8, LANES), f32),
            vmem((TICKS, 3, 8, LANES), f32),
            vmem((TICKS, 8, LANES), f32),
            vmem((3, TICKS, 8, LANES), f32),
            vmem((8, LANES), f32),
            vmem((8, LANES), f32),
            vmem((1, width), bf16),
            vmem((2, images, width), bf16),
            vmem((2, images, width), bf16),
            dma((9,)), dma((n_mp,)), dma((n_mp,)), dma((17,)),
            dma((TICKS, chunks)), dma((3,)), dma((chunks + 2,)),
            dma((3,)), dma((4,)), dma((TICKS, 2 * len(groups) + 1)), dma((TICKS,)),
            dma((8,)), dma((chunks,)),
        ],
        compiler_params=pltpu.CompilerParams(
            collective_id=0, has_side_effects=True, vmem_limit_bytes=48 * 2**20
        ),
    )(
        *[
            pltpu.with_memory_space_constraint(a, pltpu.HBM)
            for a in (
                w_query, w_key, w_value, w_out, norm_gain, saved_input, saved_query, saved_key,
                saved_value, grad_in, fresh_grad, features, image_pos,
            )
        ]
    )
    return pl.pallas_call(
        functools.partial(project_kernel, bands),
        out_shape=(
            jax.ShapeDtypeStruct((own_rows, width), bf16),
            jax.ShapeDtypeStruct(pending.shape, bf16),
        ),
        in_specs=[pl.BlockSpec(memory_space=pltpu.VMEM)] * 3,
        out_specs=(pl.BlockSpec(memory_space=pltpu.HBM),) * 2,
        scratch_shapes=[
            vmem((own_rows, width), bf16), dma((bands,)), dma(()),
        ],
        compiler_params=pltpu.CompilerParams(vmem_limit_bytes=8 * 2**20),
    )(feat_all.reshape(-1, own_rows), picks.reshape(-1, width), pending)


def solution(mesh):
    in_specs = (
        P("section", None, "mp"),
        P("section", None, "mp"),
        P("section", None, "mp"),
        P("section", "mp", None),
        P("section", "mp"),
        P("section", None, "dp", None, "mp"),
        P("section", None, "dp", None, "mp"),
        P("section", None, "dp", None, "mp"),
        P("section", None, "dp", None, "mp"),
        P("section", "dp", None, "mp"),
        P(None, "dp", None, "mp"),
        P(None, "dp", None, "section"),
        P(None, "dp", None),
    )
    out_specs = (P(("section", "dp"), "mp"), P("section", "dp", None, "mp"))
    return jax.shard_map(shards, mesh=mesh, in_specs=in_specs, out_specs=out_specs, check_vma=False)
```

```python
import functools

import jax
import jax.numpy as jnp
from jax import lax
from jax.experimental import pallas as pl
from jax.experimental.pallas import tpu as pltpu
from jax.sharding import PartitionSpec as P

HD = 128
LANES = 128
TICKS = 2
MESH = pl.DeviceIdType.MESH
LAST = (((1,), (1,)), ((), ()))
FIRST = (((0,), (0,)), ((), ()))
PLAIN = (((1,), (0,)), ((), ()))


def mul(a, b, dims):
    return lax.dot_general(a, b, dims, preferred_element_type=jnp.float32)


def lane_sum(a):
    parts = [a[:, i : i + LANES] for i in range(0, a.shape[1], LANES)]
    return functools.reduce(lambda p, q: p + q, parts)


def kernel(
    n_section, n_dp, n_mp, chunks, direct, groups,
    wq, wk, wv, wo, gain, x, q, k, v, g_in, fresh, feat, pos,
    feat_all, picks, pending,
    w_s, wo_s, gain_s, x_s, q_s, k_s, v_s, g_s, feat_s, cut_s, pos_s,
    probs_s, attn_s, grad_s, out_s, send_s, recv_s, term_s,
    scaled_s, upper_s, proj_s, cross_s, cross_r, square_s, square_r, factor_s, factor_r,
    gain_r, rows_s, rows_r, base_s, sel_s, sel_r, rstd_s, bases_s,
    load_sem, wo_sem, w_sem, out_sem, across_recv, near_recv, diag_recv,
    xg_recv, up_recv, rs_recv, cr_recv, row_recv, held_recv, sel_recv, far_recv, own_recv,
):
    section = lax.axis_index("section")
    seq = lax.axis_index("dp")
    me = lax.axis_index("mp")
    y, core = me // 2, me % 2
    partner = 2 * y + (1 - core)
    across = 2 * (1 - y) + core
    diag = 2 * (1 - y) + (1 - core)
    length = g_in.shape[2]
    width = g_in.shape[3]
    depth = width * n_mp
    kw = k.shape[4]
    kv_local = kw // HD
    group = q.shape[4] // kw
    scale = HD ** (-0.5)
    f32, bf16 = jnp.float32, jnp.bfloat16
    last = n_section - 1
    (
        S_FIRST, S_NEAR, S_EARLY, S_LATE, S_SCALED, S_UPPER, S_UPPER_NEAR, S_SUMS, S_CROSS,
        S_SQUARE, S_HELD, S_FAR, S_FEAT, S_PICK, S_ROWS, S_GAIN, S_FACTOR,
        S_CHOSEN,
    ) = (out_sem.at[i] for i in range(18))
    R_SQUARE, R_FACTOR, R_GAIN, R_SPREAD, R_FEAT, R_PICK = (row_recv.at[i] for i in range(6))
    early = [c for c in range(chunks) if c not in direct]
    late = [c for c in range(chunks) if c in direct]
    first_span, later_span = pl.ds(early[0], len(early)), pl.ds(late[0], len(late))

    def remote(src, dst, ssem, rsem, where):
        return pltpu.make_async_remote_copy(
            src_ref=src, dst_ref=dst, send_sem=ssem, recv_sem=rsem,
            device_id=where, device_id_type=MESH,
        )

    loads = {}

    def load(name, src, dst, sem):
        loads[name] = pltpu.make_async_copy(src, dst, sem)
        loads[name].start()

    cw = width // chunks
    spans = [pl.ds(c * cw, cw) for c in range(chunks)]
    for c in range(chunks):
        load(f"g{c}", g_in.at[0, 0, :, spans[c]], g_s.at[0, me, c], load_sem.at[0])
    load("gain", gain, gain_s, load_sem.at[2])
    load("x", x.at[0, :, 0], x_s, load_sem.at[1])
    load("q", q.at[0, :, 0], q_s, load_sem.at[4])
    load("k", k.at[0, :, 0], k_s, load_sem.at[5])
    load("v", v.at[0, :, 0], v_s, load_sem.at[6])
    load("feat", feat.at[:, 0], feat_s, load_sem.at[7])
    load("pos", pos.at[:, 0], pos_s, load_sem.at[8])

    def fresh_copy(c):
        return pltpu.make_async_copy(
            fresh.at[0, 0, :, spans[c]], g_s.at[1, me, c], load_sem.at[3]
        )

    @pl.when(section == last)
    def _():
        for c in range(chunks):
            fresh_copy(c).start()

    order = (me, partner, across, diag)
    for i, b in enumerate(order):
        columns = pl.ds(pl.multiple_of(b * width, width), width)
        load(f"wo{i}", wo.at[0, :, columns], wo_s.at[b], wo_sem.at[i])
    barrier = pltpu.get_barrier_semaphore()
    for b in (partner, across, diag):
        pl.semaphore_signal(barrier, inc=1, device_id={"mp": b}, device_id_type=MESH)
    for o in range(1, n_dp):
        pl.semaphore_signal(
            barrier, inc=1, device_id={"dp": (seq + o) % n_dp}, device_id_type=MESH
        )
    greets = n_mp - 1 + n_dp - 1 + n_section - 1
    for o in range(1, n_section):
        other = (section + o) % n_section
        pl.semaphore_signal(
            barrier, inc=1, device_id={"section": other}, device_id_type=MESH
        )
        pl.semaphore_signal(
            barrier, inc=1, device_id={"section": other, "mp": across}, device_id_type=MESH
        )
        greets += 1
    pl.semaphore_wait(barrier, greets)

    def block_copy(ref, ssem, rsem, where):
        return remote(ref, ref, ssem, rsem, {"mp": where})

    def drain(ref, sem):
        remote(ref, ref, sem, sem, {"mp": partner}).wait_send()

    def landed(ref, sem):
        remote(ref, ref, sem, sem, {"mp": partner}).wait_recv()

    def near_sem(t, c):
        return near_recv.at[0] if t == 0 else near_recv.at[2 if c in late else 1]

    def diag_sem(t, c):
        return diag_recv.at[c] if t == 0 else diag_recv.at[chunks + (1 if c in late else 0)]

    def to_across(t, c):
        ssem = S_FIRST if t == 0 else S_LATE if c in late else S_EARLY
        return block_copy(g_s.at[t, me, c], ssem, across_recv.at[t, c], across)

    def to_partner(t, c):
        ssem = S_FIRST if t == 0 else S_NEAR
        return block_copy(g_s.at[t, me, c], ssem, near_sem(t, c), partner)

    def forward(t, c):
        landed(g_s.at[t, across, c], across_recv.at[t, c])
        ssem = S_FIRST if t == 0 else S_NEAR
        block_copy(g_s.at[t, across, c], ssem, diag_sem(t, c), partner).start()

    def scaled_copy(slot, which, where):
        return block_copy(scaled_s.at[slot], S_SCALED, xg_recv.at[which], where)

    def upper_copy(far):
        where = {"section": section - 1}
        if far:
            where["mp"] = across
        return remote(x_s.at[0], upper_s.at[me], S_UPPER, up_recv.at[far], where)

    def upper_near(slot, which):
        return block_copy(upper_s.at[slot], S_UPPER_NEAR, up_recv.at[2 + which], partner)

    def filled(ref, sem):
        pltpu.make_async_copy(ref, ref, sem).wait()

    filled(g_s.at[0, me], load_sem.at[0])
    for c in range(chunks):
        to_across(0, c).start()
        to_partner(0, c).start()
    for i, b in enumerate((diag, across, partner, me)):
        rows = pl.ds(pl.multiple_of(b * width, width), width)
        for name, src, low, size in (
            ("wq", wq, 0, width), ("wk", wk, width, kw), ("wv", wv, width + kw, kw)
        ):
            load(f"{name}{i}", src.at[0, rows], w_s.at[b, :, pl.ds(low, size)], w_sem.at[i])

    loads["x"].wait()
    loads["gain"].wait()
    gains = gain_s[...].astype(f32)
    scaled_s[me] = (x_s[1].astype(f32) * gains).astype(bf16)

    def inputs_start():
        @pl.when(section > 0)
        def _():
            upper_copy(1).start()
            upper_copy(0).start()

        gain_copy.start()
        scaled_copy(me, 1, across).start()
        scaled_copy(me, 0, partner).start()

    def row_lanes(total):
        padded = jnp.concatenate([total, jnp.zeros((LANES - length, LANES), f32)], axis=0)
        return jnp.broadcast_to(jnp.sum(padded.T, axis=0, keepdims=True), (8, LANES))

    def as_column(lanes):
        return jnp.broadcast_to(lanes[0:1], (LANES, LANES)).T[:length, 0:1]

    def square_copy(i, where):
        return remote(
            square_s, square_r.at[i], S_SQUARE, R_SQUARE, {"mp": where}
        )

    for t in range(TICKS):
        own = x_s[t].astype(f32)
        square_s[t] = row_lanes(lane_sum(own * own))
    for i, b in enumerate((partner, across, diag)):
        square_copy(i, b).start()

    own_rows = feat_s.shape[2] // n_dp
    def feat_copy(o):
        to = (seq + o) % n_dp
        return remote(
            cut_s.at[to], feat_all.at[seq], S_FEAT, R_FEAT, {"dp": to}
        )

    @pl.when(section == last)
    def _():
        upper_s[...] = jnp.zeros(upper_s.shape, bf16)
        factor_r[...] = jnp.zeros(factor_r.shape, f32)

    loads["q"].wait()
    loads["k"].wait()
    loads["v"].wait()

    def stack(a, g):
        return jnp.concatenate(
            [a[:, (g * group + j) * HD : (g * group + j + 1) * HD] for j in range(group)], axis=0
        )

    rows_at = lax.rem(
        lax.broadcasted_iota(jnp.int32, (group * length, length), 0), jnp.int32(length)
    )
    cols_at = lax.broadcasted_iota(jnp.int32, (group * length, length), 1)
    causal = cols_at <= rows_at

    def softmax(t):
        for g in range(kv_local):
            kg = k_s[t, :, g * HD : (g + 1) * HD]
            scores = mul(stack(q_s[t], g), kg, LAST) * scale
            scores = jnp.where(causal, scores, -1e30)
            expo = jnp.exp(scores - jnp.max(scores, -1, keepdims=True))
            probs_s[t, g] = expo / jnp.sum(expo, -1, keepdims=True)

    for t in range(TICKS):
        softmax(t)

    def pick_copy(ref, o):
        return remote(ref, ref, S_PICK, R_PICK, {"dp": (seq + o) % n_dp})

    def pick_spread(o):
        ref = picks.at[seq, 0]
        return remote(ref, ref, S_ROWS, R_SPREAD, {"section": o})

    def far_rows(h, o):
        return remote(
            rows_s.at[0, h], rows_r.at[0, h], S_ROWS, far_recv.at[h],
            {"section": o, "mp": across},
        )

    def own_rows_copy(h, o):
        return remote(
            rows_s.at[1, h], rows_r.at[1, h], S_ROWS, own_recv.at[h], {"section": o}
        )

    def sel_copy(i, h):
        return remote(
            sel_s.at[i, h], sel_r.at[i, h], S_CHOSEN, sel_recv.at[i, h], {"mp": partner}
        )

    gain_copy = remote(gain_s, gain_r, S_GAIN, R_GAIN, {"mp": across})

    def chosen(t):
        at = lax.broadcasted_iota(jnp.int32, (length, pos_s.shape[1]), 0)
        return (at == pos_s[pl.ds(t, 1), :]).astype(f32)

    def rs_copy(t, i, h, where):
        part = pl.ds(h, 1) if i == 1 else pl.ds(*groups[h])
        rsem = rs_recv.at[t, (h, len(groups) + h, len(groups) + chunks)[i]]
        return remote(
            send_s.at[t, i, part], recv_s.at[t, i, part], S_SUMS, rsem, {"mp": where}
        )

    def cross_copy(t, i, where):
        return remote(
            cross_s.at[t], cross_r.at[t, i], S_CROSS, cr_recv.at[t], {"mp": where}
        )

    def cross_start(t, total):
        cross_s[t] = row_lanes(total)
        for i, b in enumerate((across, diag, partner)):
            cross_copy(t, i, b).start()

    def cross_wait(t):
        cross = cross_s[t]
        landed(cross_r.at[t], cr_recv.at[t])
        for i in range(n_mp - 1):
            cross += cross_r[t, i]
        return cross

    def held_copy(c):
        return remote(
            out_s.at[0, c], g_s.at[1, me, c], S_HELD, held_recv.at[c],
            {"section": section - 1},
        )

    def held_far(c):
        return remote(
            out_s.at[0, c], g_s.at[1, me, c], S_FAR, across_recv.at[1, c],
            {"section": section - 1, "mp": across},
        )

    factor_copy = remote(
        factor_s, factor_r, S_FACTOR, R_FACTOR, {"section": section - 1}
    )

    def wo_part(t, b, c, n=1):
        rows = [g_s[t, b, c + i] for i in range(n)]
        lhs = rows[0] if n == 1 else jnp.concatenate(rows, axis=1)
        return mul(lhs, wo_s[b, :, c * cw : (c + n) * cw], LAST)

    def project():
        scaled_copy(across, 1, partner).wait_recv()
        scaled_copy(across, 2, partner).start()
        scaled_copy(partner, 0, partner).wait_recv()
        total = mul(scaled_s[me], w_s[me], PLAIN)
        for b in (partner, across):
            total += mul(scaled_s[b], w_s[b], PLAIN)
        scaled_copy(diag, 2, partner).wait_recv()
        proj_s[...] = total + mul(scaled_s[diag], w_s[diag], PLAIN)

    def uppers_forward():
        upper_copy(1).wait_recv()
        upper_near(across, 1).start()
        upper_copy(0).wait_recv()
        upper_near(me, 0).start()

    def uppers_wait():
        upper_near(partner, 0).wait_recv()
        upper_near(diag, 1).wait_recv()

    def stacked(b, c, n):
        lhs = jnp.concatenate([g_s[1, b, c + i] for i in range(n)], axis=1)
        at = slice(c * cw, (c + n) * cw)
        both = jnp.concatenate([lhs, upper_s[b, :, at]], axis=0)
        return mul(both, wo_s[b, :, at], LAST)

    def attention(t):
        for g in range(kv_local):
            lanes = slice(g * HD, (g + 1) * HD)
            kg, vg = k_s[t, :, lanes], v_s[t, :, lanes]
            qg = stack(q_s[t], g)
            ag = stack(attn_s[...], g)
            probs = probs_s[t, g]
            d_probs = mul(ag, vg, LAST)
            inner = jnp.sum(probs * d_probs, -1, keepdims=True)
            d_scores = (probs * (d_probs - inner) * scale).astype(bf16)
            d_query = mul(d_scores, kg, PLAIN).astype(bf16)
            for j in range(group):
                grad_s[:length, (g * group + j) * HD : (g * group + j + 1) * HD] = d_query[
                    j * length : (j + 1) * length
                ]
            low = width + g * HD
            grad_s[:length, low : low + HD] = mul(d_scores, qg, FIRST).astype(bf16)
            grad_s[:length, low + kw : low + kw + HD] = mul(
                probs.astype(bf16), ag, FIRST
            ).astype(bf16)

    def partial(b, low, count, rows):
        return mul(rows, w_s[b, low * cw : (low + count) * cw], LAST)

    def pieces(term, low, count):
        return [(low + j, term[:, j * cw : (j + 1) * cw]) for j in range(count)]

    def weights_wait(t, i, b):
        if t == 0:
            filled(w_s.at[b], w_sem.at[i])

    def lanes_of(h):
        low, count = groups[h]
        return slice(low * cw, (low + count) * cw)

    def scatter_first():
        rows = grad_s[:length]
        weights_wait(0, 0, diag)
        for h in range(len(groups)):
            for c, term in pieces(partial(diag, *groups[h], rows), *groups[h]):
                send_s[0, 0, c] = term.astype(bf16)
            rs_copy(0, 0, h, partner).start()
        weights_wait(0, 1, across)
        for h in range(len(groups)):
            terms = pieces(partial(across, *groups[h], rows), *groups[h])
            rs_copy(0, 0, h, partner).wait_recv()
            for c, term in terms:
                send_s[0, 1, c] = (term + recv_s[0, 0, c].astype(f32)).astype(bf16)
            for c, _ in terms:
                rs_copy(0, 1, c, across).start()
        weights_wait(0, 2, partner)
        for c, term in pieces(partial(partner, 0, chunks, rows), 0, chunks):
            send_s[0, 2, c] = term.astype(bf16)
        for h in range(len(groups)):
            rs_copy(0, 2, h, partner).start()
        weights_wait(0, 3, me)
        term_s[...] = partial(me, 0, chunks, rows)

    def scatter_last(handed):
        pick_of = chosen(1).astype(bf16)
        rstd = rstd_s[:, 0:1]

        def pass_on(i, h, term):
            for c, piece in pieces(term, *groups[h]):
                send_s[1, i, c] = piece.astype(bf16)
            rs_copy(1, i, h, partner).start()

        def pass_rows(i, h, rows):
            sel_s[i, h] = rows.astype(bf16)
            sel_copy(i, h).start()

        grad_s[length:] = mul(pick_of, grad_s[:length], FIRST).astype(bf16)
        every = grad_s[...]
        cross_start(1, lane_sum(grad_s[:length].astype(f32) * proj_s[...]))
        def far_part(h):
            term = partial(across, *groups[h], every)
            sel_copy(0, h).wait_recv()
            rows = term[length:] + sel_r[0, h].astype(f32)
            gain_far = gain_r[:, lanes_of(h)].astype(f32)
            rows_s[0, h] = (rstd * (gain_far * rows)).astype(bf16)

            @pl.when(section == 0)
            def _():
                for o in range(n_section - 1, -1, -1):
                    far_rows(h, o).start()

            rs_copy(1, 0, h, partner).wait_recv()
            for c, piece in pieces(term[:length], *groups[h]):
                send_s[1, 1, c] = (piece + recv_s[1, 0, c].astype(f32)).astype(bf16)

        def own_part(h, rows):
            at = lanes_of(h)
            sel_copy(1, h).wait_recv()
            rows = rstd * (gains[:, at] * (rows + sel_r[1, h].astype(f32)))
            rows_s[1, h] = (bases_s[:, at] + rows).astype(bf16)

            @pl.when(section == 0)
            def _():
                for o in range(1, n_section):
                    own_rows_copy(h, o).start()

        for h in range(len(groups)):
            term = partial(diag, *groups[h], every)
            pass_rows(0, h, term[length:])
            pass_on(0, h, term[:length])
        for h in range(len(groups)):
            far_part(h)
        for c in range(chunks):
            rs_copy(1, 1, c, across).start()
        term = partial(partner, *groups[0], every)
        pass_rows(1, 0, term[length:])
        pass_on(2, 0, term[:length])
        cross = cross_wait(1)
        inverse = rstd_lanes(1)
        terms = [partial(partner, *groups[h], every) for h in range(1, len(groups))]
        factor = as_column(inverse * inverse * inverse * (cross / depth))
        for c in range(chunks):
            at = slice(c * cw, (c + 1) * cw)
            below = g_s[1, me, c].astype(f32) - handed * upper_s[me, :, at].astype(f32)
            base_s[:, at] = below - x_s[1, :, at].astype(f32) * factor
        for h, term in enumerate(terms, 1):
            pass_rows(1, h, term[length:])
            pass_on(2, h, term[:length])
        for h in range(len(groups)):
            term = partial(me, *groups[h], every)
            if h == 0:
                bases_s[...] = mul(pick_of, base_s[...].astype(bf16), FIRST)
            term_s[:, lanes_of(h)] = term[:length]
            own_part(h, term[length:])

    def rstd_lanes(t):
        squares = square_s[t] + square_r[0, t] + square_r[1, t] + square_r[2, t]
        return lax.rsqrt(squares / depth + 1e-05)

    def d_normed(t, c):
        at = slice(c * cw, (c + 1) * cw)
        return term_s[:, at] + recv_s[t, 2, c].astype(f32) + recv_s[t, 1, c].astype(f32)

    def pick_first():
        rows = jnp.concatenate([out_s[0, c] for c in range(chunks)], axis=1)
        rows = mul(chosen(0).astype(bf16), rows, FIRST).astype(bf16)
        for h in range(len(groups)):
            picks[seq, 0, h] = rows[:, lanes_of(h)]
        for o in range(1, n_section):
            pick_spread(o).start()

    def picks_join(h, own):
        far_rows(h, 0).wait_recv()
        picks[seq, 1, h] = (own.astype(f32) + rows_r[0, h].astype(f32)).astype(bf16)
        for o in range(1, n_dp):
            pick_copy(picks.at[seq, 1, h], o).start()

    loads["wo0"].wait()
    d_attn = wo_part(0, me, 0, chunks)
    landed(g_s.at[0, partner], near_recv.at[0])
    loads["wo1"].wait()
    d_attn += wo_part(0, partner, 0, chunks)
    for c in range(chunks):
        forward(0, c)
        if c == 0:
            inputs_start()
            loads["wo2"].wait()
        d_attn += wo_part(0, across, c)
        if c > 0:
            landed(g_s.at[0, diag, c - 1], diag_recv.at[c - 1])
            if c == 1:
                loads["wo3"].wait()
            d_attn += wo_part(0, diag, c - 1)
    landed(g_s.at[0, diag, chunks - 1], diag_recv.at[chunks - 1])
    d_attn += wo_part(0, diag, chunks - 1)
    attn_s[...] = d_attn.astype(bf16)
    attention(0)
    scatter_first()
    loads["feat"].wait()
    for j in range(n_dp):
        for t in range(TICKS):
            cut_s[j, pl.ds(t * feat_s.shape[1], feat_s.shape[1]), :] = feat_s[
                t, :, j * own_rows : (j + 1) * own_rows
            ]
    feat_all[seq] = cut_s[seq]
    for o in range(1, n_dp):
        feat_copy(o).start()

    landed(square_r, R_SQUARE)
    loads["pos"].wait()
    rstd_s[...] = lax.dot_general(
        chosen(1), jnp.broadcast_to(as_column(rstd_lanes(1)), (length, LANES)), FIRST,
        precision=lax.Precision.HIGHEST, preferred_element_type=f32,
    )
    rstd = as_column(rstd_lanes(0))
    total = jnp.zeros((length, LANES), f32)
    landed(recv_s.at[0, 2], rs_recv.at[0, len(groups) + chunks])
    for c in range(chunks):
        rs_copy(0, 1, c, across).wait_recv()
        at = slice(c * cw, (c + 1) * cw)
        weighted = gains[:, at] * d_normed(0, c)
        passed = g_s[0, me, c].astype(f32) + rstd * weighted
        out_s[0, c] = passed.astype(bf16)

        @pl.when(section > 0)
        def _():
            if c in early:
                held_copy(c).start()
            else:
                held_far(c).start()
            if c == late[-1]:
                for b in late:
                    held_copy(b).start()

        term_s[:, at] = passed
        total += lane_sum(x_s[0, :, at].astype(f32) * weighted)

    cross_start(0, total)

    @pl.when(section == last)
    def _():
        filled(g_s.at[1, me], load_sem.at[3])
        for c in range(chunks):
            to_across(1, c).start()
            to_partner(1, c).start()
        project()

    def factor_make():
        rstd = rstd_lanes(0)
        factor_s[...] = rstd * rstd * rstd * (cross_wait(0) / depth)

    @pl.when(section > 0)
    def _():
        factor_make()
        factor_copy.start()

    def received(c):
        held_copy(c).wait_recv()
        if c not in direct:
            to_across(1, c).start()
        to_partner(1, c).start()

    @pl.when(section < last)
    def _():
        uppers_forward()
        project()
        uppers_wait()
        for c in early:
            received(c)

    pair = stacked(me, early[0], len(early))
    landed(g_s.at[1, partner, first_span], near_recv.at[1])
    pair += stacked(partner, early[0], len(early))

    for c in late:
        forward(1, c)
    pair += stacked(across, late[0], len(late))

    @pl.when(section == 0)
    def _():
        factor_make()
        factor = as_column(factor_s[...])
        for c in range(chunks):
            at = slice(c * cw, (c + 1) * cw)
            out_s[0, c] = (term_s[:, at] - x_s[0, :, at].astype(f32) * factor).astype(bf16)
        pick_first()

    landed(g_s.at[1, diag, later_span], diag_recv.at[chunks + 1])
    pair += stacked(diag, late[0], len(late))
    for c in late:

        @pl.when(section < last)
        def _():
            received(c)

    pair += stacked(me, late[0], len(late))
    for c in early:
        forward(1, c)
    pair += stacked(across, early[0], len(early))
    landed(g_s.at[1, partner, later_span], near_recv.at[2])
    pair += stacked(partner, late[0], len(late))

    @pl.when(section < last)
    def _():
        factor_copy.wait_recv()

    handed = as_column(factor_r[...])
    landed(g_s.at[1, diag, first_span], diag_recv.at[chunks])
    pair += stacked(diag, early[0], len(early))
    d_attn = pair[:length] - handed * pair[length:]
    attn_s[...] = d_attn.astype(bf16)

    @pl.when(section > 0)
    def _():
        pick_spread(0).wait_recv()

    for o in range(1, n_dp):
        pick_copy(picks.at[seq, 0], o).start()
    attention(1)
    gain_copy.wait_recv()
    scatter_last(handed)

    @pl.when(section == 0)
    def _():
        for h in range(len(groups)):
            picks_join(h, rows_s[1, h])

    @pl.when(section > 0)
    def _():
        for h in range(len(groups)):
            own_rows_copy(h, 0).wait_recv()
            picks_join(h, rows_r[1, h])

    rstd = as_column(rstd_lanes(1))
    landed(recv_s.at[1, 2], rs_recv.at[1, len(groups) + chunks])
    for c in range(chunks):
        rs_copy(1, 1, c, across).wait_recv()
        at = slice(c * cw, (c + 1) * cw)
        out_s[1, c] = (base_s[:, at] + rstd * (gains[:, at] * d_normed(1, c))).astype(bf16)

    for c in range(chunks):
        pending[0, 0, :, c * cw : (c + 1) * cw] = out_s[1, c]

    drain(g_s.at[0, pl.ds(0, 3)], S_FIRST)
    drain(g_s.at[1, pl.ds(0, 2)], S_NEAR)
    drain(g_s.at[1, 0, first_span], S_EARLY)
    drain(scaled_s.at[pl.ds(0, 3)], S_SCALED)
    drain(send_s, S_SUMS)
    drain(cross_r, S_CROSS)
    drain(square_r, S_SQUARE)
    drain(gain_s, S_GAIN)
    drain(sel_s, S_CHOSEN)

    @pl.when(section == last)
    def _():
        drain(g_s.at[1, 0, later_span], S_LATE)

    @pl.when(section < last)
    def _():
        drain(upper_s.at[pl.ds(0, 2)], S_UPPER_NEAR)

    @pl.when(section > 0)
    def _():
        drain(out_s.at[0], S_HELD)
        drain(g_s.at[1, 0, later_span], S_FAR)
        drain(upper_s.at[pl.ds(0, 2)], S_UPPER)
        drain(factor_s, S_FACTOR)

    @pl.when(section == 0)
    def _():
        sent = 3 * n_section - 2
        drain(picks.at[pl.ds(0, sent // 2)], S_ROWS)
        if sent % 2:
            drain(picks.at[0, 0], S_ROWS)

    others = pl.ds(0, n_dp - 1)
    drain(feat_all.at[others], S_FEAT)
    landed(feat_all.at[others], R_FEAT)
    drain(picks.at[others], S_PICK)
    landed(picks.at[others], R_PICK)


def project_kernel(bands, feat, picked, pending, out, pending_out, out_s, out_sem, pending_sem):
    handed = pltpu.make_async_copy(pending, pending_out, pending_sem)
    handed.start()
    band = out.shape[0] // bands
    lhs = feat[...].T
    rhs = jnp.concatenate(
        [picked[:, h].reshape(-1, picked.shape[3]) for h in range(picked.shape[1])], axis=1
    )
    copies = []
    for i in range(bands):
        rows = pl.ds(i * band, band)
        out_s[rows, :] = mul(lhs[i * band : (i + 1) * band], rhs, PLAIN).astype(out_s.dtype)
        copies.append(pltpu.make_async_copy(out_s.at[rows], out.at[rows], out_sem.at[i]))
        copies[-1].start()
    for copy in copies:
        copy.wait()
    handed.wait()


def shards(
    w_query, w_key, w_value, w_out, norm_gain, saved_input, saved_query, saved_key,
    saved_value, grad_in, fresh_grad, features, image_pos, chunks=4, direct=(2, 3), groups=((0, 2), (2, 2)), bands=5,
):
    n_section, n_dp, n_mp = (lax.axis_size(a) for a in ("section", "dp", "mp"))
    assert n_mp == 4
    length, width = grad_in.shape[2:]
    kw = saved_key.shape[4]
    kv_local = kw // HD
    group = width // kw
    images = features.shape[2]
    own_rows = features.shape[3] // n_dp
    halves = len(groups)
    f32, bf16 = jnp.float32, jnp.bfloat16
    vmem, dma = pltpu.VMEM, pltpu.SemaphoreType.DMA
    feat_all, picks, pending = pl.pallas_call(
        functools.partial(kernel, n_section, n_dp, n_mp, chunks, direct, groups),
        out_shape=(
            jax.ShapeDtypeStruct((n_dp, TICKS * images, own_rows), bf16),
            jax.ShapeDtypeStruct((n_dp, TICKS, halves, images, width // halves), bf16),
            jax.ShapeDtypeStruct((1, 1, length, width), bf16),
        ),
        in_specs=[pl.BlockSpec(memory_space=pltpu.HBM)] * 13,
        out_specs=(pl.BlockSpec(memory_space=pltpu.VMEM),) * 3,
        scratch_shapes=[
            vmem((n_mp, width, width + 2 * kw), bf16),
            vmem((n_mp, width, width), bf16),
            vmem((1, width), bf16),
            vmem((TICKS, length, width), bf16),
            vmem((TICKS, length, width), bf16),
            vmem((TICKS, length, kw), bf16),
            vmem((TICKS, length, kw), bf16),
            vmem((TICKS, n_mp, chunks, length, width // chunks), bf16),
            vmem((TICKS, images, features.shape[3]), bf16),
            vmem((n_dp, TICKS * images, own_rows), bf16),
            vmem((TICKS, images), jnp.int32),
            vmem((TICKS, kv_local, group * length, length), f32),
            vmem((length, width), bf16),
            vmem((length + images, width + 2 * kw), bf16),
            vmem((TICKS, chunks, length, width // chunks), bf16),
            vmem((TICKS, 3, chunks, length, width // chunks), bf16),
            vmem((TICKS, 3, chunks, length, width // chunks), bf16),
            vmem((length, width), f32),
            vmem((n_mp, length, width), bf16),
            vmem((n_mp, length, width), bf16),
            vmem((length, width + 2 * kw), f32),
            vmem((TICKS, 8, LANES), f32),
            vmem((TICKS, 3, 8, LANES), f32),
            vmem((TICKS, 8, LANES), f32),
            vmem((3, TICKS, 8, LANES), f32),
            vmem((8, LANES), f32),
            vmem((8, LANES), f32),
            vmem((1, width), bf16),
            vmem((2, halves, images, width // halves), bf16),
            vmem((2, halves, images, width // halves), bf16),
            vmem((length, width), f32),
            vmem((2, halves, images, width // halves), bf16),
            vmem((2, halves, images, width // halves), bf16),
            vmem((images, LANES), f32),
            vmem((images, width), f32),
            dma((9,)), dma((n_mp,)), dma((n_mp,)), dma((18,)),
            dma((TICKS, chunks)), dma((3,)), dma((chunks + 2,)),
            dma((3,)), dma((4,)), dma((TICKS, len(groups) + chunks + 1)), dma((TICKS,)),
            dma((6,)), dma((chunks,)), dma((2, halves)), dma((halves,)), dma((halves,)),
        ],
        compiler_params=pltpu.CompilerParams(
            collective_id=0, has_side_effects=True, vmem_limit_bytes=48 * 2**20
        ),
    )(
        *[
            pltpu.with_memory_space_constraint(a, pltpu.HBM)
            for a in (
                w_query, w_key, w_value, w_out, norm_gain, saved_input, saved_query, saved_key,
                saved_value, grad_in, fresh_grad, features, image_pos,
            )
        ]
    )
    return pl.pallas_call(
        functools.partial(project_kernel, bands),
        out_shape=(
            jax.ShapeDtypeStruct((own_rows, width), bf16),
            jax.ShapeDtypeStruct(pending.shape, bf16),
        ),
        in_specs=[pl.BlockSpec(memory_space=pltpu.VMEM)] * 3,
        out_specs=(pl.BlockSpec(memory_space=pltpu.HBM),) * 2,
        scratch_shapes=[
            vmem((own_rows, width), bf16), dma((bands,)), dma(()),
        ],
        compiler_params=pltpu.CompilerParams(vmem_limit_bytes=8 * 2**20),
    )(feat_all.reshape(-1, own_rows), picks.reshape((-1,) + picks.shape[2:]), pending)


def solution(mesh):
    in_specs = (
        P("section", None, "mp"),
        P("section", None, "mp"),
        P("section", None, "mp"),
        P("section", "mp", None),
        P("section", "mp"),
        P("section", None, "dp", None, "mp"),
        P("section", None, "dp", None, "mp"),
        P("section", None, "dp", None, "mp"),
        P("section", None, "dp", None, "mp"),
        P("section", "dp", None, "mp"),
        P(None, "dp", None, "mp"),
        P(None, "dp", None, "section"),
        P(None, "dp", None),
    )
    out_specs = (P(("section", "dp"), "mp"), P("section", "dp", None, "mp"))
    return jax.shard_map(shards, mesh=mesh, in_specs=in_specs, out_specs=out_specs, check_vma=False)
```

```python
import functools

import jax
import jax.numpy as jnp
from jax import lax
from jax.experimental import pallas as pl
from jax.experimental.pallas import tpu as pltpu
from jax.sharding import PartitionSpec as P

HD = 128
LANES = 128
TICKS = 2
MESH = pl.DeviceIdType.MESH
LAST = (((1,), (1,)), ((), ()))
FIRST = (((0,), (0,)), ((), ()))
PLAIN = (((1,), (0,)), ((), ()))


def mul(a, b, dims):
    return lax.dot_general(a, b, dims, preferred_element_type=jnp.float32)


def lane_sum(a):
    parts = [a[:, i : i + LANES] for i in range(0, a.shape[1], LANES)]
    return functools.reduce(lambda p, q: p + q, parts)


def kernel(
    n_section, n_dp, n_mp, chunks, direct, groups,
    wq, wk, wv, wo, gain, x, q, k, v, g_in, fresh, feat, pos,
    feat_all, picks, pending,
    w_s, wo_s, gain_s, x_s, q_s, k_s, v_s, g_s, feat_s, cut_s, pos_s,
    probs_s, mixed_s, turned_s, attn_s, grad_s, out_s, send_s, recv_s, term_s,
    scaled_s, upper_s, proj_s, cross_s, cross_r, square_s, square_r, factor_s, factor_r,
    gain_r, rows_s, rows_r, base_s, sel_s, sel_r, rstd_s, bases_s,
    load_sem, wo_sem, w_sem, out_sem, across_recv, near_recv, diag_recv,
    xg_recv, up_recv, rs_recv, cr_recv, row_recv, held_recv, sel_recv, far_recv, own_recv,
):
    section = lax.axis_index("section")
    seq = lax.axis_index("dp")
    me = lax.axis_index("mp")
    y, core = me // 2, me % 2
    partner = 2 * y + (1 - core)
    across = 2 * (1 - y) + core
    diag = 2 * (1 - y) + (1 - core)
    length = g_in.shape[2]
    width = g_in.shape[3]
    depth = width * n_mp
    kw = k.shape[4]
    kv_local = kw // HD
    group = q.shape[4] // kw
    scale = HD ** (-0.5)
    f32, bf16 = jnp.float32, jnp.bfloat16
    last = n_section - 1
    (
        S_FIRST, S_NEAR, S_EARLY, S_LATE, S_SCALED, S_UPPER, S_UPPER_NEAR, S_SUMS, S_CROSS,
        S_SQUARE, S_HELD, S_FAR, S_FEAT, S_PICK, S_ROWS, S_GAIN, S_FACTOR,
        S_CHOSEN,
    ) = (out_sem.at[i] for i in range(18))
    R_SQUARE, R_FACTOR, R_GAIN, R_SPREAD, R_FEAT, R_PICK = (row_recv.at[i] for i in range(6))
    early = [c for c in range(chunks) if c not in direct]
    late = [c for c in range(chunks) if c in direct]
    first_span, later_span = pl.ds(early[0], len(early)), pl.ds(late[0], len(late))

    def remote(src, dst, ssem, rsem, where):
        return pltpu.make_async_remote_copy(
            src_ref=src, dst_ref=dst, send_sem=ssem, recv_sem=rsem,
            device_id=where, device_id_type=MESH,
        )

    loads = {}

    def load(name, src, dst, sem):
        loads[name] = pltpu.make_async_copy(src, dst, sem)
        loads[name].start()

    cw = width // chunks
    spans = [pl.ds(c * cw, cw) for c in range(chunks)]
    for c in range(chunks):
        load(f"g{c}", g_in.at[0, 0, :, spans[c]], g_s.at[0, me, c], load_sem.at[0])
    load("gain", gain, gain_s, load_sem.at[2])
    load("x", x.at[0, :, 0], x_s, load_sem.at[1])
    load("q", q.at[0, :, 0], q_s, load_sem.at[4])
    load("k", k.at[0, :, 0], k_s, load_sem.at[5])
    load("v", v.at[0, :, 0], v_s, load_sem.at[6])
    load("feat", feat.at[:, 0], feat_s, load_sem.at[7])
    load("pos", pos.at[:, 0], pos_s, load_sem.at[8])

    def fresh_copy(c):
        return pltpu.make_async_copy(
            fresh.at[0, 0, :, spans[c]], g_s.at[1, me, c], load_sem.at[3]
        )

    @pl.when(section == last)
    def _():
        for c in range(chunks):
            fresh_copy(c).start()

    order = (me, partner, across, diag)
    for i, b in enumerate(order):
        columns = pl.ds(pl.multiple_of(b * width, width), width)
        load(f"wo{i}", wo.at[0, :, columns], wo_s.at[b], wo_sem.at[i])
    barrier = pltpu.get_barrier_semaphore()
    for b in (partner, across, diag):
        pl.semaphore_signal(barrier, inc=1, device_id={"mp": b}, device_id_type=MESH)
    for o in range(1, n_dp):
        pl.semaphore_signal(
            barrier, inc=1, device_id={"dp": (seq + o) % n_dp}, device_id_type=MESH
        )
    greets = n_mp - 1 + n_dp - 1 + n_section - 1
    for o in range(1, n_section):
        other = (section + o) % n_section
        pl.semaphore_signal(
            barrier, inc=1, device_id={"section": other}, device_id_type=MESH
        )
        pl.semaphore_signal(
            barrier, inc=1, device_id={"section": other, "mp": across}, device_id_type=MESH
        )
        greets += 1
    pl.semaphore_wait(barrier, greets)

    def block_copy(ref, ssem, rsem, where):
        return remote(ref, ref, ssem, rsem, {"mp": where})

    def drain(ref, sem):
        remote(ref, ref, sem, sem, {"mp": partner}).wait_send()

    def landed(ref, sem):
        remote(ref, ref, sem, sem, {"mp": partner}).wait_recv()

    def near_sem(t, c):
        return near_recv.at[0] if t == 0 else near_recv.at[2 if c in late else 1]

    def diag_sem(t, c):
        return diag_recv.at[c] if t == 0 else diag_recv.at[chunks + (1 if c in late else 0)]

    def to_across(t, c):
        ssem = S_FIRST if t == 0 else S_LATE if c in late else S_EARLY
        return block_copy(g_s.at[t, me, c], ssem, across_recv.at[t, c], across)

    def to_partner(t, c):
        ssem = S_FIRST if t == 0 else S_NEAR
        return block_copy(g_s.at[t, me, c], ssem, near_sem(t, c), partner)

    def forward(t, c):
        landed(g_s.at[t, across, c], across_recv.at[t, c])
        ssem = S_FIRST if t == 0 else S_NEAR
        block_copy(g_s.at[t, across, c], ssem, diag_sem(t, c), partner).start()

    def scaled_copy(slot, which, where):
        return block_copy(scaled_s.at[slot], S_SCALED, xg_recv.at[which], where)

    def upper_copy(far):
        where = {"section": section - 1}
        if far:
            where["mp"] = across
        return remote(x_s.at[0], upper_s.at[me], S_UPPER, up_recv.at[far], where)

    def upper_near(slot, which):
        return block_copy(upper_s.at[slot], S_UPPER_NEAR, up_recv.at[2 + which], partner)

    def filled(ref, sem):
        pltpu.make_async_copy(ref, ref, sem).wait()

    filled(g_s.at[0, me], load_sem.at[0])
    for c in range(chunks):
        to_across(0, c).start()
        to_partner(0, c).start()
    for i, b in enumerate((diag, across, partner, me)):
        rows = pl.ds(pl.multiple_of(b * width, width), width)
        for name, src, low, size in (
            ("wq", wq, 0, width), ("wk", wk, width, kw), ("wv", wv, width + kw, kw)
        ):
            load(f"{name}{i}", src.at[0, rows], w_s.at[b, :, pl.ds(low, size)], w_sem.at[i])

    loads["x"].wait()
    loads["gain"].wait()
    gains = gain_s[...].astype(f32)
    scaled_s[me] = (x_s[1].astype(f32) * gains).astype(bf16)

    def inputs_start():
        @pl.when(section > 0)
        def _():
            upper_copy(1).start()
            upper_copy(0).start()

        gain_copy.start()
        scaled_copy(me, 1, across).start()
        scaled_copy(me, 0, partner).start()

    def row_lanes(total):
        padded = jnp.concatenate([total, jnp.zeros((LANES - length, LANES), f32)], axis=0)
        return jnp.broadcast_to(jnp.sum(padded.T, axis=0, keepdims=True), (8, LANES))

    def as_column(lanes):
        return jnp.broadcast_to(lanes[0:1], (LANES, LANES)).T[:length, 0:1]

    def square_copy(i, where):
        return remote(
            square_s, square_r.at[i], S_SQUARE, R_SQUARE, {"mp": where}
        )

    for t in range(TICKS):
        own = x_s[t].astype(f32)
        square_s[t] = row_lanes(lane_sum(own * own))
    for i, b in enumerate((partner, across, diag)):
        square_copy(i, b).start()

    own_rows = feat_s.shape[2] // n_dp
    def feat_copy(o):
        to = (seq + o) % n_dp
        return remote(
            cut_s.at[to], feat_all.at[seq], S_FEAT, R_FEAT, {"dp": to}
        )

    @pl.when(section == last)
    def _():
        upper_s[...] = jnp.zeros(upper_s.shape, bf16)
        factor_r[...] = jnp.zeros(factor_r.shape, f32)

    loads["q"].wait()
    loads["k"].wait()
    loads["v"].wait()

    def stack(a, g):
        return jnp.concatenate(
            [a[:, (g * group + j) * HD : (g * group + j + 1) * HD] for j in range(group)], axis=0
        )

    rows_at = lax.rem(
        lax.broadcasted_iota(jnp.int32, (group * length, length), 0), jnp.int32(length)
    )
    cols_at = lax.broadcasted_iota(jnp.int32, (group * length, length), 1)
    causal = cols_at <= rows_at

    def softmax(t):
        for g in range(kv_local):
            kg = k_s[t, :, g * HD : (g + 1) * HD]
            scores = mul(stack(q_s[t], g), kg, LAST) * scale
            scores = jnp.where(causal, scores, -1e30)
            expo = jnp.exp(scores - jnp.max(scores, -1, keepdims=True))
            probs = expo / jnp.sum(expo, -1, keepdims=True)
            probs_s[t, g] = probs
            vg = v_s[t, :, g * HD : (g + 1) * HD].astype(f32)
            mixed_s[t, g] = lax.dot_general(
                probs, vg, PLAIN, precision=lax.Precision.HIGHEST, preferred_element_type=f32
            )
            turned_s[t, g] = probs.astype(bf16).T

    for t in range(TICKS):
        softmax(t)

    def pick_copy(ref, o):
        return remote(ref, ref, S_PICK, R_PICK, {"dp": (seq + o) % n_dp})

    def pick_spread(o):
        ref = picks.at[seq, 0]
        return remote(ref, ref, S_ROWS, R_SPREAD, {"section": o})

    def far_rows(h, o):
        return remote(
            rows_s.at[0, h], rows_r.at[0, h], S_ROWS, far_recv.at[h],
            {"section": o, "mp": across},
        )

    def own_rows_copy(h, o):
        return remote(
            rows_s.at[1, h], rows_r.at[1, h], S_ROWS, own_recv.at[h], {"section": o}
        )

    def sel_copy(i, h):
        return remote(
            sel_s.at[i, h], sel_r.at[i, h], S_CHOSEN, sel_recv.at[i, h], {"mp": partner}
        )

    gain_copy = remote(gain_s, gain_r, S_GAIN, R_GAIN, {"mp": across})

    def chosen(t):
        at = lax.broadcasted_iota(jnp.int32, (length, pos_s.shape[1]), 0)
        return (at == pos_s[pl.ds(t, 1), :]).astype(f32)

    def rs_copy(t, i, h, where):
        part = pl.ds(h, 1) if i == 1 else pl.ds(*groups[h])
        rsem = rs_recv.at[t, (h, len(groups) + h, len(groups) + chunks)[i]]
        return remote(
            send_s.at[t, i, part], recv_s.at[t, i, part], S_SUMS, rsem, {"mp": where}
        )

    def cross_copy(t, i, where):
        return remote(
            cross_s.at[t], cross_r.at[t, i], S_CROSS, cr_recv.at[t], {"mp": where}
        )

    def cross_start(t, total):
        cross_s[t] = row_lanes(total)
        for i, b in enumerate((across, diag, partner)):
            cross_copy(t, i, b).start()

    def cross_wait(t):
        cross = cross_s[t]
        landed(cross_r.at[t], cr_recv.at[t])
        for i in range(n_mp - 1):
            cross += cross_r[t, i]
        return cross

    def held_copy(c):
        return remote(
            out_s.at[0, c], g_s.at[1, me, c], S_HELD, held_recv.at[c],
            {"section": section - 1},
        )

    def held_far(c):
        return remote(
            out_s.at[0, c], g_s.at[1, me, c], S_FAR, across_recv.at[1, c],
            {"section": section - 1, "mp": across},
        )

    factor_copy = remote(
        factor_s, factor_r, S_FACTOR, R_FACTOR, {"section": section - 1}
    )

    def wo_part(t, b, c, n=1):
        rows = [g_s[t, b, c + i] for i in range(n)]
        lhs = rows[0] if n == 1 else jnp.concatenate(rows, axis=1)
        return mul(lhs, wo_s[b, :, c * cw : (c + n) * cw], LAST)

    def project():
        scaled_copy(across, 1, partner).wait_recv()
        scaled_copy(across, 2, partner).start()
        scaled_copy(partner, 0, partner).wait_recv()
        total = mul(scaled_s[me], w_s[me], PLAIN)
        for b in (partner, across):
            total += mul(scaled_s[b], w_s[b], PLAIN)
        scaled_copy(diag, 2, partner).wait_recv()
        proj_s[...] = total + mul(scaled_s[diag], w_s[diag], PLAIN)

    def uppers_forward():
        upper_copy(1).wait_recv()
        upper_near(across, 1).start()
        upper_copy(0).wait_recv()
        upper_near(me, 0).start()

    def uppers_wait():
        upper_near(partner, 0).wait_recv()
        upper_near(diag, 1).wait_recv()

    def stacked(b, c, n):
        lhs = jnp.concatenate([g_s[1, b, c + i] for i in range(n)], axis=1)
        at = slice(c * cw, (c + n) * cw)
        both = jnp.concatenate([lhs, upper_s[b, :, at]], axis=0)
        return mul(both, wo_s[b, :, at], LAST)

    def attention(t):
        for g in range(kv_local):
            lanes = slice(g * HD, (g + 1) * HD)
            kg, vg = k_s[t, :, lanes], v_s[t, :, lanes]
            qg = stack(q_s[t], g)
            ag = stack(attn_s[...], g)
            probs = probs_s[t, g]
            d_probs = mul(ag, vg, LAST)
            inner = jnp.sum(ag.astype(f32) * mixed_s[t, g], -1, keepdims=True)
            d_scores = (probs * (d_probs - inner) * scale).astype(bf16)
            d_query = mul(d_scores, kg, PLAIN).astype(bf16)
            for j in range(group):
                grad_s[:length, (g * group + j) * HD : (g * group + j + 1) * HD] = d_query[
                    j * length : (j + 1) * length
                ]
            low = width + g * HD
            grad_s[:length, low : low + HD] = mul(d_scores, qg, FIRST).astype(bf16)
            grad_s[:length, low + kw : low + kw + HD] = mul(
                turned_s[t, g], ag, PLAIN
            ).astype(bf16)

    def partial(b, low, count, rows):
        return mul(rows, w_s[b, low * cw : (low + count) * cw], LAST)

    def pieces(term, low, count):
        return [(low + j, term[:, j * cw : (j + 1) * cw]) for j in range(count)]

    def weights_wait(t, i, b):
        if t == 0:
            filled(w_s.at[b], w_sem.at[i])

    def lanes_of(h):
        low, count = groups[h]
        return slice(low * cw, (low + count) * cw)

    def scatter_first():
        rows = grad_s[:length]
        weights_wait(0, 0, diag)
        for h in range(len(groups)):
            for c, term in pieces(partial(diag, *groups[h], rows), *groups[h]):
                send_s[0, 0, c] = term.astype(bf16)
            rs_copy(0, 0, h, partner).start()
        weights_wait(0, 1, across)
        for h in range(len(groups)):
            terms = pieces(partial(across, *groups[h], rows), *groups[h])
            rs_copy(0, 0, h, partner).wait_recv()
            for c, term in terms:
                send_s[0, 1, c] = (term + recv_s[0, 0, c].astype(f32)).astype(bf16)
            for c, _ in terms:
                rs_copy(0, 1, c, across).start()
        weights_wait(0, 2, partner)
        for c, term in pieces(partial(partner, 0, chunks, rows), 0, chunks):
            send_s[0, 2, c] = term.astype(bf16)
        for h in range(len(groups)):
            rs_copy(0, 2, h, partner).start()
        weights_wait(0, 3, me)
        term_s[...] = partial(me, 0, chunks, rows)

    def scatter_last(handed):
        pick_of = chosen(1).astype(bf16)
        rstd = rstd_s[:, 0:1]

        def pass_on(i, h, term):
            for c, piece in pieces(term, *groups[h]):
                send_s[1, i, c] = piece.astype(bf16)
            rs_copy(1, i, h, partner).start()

        def pass_rows(i, h, rows):
            sel_s[i, h] = rows.astype(bf16)
            sel_copy(i, h).start()

        grad_s[length:] = mul(pick_of, grad_s[:length], FIRST).astype(bf16)
        every = grad_s[...]
        cross_start(1, lane_sum(grad_s[:length].astype(f32) * proj_s[...]))
        def far_part(h):
            term = partial(across, *groups[h], every)
            sel_copy(0, h).wait_recv()
            rows = term[length:] + sel_r[0, h].astype(f32)
            gain_far = gain_r[:, lanes_of(h)].astype(f32)
            rows_s[0, h] = (rstd * (gain_far * rows)).astype(bf16)

            @pl.when(section == 0)
            def _():
                for o in range(n_section - 1, -1, -1):
                    far_rows(h, o).start()

            rs_copy(1, 0, h, partner).wait_recv()
            for c, piece in pieces(term[:length], *groups[h]):
                send_s[1, 1, c] = (piece + recv_s[1, 0, c].astype(f32)).astype(bf16)

        def own_part(h, rows):
            at = lanes_of(h)
            sel_copy(1, h).wait_recv()
            rows = rstd * (gains[:, at] * (rows + sel_r[1, h].astype(f32)))
            rows_s[1, h] = (bases_s[:, at] + rows).astype(bf16)

            @pl.when(section == 0)
            def _():
                for o in range(1, n_section):
                    own_rows_copy(h, o).start()

        for h in range(len(groups)):
            term = partial(diag, *groups[h], every)
            pass_rows(0, h, term[length:])
            pass_on(0, h, term[:length])
        for h in range(len(groups)):
            far_part(h)
        for c in range(chunks):
            rs_copy(1, 1, c, across).start()
        term = partial(partner, *groups[0], every)
        pass_rows(1, 0, term[length:])
        pass_on(2, 0, term[:length])
        cross = cross_wait(1)
        inverse = rstd_lanes(1)
        terms = [partial(partner, *groups[h], every) for h in range(1, len(groups))]
        factor = as_column(inverse * inverse * inverse * (cross / depth))
        for c in range(chunks):
            at = slice(c * cw, (c + 1) * cw)
            below = g_s[1, me, c].astype(f32) - handed * upper_s[me, :, at].astype(f32)
            base_s[:, at] = below - x_s[1, :, at].astype(f32) * factor
        for h, term in enumerate(terms, 1):
            pass_rows(1, h, term[length:])
            pass_on(2, h, term[:length])
        for h in range(len(groups)):
            term = partial(me, *groups[h], every)
            if h == 0:
                bases_s[...] = mul(pick_of, base_s[...].astype(bf16), FIRST)
            term_s[:, lanes_of(h)] = term[:length]
            own_part(h, term[length:])

    def rstd_lanes(t):
        squares = square_s[t] + square_r[0, t] + square_r[1, t] + square_r[2, t]
        return lax.rsqrt(squares / depth + 1e-05)

    def d_normed(t, c):
        at = slice(c * cw, (c + 1) * cw)
        return term_s[:, at] + recv_s[t, 2, c].astype(f32) + recv_s[t, 1, c].astype(f32)

    def pick_first():
        rows = jnp.concatenate([out_s[0, c] for c in range(chunks)], axis=1)
        rows = mul(chosen(0).astype(bf16), rows, FIRST).astype(bf16)
        for h in range(len(groups)):
            picks[seq, 0, h] = rows[:, lanes_of(h)]
        for o in range(1, n_section):
            pick_spread(o).start()

    def picks_join(h, own):
        far_rows(h, 0).wait_recv()
        picks[seq, 1, h] = (own.astype(f32) + rows_r[0, h].astype(f32)).astype(bf16)
        for o in range(1, n_dp):
            pick_copy(picks.at[seq, 1, h], o).start()

    loads["wo0"].wait()
    d_attn = wo_part(0, me, 0, chunks)
    landed(g_s.at[0, partner], near_recv.at[0])
    loads["wo1"].wait()
    d_attn += wo_part(0, partner, 0, chunks)
    for c in range(chunks):
        forward(0, c)
        if c == 0:
            inputs_start()
            loads["wo2"].wait()
        d_attn += wo_part(0, across, c)
        if c > 0:
            landed(g_s.at[0, diag, c - 1], diag_recv.at[c - 1])
            if c == 1:
                loads["wo3"].wait()
            d_attn += wo_part(0, diag, c - 1)
    landed(g_s.at[0, diag, chunks - 1], diag_recv.at[chunks - 1])
    d_attn += wo_part(0, diag, chunks - 1)
    attn_s[...] = d_attn.astype(bf16)
    attention(0)
    scatter_first()
    loads["feat"].wait()
    for j in range(n_dp):
        for t in range(TICKS):
            cut_s[j, pl.ds(t * feat_s.shape[1], feat_s.shape[1]), :] = feat_s[
                t, :, j * own_rows : (j + 1) * own_rows
            ]
    feat_all[seq] = cut_s[seq]
    for o in range(1, n_dp):
        feat_copy(o).start()

    landed(square_r, R_SQUARE)
    loads["pos"].wait()
    rstd_s[...] = lax.dot_general(
        chosen(1), jnp.broadcast_to(as_column(rstd_lanes(1)), (length, LANES)), FIRST,
        precision=lax.Precision.HIGHEST, preferred_element_type=f32,
    )
    rstd = as_column(rstd_lanes(0))
    total = jnp.zeros((length, LANES), f32)
    landed(recv_s.at[0, 2], rs_recv.at[0, len(groups) + chunks])
    for c in range(chunks):
        rs_copy(0, 1, c, across).wait_recv()
        at = slice(c * cw, (c + 1) * cw)
        weighted = gains[:, at] * d_normed(0, c)
        passed = g_s[0, me, c].astype(f32) + rstd * weighted
        out_s[0, c] = passed.astype(bf16)

        @pl.when(section > 0)
        def _():
            if c in early:
                held_copy(c).start()
            else:
                held_far(c).start()
            if c == late[-1]:
                for b in late:
                    held_copy(b).start()

        term_s[:, at] = passed
        total += lane_sum(x_s[0, :, at].astype(f32) * weighted)

    cross_start(0, total)

    @pl.when(section == last)
    def _():
        filled(g_s.at[1, me], load_sem.at[3])
        for c in range(chunks):
            to_across(1, c).start()
            to_partner(1, c).start()
        project()

    def factor_make():
        rstd = rstd_lanes(0)
        factor_s[...] = rstd * rstd * rstd * (cross_wait(0) / depth)

    @pl.when(section > 0)
    def _():
        factor_make()
        factor_copy.start()

    def received(c):
        held_copy(c).wait_recv()
        if c not in direct:
            to_across(1, c).start()
        to_partner(1, c).start()

    @pl.when(section < last)
    def _():
        uppers_forward()
        project()
        uppers_wait()
        for c in early:
            received(c)

    pair = stacked(me, early[0], len(early))
    landed(g_s.at[1, partner, first_span], near_recv.at[1])
    pair += stacked(partner, early[0], len(early))

    for c in late:
        forward(1, c)
    pair += stacked(across, late[0], len(late))

    @pl.when(section == 0)
    def _():
        factor_make()
        factor = as_column(factor_s[...])
        for c in range(chunks):
            at = slice(c * cw, (c + 1) * cw)
            out_s[0, c] = (term_s[:, at] - x_s[0, :, at].astype(f32) * factor).astype(bf16)
        pick_first()

    landed(g_s.at[1, diag, later_span], diag_recv.at[chunks + 1])
    pair += stacked(diag, late[0], len(late))
    for c in late:

        @pl.when(section < last)
        def _():
            received(c)

    pair += stacked(me, late[0], len(late))
    for c in early:
        forward(1, c)
    pair += stacked(across, early[0], len(early))
    landed(g_s.at[1, partner, later_span], near_recv.at[2])
    pair += stacked(partner, late[0], len(late))

    @pl.when(section < last)
    def _():
        factor_copy.wait_recv()

    handed = as_column(factor_r[...])
    landed(g_s.at[1, diag, first_span], diag_recv.at[chunks])
    pair += stacked(diag, early[0], len(early))
    d_attn = pair[:length] - handed * pair[length:]
    attn_s[...] = d_attn.astype(bf16)

    @pl.when(section > 0)
    def _():
        pick_spread(0).wait_recv()

    for o in range(1, n_dp):
        pick_copy(picks.at[seq, 0], o).start()
    attention(1)
    gain_copy.wait_recv()
    scatter_last(handed)

    @pl.when(section == 0)
    def _():
        for h in range(len(groups)):
            picks_join(h, rows_s[1, h])

    @pl.when(section > 0)
    def _():
        for h in range(len(groups)):
            own_rows_copy(h, 0).wait_recv()
            picks_join(h, rows_r[1, h])

    rstd = as_column(rstd_lanes(1))
    landed(recv_s.at[1, 2], rs_recv.at[1, len(groups) + chunks])
    for c in range(chunks):
        rs_copy(1, 1, c, across).wait_recv()
        at = slice(c * cw, (c + 1) * cw)
        out_s[1, c] = (base_s[:, at] + rstd * (gains[:, at] * d_normed(1, c))).astype(bf16)

    for c in range(chunks):
        pending[0, 0, :, c * cw : (c + 1) * cw] = out_s[1, c]

    drain(g_s.at[0, pl.ds(0, 3)], S_FIRST)
    drain(g_s.at[1, pl.ds(0, 2)], S_NEAR)
    drain(g_s.at[1, 0, first_span], S_EARLY)
    drain(scaled_s.at[pl.ds(0, 3)], S_SCALED)
    drain(send_s, S_SUMS)
    drain(cross_r, S_CROSS)
    drain(square_r, S_SQUARE)
    drain(gain_s, S_GAIN)
    drain(sel_s, S_CHOSEN)

    @pl.when(section == last)
    def _():
        drain(g_s.at[1, 0, later_span], S_LATE)

    @pl.when(section < last)
    def _():
        drain(upper_s.at[pl.ds(0, 2)], S_UPPER_NEAR)

    @pl.when(section > 0)
    def _():
        drain(out_s.at[0], S_HELD)
        drain(g_s.at[1, 0, later_span], S_FAR)
        drain(upper_s.at[pl.ds(0, 2)], S_UPPER)
        drain(factor_s, S_FACTOR)

    @pl.when(section == 0)
    def _():
        sent = 3 * n_section - 2
        drain(picks.at[pl.ds(0, sent // 2)], S_ROWS)
        if sent % 2:
            drain(picks.at[0, 0], S_ROWS)

    others = pl.ds(0, n_dp - 1)
    drain(feat_all.at[others], S_FEAT)
    landed(feat_all.at[others], R_FEAT)
    drain(picks.at[others], S_PICK)
    landed(picks.at[others], R_PICK)


def project_kernel(bands, feat, picked, pending, out, pending_out, out_s, out_sem, pending_sem):
    handed = pltpu.make_async_copy(pending, pending_out, pending_sem)
    handed.start()
    band = out.shape[0] // bands
    lhs = feat[...].T
    rhs = jnp.concatenate(
        [picked[:, h].reshape(-1, picked.shape[3]) for h in range(picked.shape[1])], axis=1
    )
    copies = []
    for i in range(bands):
        rows = pl.ds(i * band, band)
        out_s[rows, :] = mul(lhs[i * band : (i + 1) * band], rhs, PLAIN).astype(out_s.dtype)
        copies.append(pltpu.make_async_copy(out_s.at[rows], out.at[rows], out_sem.at[i]))
        copies[-1].start()
    for copy in copies:
        copy.wait()
    handed.wait()


def shards(
    w_query, w_key, w_value, w_out, norm_gain, saved_input, saved_query, saved_key,
    saved_value, grad_in, fresh_grad, features, image_pos, chunks=4, direct=(2, 3), groups=((0, 2), (2, 2)), bands=5,
):
    n_section, n_dp, n_mp = (lax.axis_size(a) for a in ("section", "dp", "mp"))
    assert n_mp == 4
    length, width = grad_in.shape[2:]
    kw = saved_key.shape[4]
    kv_local = kw // HD
    group = width // kw
    images = features.shape[2]
    own_rows = features.shape[3] // n_dp
    halves = len(groups)
    f32, bf16 = jnp.float32, jnp.bfloat16
    vmem, dma = pltpu.VMEM, pltpu.SemaphoreType.DMA
    feat_all, picks, pending = pl.pallas_call(
        functools.partial(kernel, n_section, n_dp, n_mp, chunks, direct, groups),
        out_shape=(
            jax.ShapeDtypeStruct((n_dp, TICKS * images, own_rows), bf16),
            jax.ShapeDtypeStruct((n_dp, TICKS, halves, images, width // halves), bf16),
            jax.ShapeDtypeStruct((1, 1, length, width), bf16),
        ),
        in_specs=[pl.BlockSpec(memory_space=pltpu.HBM)] * 13,
        out_specs=(pl.BlockSpec(memory_space=pltpu.VMEM),) * 3,
        scratch_shapes=[
            vmem((n_mp, width, width + 2 * kw), bf16),
            vmem((n_mp, width, width), bf16),
            vmem((1, width), bf16),
            vmem((TICKS, length, width), bf16),
            vmem((TICKS, length, width), bf16),
            vmem((TICKS, length, kw), bf16),
            vmem((TICKS, length, kw), bf16),
            vmem((TICKS, n_mp, chunks, length, width // chunks), bf16),
            vmem((TICKS, images, features.shape[3]), bf16),
            vmem((n_dp, TICKS * images, own_rows), bf16),
            vmem((TICKS, images), jnp.int32),
            vmem((TICKS, kv_local, group * length, length), f32),
            vmem((TICKS, kv_local, group * length, HD), f32),
            vmem((TICKS, kv_local, length, group * length), bf16),
            vmem((length, width), bf16),
            vmem((length + images, width + 2 * kw), bf16),
            vmem((TICKS, chunks, length, width // chunks), bf16),
            vmem((TICKS, 3, chunks, length, width // chunks), bf16),
            vmem((TICKS, 3, chunks, length, width // chunks), bf16),
            vmem((length, width), f32),
            vmem((n_mp, length, width), bf16),
            vmem((n_mp, length, width), bf16),
            vmem((length, width + 2 * kw), f32),
            vmem((TICKS, 8, LANES), f32),
            vmem((TICKS, 3, 8, LANES), f32),
            vmem((TICKS, 8, LANES), f32),
            vmem((3, TICKS, 8, LANES), f32),
            vmem((8, LANES), f32),
            vmem((8, LANES), f32),
            vmem((1, width), bf16),
            vmem((2, halves, images, width // halves), bf16),
            vmem((2, halves, images, width // halves), bf16),
            vmem((length, width), f32),
            vmem((2, halves, images, width // halves), bf16),
            vmem((2, halves, images, width // halves), bf16),
            vmem((images, LANES), f32),
            vmem((images, width), f32),
            dma((9,)), dma((n_mp,)), dma((n_mp,)), dma((18,)),
            dma((TICKS, chunks)), dma((3,)), dma((chunks + 2,)),
            dma((3,)), dma((4,)), dma((TICKS, len(groups) + chunks + 1)), dma((TICKS,)),
            dma((6,)), dma((chunks,)), dma((2, halves)), dma((halves,)), dma((halves,)),
        ],
        compiler_params=pltpu.CompilerParams(
            collective_id=0, has_side_effects=True, vmem_limit_bytes=48 * 2**20
        ),
    )(
        *[
            pltpu.with_memory_space_constraint(a, pltpu.HBM)
            for a in (
                w_query, w_key, w_value, w_out, norm_gain, saved_input, saved_query, saved_key,
                saved_value, grad_in, fresh_grad, features, image_pos,
            )
        ]
    )
    return pl.pallas_call(
        functools.partial(project_kernel, bands),
        out_shape=(
            jax.ShapeDtypeStruct((own_rows, width), bf16),
            jax.ShapeDtypeStruct(pending.shape, bf16),
        ),
        in_specs=[pl.BlockSpec(memory_space=pltpu.VMEM)] * 3,
        out_specs=(pl.BlockSpec(memory_space=pltpu.HBM),) * 2,
        scratch_shapes=[
            vmem((own_rows, width), bf16), dma((bands,)), dma(()),
        ],
        compiler_params=pltpu.CompilerParams(vmem_limit_bytes=8 * 2**20),
    )(feat_all.reshape(-1, own_rows), picks.reshape((-1,) + picks.shape[2:]), pending)


def solution(mesh):
    in_specs = (
        P("section", None, "mp"),
        P("section", None, "mp"),
        P("section", None, "mp"),
        P("section", "mp", None),
        P("section", "mp"),
        P("section", None, "dp", None, "mp"),
        P("section", None, "dp", None, "mp"),
        P("section", None, "dp", None, "mp"),
        P("section", None, "dp", None, "mp"),
        P("section", "dp", None, "mp"),
        P(None, "dp", None, "mp"),
        P(None, "dp", None, "section"),
        P(None, "dp", None),
    )
    out_specs = (P(("section", "dp"), "mp"), P("section", "dp", None, "mp"))
    return jax.shard_map(shards, mesh=mesh, in_specs=in_specs, out_specs=out_specs, check_vma=False)
```

```python
import functools

import jax
import jax.numpy as jnp
from jax import lax
from jax.experimental import pallas as pl
from jax.experimental.pallas import tpu as pltpu
from jax.sharding import PartitionSpec as P

HD = 128
LANES = 128
TICKS = 2
MESH = pl.DeviceIdType.MESH
LAST = (((1,), (1,)), ((), ()))
FIRST = (((0,), (0,)), ((), ()))
PLAIN = (((1,), (0,)), ((), ()))


def mul(a, b, dims):
    return lax.dot_general(a, b, dims, preferred_element_type=jnp.float32)


def lane_sum(a):
    parts = [a[:, i : i + LANES] for i in range(0, a.shape[1], LANES)]
    return functools.reduce(lambda p, q: p + q, parts)


def kernel(
    n_section, n_dp, n_mp, chunks, direct, groups,
    wq, wk, wv, wo, gain, x, q, k, v, g_in, fresh, feat, pos,
    feat_all, picks, pending,
    w_s, wo_s, gain_s, x_s, q_s, k_s, v_s, g_s, feat_s, cut_s, pos_s,
    probs_s, mixed_s, turned_s, attn_s, grad_s, out_s, send_s, recv_s, term_s,
    scaled_s, upper_s, proj_s, cross_s, cross_r, square_s, square_r, factor_s, factor_r,
    gain_r, rows_s, rows_r, base_s, sel_s, sel_r, rstd_s, bases_s,
    load_sem, wo_sem, w_sem, out_sem, across_recv, near_recv, diag_recv,
    xg_recv, up_recv, rs_recv, cr_recv, row_recv, held_recv, sel_recv, far_recv, own_recv,
):
    section = lax.axis_index("section")
    seq = lax.axis_index("dp")
    me = lax.axis_index("mp")
    y, core = me // 2, me % 2
    partner = 2 * y + (1 - core)
    across = 2 * (1 - y) + core
    diag = 2 * (1 - y) + (1 - core)
    length = g_in.shape[2]
    width = g_in.shape[3]
    depth = width * n_mp
    kw = k.shape[4]
    kv_local = kw // HD
    group = q.shape[4] // kw
    scale = HD ** (-0.5)
    f32, bf16 = jnp.float32, jnp.bfloat16
    last = n_section - 1
    (
        S_FIRST, S_NEAR, S_EARLY, S_LATE, S_SCALED, S_UPPER, S_UPPER_NEAR, S_SUMS, S_CROSS,
        S_SQUARE, S_HELD, S_FAR, S_FEAT, S_PICK, S_ROWS, S_GAIN, S_FACTOR,
        S_CHOSEN,
    ) = (out_sem.at[i] for i in range(18))
    R_SQUARE, R_FACTOR, R_GAIN, R_SPREAD, R_FEAT, R_PICK = (row_recv.at[i] for i in range(6))
    early = [c for c in range(chunks) if c not in direct]
    late = [c for c in range(chunks) if c in direct]
    first_span, later_span = pl.ds(early[0], len(early)), pl.ds(late[0], len(late))

    def remote(src, dst, ssem, rsem, where):
        return pltpu.make_async_remote_copy(
            src_ref=src, dst_ref=dst, send_sem=ssem, recv_sem=rsem,
            device_id=where, device_id_type=MESH,
        )

    barrier = pltpu.get_barrier_semaphore()
    for b in (partner, across, diag):
        pl.semaphore_signal(barrier, inc=1, device_id={"mp": b}, device_id_type=MESH)
    for o in range(1, n_dp):
        pl.semaphore_signal(
            barrier, inc=1, device_id={"dp": (seq + o) % n_dp}, device_id_type=MESH
        )
    greets = n_mp - 1 + n_dp - 1 + n_section - 1
    for o in range(1, n_section):
        other = (section + o) % n_section
        pl.semaphore_signal(
            barrier, inc=1, device_id={"section": other}, device_id_type=MESH
        )
        pl.semaphore_signal(
            barrier, inc=1, device_id={"section": other, "mp": across}, device_id_type=MESH
        )
        greets += 1

    loads = {}

    def load(name, src, dst, sem):
        loads[name] = pltpu.make_async_copy(src, dst, sem)
        loads[name].start()

    cw = width // chunks
    spans = [pl.ds(c * cw, cw) for c in range(chunks)]
    for c in range(chunks):
        load(f"g{c}", g_in.at[0, 0, :, spans[c]], g_s.at[0, me, c], load_sem.at[0])
    load("gain", gain, gain_s, load_sem.at[2])
    load("x", x.at[0, :, 0], x_s, load_sem.at[1])
    load("q", q.at[0, :, 0], q_s, load_sem.at[4])
    load("k", k.at[0, :, 0], k_s, load_sem.at[5])
    load("v", v.at[0, :, 0], v_s, load_sem.at[6])
    load("feat", feat.at[:, 0], feat_s, load_sem.at[7])
    load("pos", pos.at[:, 0], pos_s, load_sem.at[8])

    def fresh_copy(c):
        return pltpu.make_async_copy(
            fresh.at[0, 0, :, spans[c]], g_s.at[1, me, c], load_sem.at[3]
        )

    @pl.when(section == last)
    def _():
        for c in range(chunks):
            fresh_copy(c).start()

    order = (me, partner, across, diag)
    for i, b in enumerate(order):
        columns = pl.ds(pl.multiple_of(b * width, width), width)
        load(f"wo{i}", wo.at[0, :, columns], wo_s.at[b], wo_sem.at[i])
    pl.semaphore_wait(barrier, greets)

    def block_copy(ref, ssem, rsem, where):
        return remote(ref, ref, ssem, rsem, {"mp": where})

    def drain(ref, sem):
        remote(ref, ref, sem, sem, {"mp": partner}).wait_send()

    def landed(ref, sem):
        remote(ref, ref, sem, sem, {"mp": partner}).wait_recv()

    def near_sem(t, c):
        return near_recv.at[0] if t == 0 else near_recv.at[2 if c in late else 1]

    def diag_sem(t, c):
        return diag_recv.at[c] if t == 0 else diag_recv.at[chunks + (1 if c in late else 0)]

    def to_across(t, c):
        ssem = S_FIRST if t == 0 else S_LATE if c in late else S_EARLY
        return block_copy(g_s.at[t, me, c], ssem, across_recv.at[t, c], across)

    def to_partner(t, c):
        ssem = S_FIRST if t == 0 else S_NEAR
        return block_copy(g_s.at[t, me, c], ssem, near_sem(t, c), partner)

    def forward(t, c):
        landed(g_s.at[t, across, c], across_recv.at[t, c])
        ssem = S_FIRST if t == 0 else S_NEAR
        block_copy(g_s.at[t, across, c], ssem, diag_sem(t, c), partner).start()

    def scaled_copy(slot, which, where):
        return block_copy(scaled_s.at[slot], S_SCALED, xg_recv.at[which], where)

    def upper_copy(far):
        where = {"section": section - 1}
        if far:
            where["mp"] = across
        return remote(x_s.at[0], upper_s.at[me], S_UPPER, up_recv.at[far], where)

    def upper_near(slot, which):
        return block_copy(upper_s.at[slot], S_UPPER_NEAR, up_recv.at[2 + which], partner)

    def filled(ref, sem):
        pltpu.make_async_copy(ref, ref, sem).wait()

    filled(g_s.at[0, me], load_sem.at[0])
    for c in range(chunks):
        to_across(0, c).start()
    for c in range(chunks):
        to_partner(0, c).start()
    for i, b in enumerate((diag, across, partner, me)):
        rows = pl.ds(pl.multiple_of(b * width, width), width)
        for name, src, low, size in (
            ("wq", wq, 0, width), ("wk", wk, width, kw), ("wv", wv, width + kw, kw)
        ):
            load(f"{name}{i}", src.at[0, rows], w_s.at[b, :, pl.ds(low, size)], w_sem.at[i])

    loads["x"].wait()
    loads["gain"].wait()
    gains = gain_s[...].astype(f32)
    scaled_s[me] = (x_s[1].astype(f32) * gains).astype(bf16)

    def inputs_start():
        @pl.when(section > 0)
        def _():
            upper_copy(1).start()
            upper_copy(0).start()

        gain_copy.start()
        scaled_copy(me, 1, across).start()
        scaled_copy(me, 0, partner).start()

    def row_lanes(total):
        padded = jnp.concatenate([total, jnp.zeros((LANES - length, LANES), f32)], axis=0)
        return jnp.broadcast_to(jnp.sum(padded.T, axis=0, keepdims=True), (8, LANES))

    def as_column(lanes):
        return jnp.broadcast_to(lanes[0:1], (LANES, LANES)).T[:length, 0:1]

    def square_copy(i, where):
        return remote(
            square_s, square_r.at[i], S_SQUARE, R_SQUARE, {"mp": where}
        )

    for t in range(TICKS):
        own = x_s[t].astype(f32)
        square_s[t] = row_lanes(lane_sum(own * own))
    for i, b in enumerate((partner, across, diag)):
        square_copy(i, b).start()

    own_rows = feat_s.shape[2] // n_dp
    def feat_copy(o):
        to = (seq + o) % n_dp
        return remote(
            cut_s.at[to], feat_all.at[seq], S_FEAT, R_FEAT, {"dp": to}
        )

    @pl.when(section == last)
    def _():
        upper_s[...] = jnp.zeros(upper_s.shape, bf16)
        factor_r[...] = jnp.zeros(factor_r.shape, f32)

    loads["q"].wait()
    loads["k"].wait()
    loads["v"].wait()

    def stack(a, g):
        return jnp.concatenate(
            [a[:, (g * group + j) * HD : (g * group + j + 1) * HD] for j in range(group)], axis=0
        )

    rows_at = lax.rem(
        lax.broadcasted_iota(jnp.int32, (group * length, length), 0), jnp.int32(length)
    )
    cols_at = lax.broadcasted_iota(jnp.int32, (group * length, length), 1)
    causal = cols_at <= rows_at

    def softmax(t):
        for g in range(kv_local):
            kg = k_s[t, :, g * HD : (g + 1) * HD]
            scores = mul(stack(q_s[t], g), kg, LAST) * scale
            scores = jnp.where(causal, scores, -1e30)
            expo = jnp.exp(scores - jnp.max(scores, -1, keepdims=True))
            probs = expo / jnp.sum(expo, -1, keepdims=True)
            probs_s[t, g] = probs
            vg = v_s[t, :, g * HD : (g + 1) * HD].astype(f32)
            mixed_s[t, g] = lax.dot_general(
                probs, vg, PLAIN, precision=lax.Precision.HIGHEST, preferred_element_type=f32
            )
            turned_s[t, g] = probs.astype(bf16).T

    for t in range(TICKS):
        softmax(t)

    def pick_copy(ref, o):
        return remote(ref, ref, S_PICK, R_PICK, {"dp": (seq + o) % n_dp})

    def pick_spread(o):
        ref = picks.at[seq, 0]
        return remote(ref, ref, S_ROWS, R_SPREAD, {"section": o})

    def far_rows(h, o):
        return remote(
            rows_s.at[0, h], rows_r.at[0, h], S_ROWS, far_recv.at[h],
            {"section": o, "mp": across},
        )

    def own_rows_copy(h, o):
        return remote(
            rows_s.at[1, h], rows_r.at[1, h], S_ROWS, own_recv.at[h], {"section": o}
        )

    def sel_copy(i, h):
        return remote(
            sel_s.at[i, h], sel_r.at[i, h], S_CHOSEN, sel_recv.at[i, h], {"mp": partner}
        )

    gain_copy = remote(gain_s, gain_r, S_GAIN, R_GAIN, {"mp": across})

    def chosen(t):
        at = lax.broadcasted_iota(jnp.int32, (length, pos_s.shape[1]), 0)
        return (at == pos_s[pl.ds(t, 1), :]).astype(f32)

    def rs_copy(t, i, h, where):
        part = pl.ds(h, 1) if i == 1 else pl.ds(*groups[h])
        rsem = rs_recv.at[t, (h, len(groups) + h, len(groups) + chunks)[i]]
        return remote(
            send_s.at[t, i, part], recv_s.at[t, i, part], S_SUMS, rsem, {"mp": where}
        )

    def cross_copy(t, i, where):
        return remote(
            cross_s.at[t], cross_r.at[t, i], S_CROSS, cr_recv.at[t], {"mp": where}
        )

    def cross_start(t, total):
        cross_s[t] = row_lanes(total)
        for i, b in enumerate((across, diag, partner)):
            cross_copy(t, i, b).start()

    def cross_wait(t):
        cross = cross_s[t]
        landed(cross_r.at[t], cr_recv.at[t])
        for i in range(n_mp - 1):
            cross += cross_r[t, i]
        return cross

    def held_copy(c):
        return remote(
            out_s.at[0, c], g_s.at[1, me, c], S_HELD, held_recv.at[c],
            {"section": section - 1},
        )

    def held_far(c):
        return remote(
            out_s.at[0, c], g_s.at[1, me, c], S_FAR, across_recv.at[1, c],
            {"section": section - 1, "mp": across},
        )

    factor_copy = remote(
        factor_s, factor_r, S_FACTOR, R_FACTOR, {"section": section - 1}
    )

    def wo_part(t, b, c, n=1):
        rows = [g_s[t, b, c + i] for i in range(n)]
        lhs = rows[0] if n == 1 else jnp.concatenate(rows, axis=1)
        return mul(lhs, wo_s[b, :, c * cw : (c + n) * cw], LAST)

    def project():
        scaled_copy(across, 1, partner).wait_recv()
        scaled_copy(across, 2, partner).start()
        scaled_copy(partner, 0, partner).wait_recv()
        total = mul(scaled_s[me], w_s[me], PLAIN)
        for b in (partner, across):
            total += mul(scaled_s[b], w_s[b], PLAIN)
        scaled_copy(diag, 2, partner).wait_recv()
        proj_s[...] = total + mul(scaled_s[diag], w_s[diag], PLAIN)

    def uppers_forward():
        upper_copy(1).wait_recv()
        upper_near(across, 1).start()
        upper_copy(0).wait_recv()
        upper_near(me, 0).start()

    def uppers_wait():
        upper_near(partner, 0).wait_recv()
        upper_near(diag, 1).wait_recv()

    def stacked(b, c, n):
        lhs = jnp.concatenate([g_s[1, b, c + i] for i in range(n)], axis=1)
        at = slice(c * cw, (c + n) * cw)
        both = jnp.concatenate([lhs, upper_s[b, :, at]], axis=0)
        return mul(both, wo_s[b, :, at], LAST)

    def attention(t):
        for g in range(kv_local):
            lanes = slice(g * HD, (g + 1) * HD)
            kg, vg = k_s[t, :, lanes], v_s[t, :, lanes]
            qg = stack(q_s[t], g)
            ag = stack(attn_s[...], g)
            probs = probs_s[t, g]
            d_probs = mul(ag, vg, LAST)
            inner = jnp.sum(ag.astype(f32) * mixed_s[t, g], -1, keepdims=True)
            d_scores = (probs * (d_probs - inner) * scale).astype(bf16)
            d_query = mul(d_scores, kg, PLAIN).astype(bf16)
            for j in range(group):
                grad_s[:length, (g * group + j) * HD : (g * group + j + 1) * HD] = d_query[
                    j * length : (j + 1) * length
                ]
            low = width + g * HD
            grad_s[:length, low : low + HD] = mul(d_scores, qg, FIRST).astype(bf16)
            grad_s[:length, low + kw : low + kw + HD] = mul(
                turned_s[t, g], ag, PLAIN
            ).astype(bf16)

    def partial(b, low, count, rows):
        return mul(rows, w_s[b, low * cw : (low + count) * cw], LAST)

    def pieces(term, low, count):
        return [(low + j, term[:, j * cw : (j + 1) * cw]) for j in range(count)]

    def weights_wait(t, i, b):
        if t == 0:
            filled(w_s.at[b], w_sem.at[i])

    def lanes_of(h):
        low, count = groups[h]
        return slice(low * cw, (low + count) * cw)

    def scatter_first():
        rows = grad_s[:length]
        weights_wait(0, 0, diag)
        for h in range(len(groups)):
            for c, term in pieces(partial(diag, *groups[h], rows), *groups[h]):
                send_s[0, 0, c] = term.astype(bf16)
            rs_copy(0, 0, h, partner).start()
        weights_wait(0, 1, across)
        for h in range(len(groups)):
            terms = pieces(partial(across, *groups[h], rows), *groups[h])
            rs_copy(0, 0, h, partner).wait_recv()
            for c, term in terms:
                send_s[0, 1, c] = (term + recv_s[0, 0, c].astype(f32)).astype(bf16)
            for c, _ in terms:
                rs_copy(0, 1, c, across).start()
        weights_wait(0, 2, partner)
        for c, term in pieces(partial(partner, 0, chunks, rows), 0, chunks):
            send_s[0, 2, c] = term.astype(bf16)
        for h in range(len(groups)):
            rs_copy(0, 2, h, partner).start()
        weights_wait(0, 3, me)
        term_s[...] = partial(me, 0, chunks, rows)

    def scatter_last(handed):
        pick_of = chosen(1).astype(bf16)
        rstd = rstd_s[:, 0:1]

        def pass_on(i, h, term):
            for c, piece in pieces(term, *groups[h]):
                send_s[1, i, c] = piece.astype(bf16)
            rs_copy(1, i, h, partner).start()

        def pass_rows(i, h, rows):
            sel_s[i, h] = rows.astype(bf16)
            sel_copy(i, h).start()

        grad_s[length:] = mul(pick_of, grad_s[:length], FIRST).astype(bf16)
        every = grad_s[...]
        cross_start(1, lane_sum(grad_s[:length].astype(f32) * proj_s[...]))
        def far_part(h):
            term = partial(across, *groups[h], every)
            sel_copy(0, h).wait_recv()
            rows = term[length:] + sel_r[0, h].astype(f32)
            gain_far = gain_r[:, lanes_of(h)].astype(f32)
            rows_s[0, h] = (rstd * (gain_far * rows)).astype(bf16)

            @pl.when(section == 0)
            def _():
                for o in range(n_section - 1, -1, -1):
                    far_rows(h, o).start()

            rs_copy(1, 0, h, partner).wait_recv()
            for c, piece in pieces(term[:length], *groups[h]):
                send_s[1, 1, c] = (piece + recv_s[1, 0, c].astype(f32)).astype(bf16)

        def own_part(h, rows):
            at = lanes_of(h)
            sel_copy(1, h).wait_recv()
            rows = rstd * (gains[:, at] * (rows + sel_r[1, h].astype(f32)))
            rows_s[1, h] = (bases_s[:, at] + rows).astype(bf16)

            @pl.when(section == 0)
            def _():
                for o in range(1, n_section):
                    own_rows_copy(h, o).start()

        for h in range(len(groups)):
            term = partial(diag, *groups[h], every)
            pass_rows(0, h, term[length:])
            pass_on(0, h, term[:length])
        for h in range(len(groups)):
            far_part(h)
        for c in range(chunks):
            rs_copy(1, 1, c, across).start()
        term = partial(partner, *groups[0], every)
        pass_rows(1, 0, term[length:])
        pass_on(2, 0, term[:length])
        cross = cross_wait(1)
        inverse = rstd_lanes(1)
        terms = [partial(partner, *groups[h], every) for h in range(1, len(groups))]
        factor = as_column(inverse * inverse * inverse * (cross / depth))
        for c in range(chunks):
            at = slice(c * cw, (c + 1) * cw)
            below = g_s[1, me, c].astype(f32) - handed * upper_s[me, :, at].astype(f32)
            base_s[:, at] = below - x_s[1, :, at].astype(f32) * factor
        for h, term in enumerate(terms, 1):
            pass_rows(1, h, term[length:])
            pass_on(2, h, term[:length])
        for h in range(len(groups)):
            term = partial(me, *groups[h], every)
            if h == 0:
                bases_s[...] = mul(pick_of, base_s[...].astype(bf16), FIRST)
            term_s[:, lanes_of(h)] = term[:length]
            own_part(h, term[length:])

    def rstd_lanes(t):
        squares = square_s[t] + square_r[0, t] + square_r[1, t] + square_r[2, t]
        return lax.rsqrt(squares / depth + 1e-05)

    def d_normed(t, c):
        at = slice(c * cw, (c + 1) * cw)
        return term_s[:, at] + recv_s[t, 2, c].astype(f32) + recv_s[t, 1, c].astype(f32)

    def pick_first():
        rows = jnp.concatenate([out_s[0, c] for c in range(chunks)], axis=1)
        rows = mul(chosen(0).astype(bf16), rows, FIRST).astype(bf16)
        for h in range(len(groups)):
            picks[seq, 0, h] = rows[:, lanes_of(h)]
        for o in range(1, n_section):
            pick_spread(o).start()

    def picks_join(h, own):
        far_rows(h, 0).wait_recv()
        picks[seq, 1, h] = (own.astype(f32) + rows_r[0, h].astype(f32)).astype(bf16)
        for o in range(1, n_dp):
            pick_copy(picks.at[seq, 1, h], o).start()

    loads["wo0"].wait()
    d_attn = wo_part(0, me, 0, chunks)
    landed(g_s.at[0, partner], near_recv.at[0])
    loads["wo1"].wait()
    d_attn += wo_part(0, partner, 0, chunks)
    for c in range(chunks):
        forward(0, c)
        if c == 1:
            inputs_start()
        if c == 0:
            loads["wo2"].wait()
        d_attn += wo_part(0, across, c)
        if c > 0:
            landed(g_s.at[0, diag, c - 1], diag_recv.at[c - 1])
            if c == 1:
                loads["wo3"].wait()
            d_attn += wo_part(0, diag, c - 1)
    landed(g_s.at[0, diag, chunks - 1], diag_recv.at[chunks - 1])
    d_attn += wo_part(0, diag, chunks - 1)
    attn_s[...] = d_attn.astype(bf16)
    attention(0)
    scatter_first()
    loads["feat"].wait()
    for j in range(n_dp):
        for t in range(TICKS):
            cut_s[j, pl.ds(t * feat_s.shape[1], feat_s.shape[1]), :] = feat_s[
                t, :, j * own_rows : (j + 1) * own_rows
            ]
    feat_all[seq] = cut_s[seq]
    for o in range(1, n_dp):
        feat_copy(o).start()

    landed(square_r, R_SQUARE)
    loads["pos"].wait()
    rstd_s[...] = lax.dot_general(
        chosen(1), jnp.broadcast_to(as_column(rstd_lanes(1)), (length, LANES)), FIRST,
        precision=lax.Precision.HIGHEST, preferred_element_type=f32,
    )
    rstd = as_column(rstd_lanes(0))
    total = jnp.zeros((length, LANES), f32)
    landed(recv_s.at[0, 2], rs_recv.at[0, len(groups) + chunks])
    for c in range(chunks):
        rs_copy(0, 1, c, across).wait_recv()
        at = slice(c * cw, (c + 1) * cw)
        weighted = gains[:, at] * d_normed(0, c)
        passed = g_s[0, me, c].astype(f32) + rstd * weighted
        out_s[0, c] = passed.astype(bf16)

        @pl.when(section > 0)
        def _():
            if c in early:
                held_copy(c).start()
            else:
                held_far(c).start()
            if c == late[-1]:
                for b in late:
                    held_copy(b).start()

        term_s[:, at] = passed
        total += lane_sum(x_s[0, :, at].astype(f32) * weighted)

    cross_start(0, total)

    @pl.when(section == last)
    def _():
        filled(g_s.at[1, me], load_sem.at[3])
        for c in range(chunks):
            to_across(1, c).start()
            to_partner(1, c).start()
        project()

    def factor_make():
        rstd = rstd_lanes(0)
        factor_s[...] = rstd * rstd * rstd * (cross_wait(0) / depth)

    @pl.when(section > 0)
    def _():
        factor_make()
        factor_copy.start()

    def received(c):
        held_copy(c).wait_recv()
        if c not in direct:
            to_across(1, c).start()
        to_partner(1, c).start()

    @pl.when(section < last)
    def _():
        uppers_forward()
        project()
        uppers_wait()
        for c in early:
            received(c)

    pair = stacked(me, early[0], len(early))
    landed(g_s.at[1, partner, first_span], near_recv.at[1])
    pair += stacked(partner, early[0], len(early))

    for c in late:
        forward(1, c)
    pair += stacked(across, late[0], len(late))

    @pl.when(section == 0)
    def _():
        factor_make()
        factor = as_column(factor_s[...])
        for c in range(chunks):
            at = slice(c * cw, (c + 1) * cw)
            out_s[0, c] = (term_s[:, at] - x_s[0, :, at].astype(f32) * factor).astype(bf16)
        pick_first()

    landed(g_s.at[1, diag, later_span], diag_recv.at[chunks + 1])
    pair += stacked(diag, late[0], len(late))
    for c in late:

        @pl.when(section < last)
        def _():
            received(c)

    pair += stacked(me, late[0], len(late))
    for c in early:
        forward(1, c)
    pair += stacked(across, early[0], len(early))
    landed(g_s.at[1, partner, later_span], near_recv.at[2])
    pair += stacked(partner, late[0], len(late))

    @pl.when(section < last)
    def _():
        factor_copy.wait_recv()

    handed = as_column(factor_r[...])
    landed(g_s.at[1, diag, first_span], diag_recv.at[chunks])
    pair += stacked(diag, early[0], len(early))
    d_attn = pair[:length] - handed * pair[length:]
    attn_s[...] = d_attn.astype(bf16)

    @pl.when(section > 0)
    def _():
        pick_spread(0).wait_recv()

    for o in range(1, n_dp):
        pick_copy(picks.at[seq, 0], o).start()
    attention(1)
    gain_copy.wait_recv()
    scatter_last(handed)

    @pl.when(section == 0)
    def _():
        for h in range(len(groups)):
            picks_join(h, rows_s[1, h])

    @pl.when(section > 0)
    def _():
        for h in range(len(groups)):
            own_rows_copy(h, 0).wait_recv()
            picks_join(h, rows_r[1, h])

    rstd = as_column(rstd_lanes(1))
    landed(recv_s.at[1, 2], rs_recv.at[1, len(groups) + chunks])
    for c in range(chunks):
        rs_copy(1, 1, c, across).wait_recv()
        at = slice(c * cw, (c + 1) * cw)
        out_s[1, c] = (base_s[:, at] + rstd * (gains[:, at] * d_normed(1, c))).astype(bf16)

    for c in range(chunks):
        pending[0, 0, :, c * cw : (c + 1) * cw] = out_s[1, c]

    drain(g_s.at[0, pl.ds(0, 3)], S_FIRST)
    drain(g_s.at[1, pl.ds(0, 2)], S_NEAR)
    drain(g_s.at[1, 0, first_span], S_EARLY)
    drain(scaled_s.at[pl.ds(0, 3)], S_SCALED)
    drain(send_s, S_SUMS)
    drain(cross_r, S_CROSS)
    drain(square_r, S_SQUARE)
    drain(gain_s, S_GAIN)
    drain(sel_s, S_CHOSEN)

    @pl.when(section == last)
    def _():
        drain(g_s.at[1, 0, later_span], S_LATE)

    @pl.when(section < last)
    def _():
        drain(upper_s.at[pl.ds(0, 2)], S_UPPER_NEAR)

    @pl.when(section > 0)
    def _():
        drain(out_s.at[0], S_HELD)
        drain(g_s.at[1, 0, later_span], S_FAR)
        drain(upper_s.at[pl.ds(0, 2)], S_UPPER)
        drain(factor_s, S_FACTOR)

    @pl.when(section == 0)
    def _():
        sent = 3 * n_section - 2
        drain(picks.at[pl.ds(0, sent // 2)], S_ROWS)
        if sent % 2:
            drain(picks.at[0, 0], S_ROWS)

    others = pl.ds(0, n_dp - 1)
    drain(feat_all.at[others], S_FEAT)
    landed(feat_all.at[others], R_FEAT)
    drain(picks.at[others], S_PICK)
    landed(picks.at[others], R_PICK)


def project_kernel(bands, feat, picked, pending, out, pending_out, out_s, out_sem, pending_sem):
    handed = pltpu.make_async_copy(pending, pending_out, pending_sem)
    handed.start()
    band = out.shape[0] // bands
    lhs = feat[...].T
    rhs = jnp.concatenate(
        [picked[:, h].reshape(-1, picked.shape[3]) for h in range(picked.shape[1])], axis=1
    )
    copies = []
    for i in range(bands):
        rows = pl.ds(i * band, band)
        out_s[rows, :] = mul(lhs[i * band : (i + 1) * band], rhs, PLAIN).astype(out_s.dtype)
        copies.append(pltpu.make_async_copy(out_s.at[rows], out.at[rows], out_sem.at[i]))
        copies[-1].start()
    for copy in copies:
        copy.wait()
    handed.wait()


def shards(
    w_query, w_key, w_value, w_out, norm_gain, saved_input, saved_query, saved_key,
    saved_value, grad_in, fresh_grad, features, image_pos, chunks=4, direct=(2, 3), groups=((0, 2), (2, 2)), bands=5,
):
    n_section, n_dp, n_mp = (lax.axis_size(a) for a in ("section", "dp", "mp"))
    assert n_mp == 4
    length, width = grad_in.shape[2:]
    kw = saved_key.shape[4]
    kv_local = kw // HD
    group = width // kw
    images = features.shape[2]
    own_rows = features.shape[3] // n_dp
    halves = len(groups)
    f32, bf16 = jnp.float32, jnp.bfloat16
    vmem, dma = pltpu.VMEM, pltpu.SemaphoreType.DMA
    feat_all, picks, pending = pl.pallas_call(
        functools.partial(kernel, n_section, n_dp, n_mp, chunks, direct, groups),
        out_shape=(
            jax.ShapeDtypeStruct((n_dp, TICKS * images, own_rows), bf16),
            jax.ShapeDtypeStruct((n_dp, TICKS, halves, images, width // halves), bf16),
            jax.ShapeDtypeStruct((1, 1, length, width), bf16),
        ),
        in_specs=[pl.BlockSpec(memory_space=pltpu.HBM)] * 13,
        out_specs=(pl.BlockSpec(memory_space=pltpu.VMEM),) * 3,
        scratch_shapes=[
            vmem((n_mp, width, width + 2 * kw), bf16),
            vmem((n_mp, width, width), bf16),
            vmem((1, width), bf16),
            vmem((TICKS, length, width), bf16),
            vmem((TICKS, length, width), bf16),
            vmem((TICKS, length, kw), bf16),
            vmem((TICKS, length, kw), bf16),
            vmem((TICKS, n_mp, chunks, length, width // chunks), bf16),
            vmem((TICKS, images, features.shape[3]), bf16),
            vmem((n_dp, TICKS * images, own_rows), bf16),
            vmem((TICKS, images), jnp.int32),
            vmem((TICKS, kv_local, group * length, length), f32),
            vmem((TICKS, kv_local, group * length, HD), f32),
            vmem((TICKS, kv_local, length, group * length), bf16),
            vmem((length, width), bf16),
            vmem((length + images, width + 2 * kw), bf16),
            vmem((TICKS, chunks, length, width // chunks), bf16),
            vmem((TICKS, 3, chunks, length, width // chunks), bf16),
            vmem((TICKS, 3, chunks, length, width // chunks), bf16),
            vmem((length, width), f32),
            vmem((n_mp, length, width), bf16),
            vmem((n_mp, length, width), bf16),
            vmem((length, width + 2 * kw), f32),
            vmem((TICKS, 8, LANES), f32),
            vmem((TICKS, 3, 8, LANES), f32),
            vmem((TICKS, 8, LANES), f32),
            vmem((3, TICKS, 8, LANES), f32),
            vmem((8, LANES), f32),
            vmem((8, LANES), f32),
            vmem((1, width), bf16),
            vmem((2, halves, images, width // halves), bf16),
            vmem((2, halves, images, width // halves), bf16),
            vmem((length, width), f32),
            vmem((2, halves, images, width // halves), bf16),
            vmem((2, halves, images, width // halves), bf16),
            vmem((images, LANES), f32),
            vmem((images, width), f32),
            dma((9,)), dma((n_mp,)), dma((n_mp,)), dma((18,)),
            dma((TICKS, chunks)), dma((3,)), dma((chunks + 2,)),
            dma((3,)), dma((4,)), dma((TICKS, len(groups) + chunks + 1)), dma((TICKS,)),
            dma((6,)), dma((chunks,)), dma((2, halves)), dma((halves,)), dma((halves,)),
        ],
        compiler_params=pltpu.CompilerParams(
            collective_id=0, has_side_effects=True, vmem_limit_bytes=48 * 2**20
        ),
    )(
        *[
            pltpu.with_memory_space_constraint(a, pltpu.HBM)
            for a in (
                w_query, w_key, w_value, w_out, norm_gain, saved_input, saved_query, saved_key,
                saved_value, grad_in, fresh_grad, features, image_pos,
            )
        ]
    )
    return pl.pallas_call(
        functools.partial(project_kernel, bands),
        out_shape=(
            jax.ShapeDtypeStruct((own_rows, width), bf16),
            jax.ShapeDtypeStruct(pending.shape, bf16),
        ),
        in_specs=[pl.BlockSpec(memory_space=pltpu.VMEM)] * 3,
        out_specs=(pl.BlockSpec(memory_space=pltpu.HBM),) * 2,
        scratch_shapes=[
            vmem((own_rows, width), bf16), dma((bands,)), dma(()),
        ],
        compiler_params=pltpu.CompilerParams(vmem_limit_bytes=8 * 2**20),
    )(feat_all.reshape(-1, own_rows), picks.reshape((-1,) + picks.shape[2:]), pending)


def solution(mesh):
    in_specs = (
        P("section", None, "mp"),
        P("section", None, "mp"),
        P("section", None, "mp"),
        P("section", "mp", None),
        P("section", "mp"),
        P("section", None, "dp", None, "mp"),
        P("section", None, "dp", None, "mp"),
        P("section", None, "dp", None, "mp"),
        P("section", None, "dp", None, "mp"),
        P("section", "dp", None, "mp"),
        P(None, "dp", None, "mp"),
        P(None, "dp", None, "section"),
        P(None, "dp", None),
    )
    out_specs = (P(("section", "dp"), "mp"), P("section", "dp", None, "mp"))
    return jax.shard_map(shards, mesh=mesh, in_specs=in_specs, out_specs=out_specs, check_vma=False)
```

```python
import functools

import jax
import jax.numpy as jnp
from jax import lax
from jax.experimental import pallas as pl
from jax.experimental.pallas import tpu as pltpu
from jax.sharding import PartitionSpec as P

HD = 128
LANES = 128
TICKS = 2
MESH = pl.DeviceIdType.MESH
LAST = (((1,), (1,)), ((), ()))
FIRST = (((0,), (0,)), ((), ()))
PLAIN = (((1,), (0,)), ((), ()))


def mul(a, b, dims):
    return lax.dot_general(a, b, dims, preferred_element_type=jnp.float32)


def lane_sum(a):
    parts = [a[:, i : i + LANES] for i in range(0, a.shape[1], LANES)]
    return functools.reduce(lambda p, q: p + q, parts)


def kernel(
    n_section, n_dp, n_mp, chunks, direct, groups,
    wq, wk, wv, wo, gain, x, q, k, v, g_in, fresh, feat, pos,
    feat_turned, picks, pending,
    w_s, wo_s, gain_s, x_s, q_s, k_s, v_s, g_s, feat_s, cut_s, pos_s,
    probs_s, mixed_s, turned_s, attn_s, grad_s, out_s, send_s, recv_s, term_s,
    scaled_s, upper_s, proj_s, cross_s, cross_r, square_s, square_r, factor_s, factor_r,
    gain_r, feat_all, rows_s, rows_r, base_s, sel_s, sel_r, rstd_s, bases_s,
    load_sem, wo_sem, w_sem, out_sem, across_recv, near_recv, diag_recv,
    xg_recv, up_recv, rs_recv, cr_recv, row_recv, held_recv, sel_recv, far_recv, own_recv,
):
    section = lax.axis_index("section")
    seq = lax.axis_index("dp")
    me = lax.axis_index("mp")
    y, core = me // 2, me % 2
    partner = 2 * y + (1 - core)
    across = 2 * (1 - y) + core
    diag = 2 * (1 - y) + (1 - core)
    length = g_in.shape[2]
    width = g_in.shape[3]
    depth = width * n_mp
    kw = k.shape[4]
    kv_local = kw // HD
    group = q.shape[4] // kw
    scale = HD ** (-0.5)
    f32, bf16 = jnp.float32, jnp.bfloat16
    last = n_section - 1
    (
        S_FIRST, S_NEAR, S_EARLY, S_LATE, S_SCALED, S_UPPER, S_UPPER_NEAR, S_SUMS, S_CROSS,
        S_SQUARE, S_HELD, S_FAR, S_FEAT, S_PICK, S_ROWS, S_GAIN, S_FACTOR,
        S_CHOSEN,
    ) = (out_sem.at[i] for i in range(18))
    R_SQUARE, R_FACTOR, R_GAIN, R_SPREAD, R_FEAT, R_PICK = (row_recv.at[i] for i in range(6))
    early = [c for c in range(chunks) if c not in direct]
    late = [c for c in range(chunks) if c in direct]
    first_span, later_span = pl.ds(early[0], len(early)), pl.ds(late[0], len(late))

    def remote(src, dst, ssem, rsem, where):
        return pltpu.make_async_remote_copy(
            src_ref=src, dst_ref=dst, send_sem=ssem, recv_sem=rsem,
            device_id=where, device_id_type=MESH,
        )

    barrier = pltpu.get_barrier_semaphore()
    for b in (partner, across, diag):
        pl.semaphore_signal(barrier, inc=1, device_id={"mp": b}, device_id_type=MESH)
    for o in range(1, n_dp):
        pl.semaphore_signal(
            barrier, inc=1, device_id={"dp": (seq + o) % n_dp}, device_id_type=MESH
        )
    greets = n_mp - 1 + n_dp - 1 + n_section - 1
    for o in range(1, n_section):
        other = (section + o) % n_section
        pl.semaphore_signal(
            barrier, inc=1, device_id={"section": other}, device_id_type=MESH
        )
        pl.semaphore_signal(
            barrier, inc=1, device_id={"section": other, "mp": across}, device_id_type=MESH
        )
        greets += 1

    loads = {}

    def load(name, src, dst, sem):
        loads[name] = pltpu.make_async_copy(src, dst, sem)
        loads[name].start()

    cw = width // chunks
    spans = [pl.ds(c * cw, cw) for c in range(chunks)]
    for c in range(chunks):
        load(f"g{c}", g_in.at[0, 0, :, spans[c]], g_s.at[0, me, c], load_sem.at[0])
    load("gain", gain, gain_s, load_sem.at[2])
    load("x", x.at[0, :, 0], x_s, load_sem.at[1])
    load("q", q.at[0, :, 0], q_s, load_sem.at[4])
    load("k", k.at[0, :, 0], k_s, load_sem.at[5])
    load("v", v.at[0, :, 0], v_s, load_sem.at[6])
    load("feat", feat.at[:, 0], feat_s, load_sem.at[7])
    load("pos", pos.at[:, 0], pos_s, load_sem.at[8])

    def fresh_copy(c):
        return pltpu.make_async_copy(
            fresh.at[0, 0, :, spans[c]], g_s.at[1, me, c], load_sem.at[3]
        )

    @pl.when(section == last)
    def _():
        for c in range(chunks):
            fresh_copy(c).start()

    order = (me, partner, across, diag)
    for i, b in enumerate(order):
        columns = pl.ds(pl.multiple_of(b * width, width), width)
        load(f"wo{i}", wo.at[0, :, columns], wo_s.at[b], wo_sem.at[i])
    pl.semaphore_wait(barrier, greets)

    def block_copy(ref, ssem, rsem, where):
        return remote(ref, ref, ssem, rsem, {"mp": where})

    def drain(ref, sem):
        remote(ref, ref, sem, sem, {"mp": partner}).wait_send()

    def landed(ref, sem):
        remote(ref, ref, sem, sem, {"mp": partner}).wait_recv()

    def near_sem(t, c):
        return near_recv.at[0] if t == 0 else near_recv.at[2 if c in late else 1]

    def diag_sem(t, c):
        return diag_recv.at[c] if t == 0 else diag_recv.at[chunks + (1 if c in late else 0)]

    def to_across(t, c):
        ssem = S_FIRST if t == 0 else S_LATE if c in late else S_EARLY
        return block_copy(g_s.at[t, me, c], ssem, across_recv.at[t, c], across)

    def to_partner(t, c):
        ssem = S_FIRST if t == 0 else S_NEAR
        return block_copy(g_s.at[t, me, c], ssem, near_sem(t, c), partner)

    def forward(t, c):
        landed(g_s.at[t, across, c], across_recv.at[t, c])
        ssem = S_FIRST if t == 0 else S_NEAR
        block_copy(g_s.at[t, across, c], ssem, diag_sem(t, c), partner).start()

    def scaled_copy(slot, which, where):
        return block_copy(scaled_s.at[slot], S_SCALED, xg_recv.at[which], where)

    def upper_copy(far):
        where = {"section": section - 1}
        if far:
            where["mp"] = across
        return remote(x_s.at[0], upper_s.at[me], S_UPPER, up_recv.at[far], where)

    def upper_near(slot, which):
        return block_copy(upper_s.at[slot], S_UPPER_NEAR, up_recv.at[2 + which], partner)

    def filled(ref, sem):
        pltpu.make_async_copy(ref, ref, sem).wait()

    filled(g_s.at[0, me], load_sem.at[0])
    for c in range(chunks):
        to_across(0, c).start()
    for c in range(chunks):
        to_partner(0, c).start()
    for i, b in enumerate((diag, across, partner, me)):
        rows = pl.ds(pl.multiple_of(b * width, width), width)
        for name, src, low, size in (
            ("wq", wq, 0, width), ("wk", wk, width, kw), ("wv", wv, width + kw, kw)
        ):
            load(f"{name}{i}", src.at[0, rows], w_s.at[b, :, pl.ds(low, size)], w_sem.at[i])

    loads["x"].wait()
    loads["gain"].wait()
    gains = gain_s[...].astype(f32)
    scaled_s[me] = (x_s[1].astype(f32) * gains).astype(bf16)

    def inputs_start():
        @pl.when(section > 0)
        def _():
            upper_copy(1).start()
            upper_copy(0).start()

        gain_copy.start()
        scaled_copy(me, 1, across).start()
        scaled_copy(me, 0, partner).start()

    def row_lanes(total):
        padded = jnp.concatenate([total, jnp.zeros((LANES - length, LANES), f32)], axis=0)
        return jnp.broadcast_to(jnp.sum(padded.T, axis=0, keepdims=True), (8, LANES))

    def as_column(lanes):
        return jnp.broadcast_to(lanes[0:1], (LANES, LANES)).T[:length, 0:1]

    def square_copy(i, where):
        return remote(
            square_s, square_r.at[i], S_SQUARE, R_SQUARE, {"mp": where}
        )

    for t in range(TICKS):
        own = x_s[t].astype(f32)
        square_s[t] = row_lanes(lane_sum(own * own))
    for i, b in enumerate((partner, across, diag)):
        square_copy(i, b).start()

    own_rows = feat_s.shape[2] // n_dp
    def feat_copy(o):
        to = (seq + o) % n_dp
        return remote(
            cut_s.at[to], feat_all.at[seq], S_FEAT, R_FEAT, {"dp": to}
        )

    @pl.when(section == last)
    def _():
        upper_s[...] = jnp.zeros(upper_s.shape, bf16)
        factor_r[...] = jnp.zeros(factor_r.shape, f32)

    loads["q"].wait()
    loads["k"].wait()
    loads["v"].wait()

    def stack(a, g):
        return jnp.concatenate(
            [a[:, (g * group + j) * HD : (g * group + j + 1) * HD] for j in range(group)], axis=0
        )

    rows_at = lax.rem(
        lax.broadcasted_iota(jnp.int32, (group * length, length), 0), jnp.int32(length)
    )
    cols_at = lax.broadcasted_iota(jnp.int32, (group * length, length), 1)
    causal = cols_at <= rows_at

    def softmax(t):
        for g in range(kv_local):
            kg = k_s[t, :, g * HD : (g + 1) * HD]
            scores = mul(stack(q_s[t], g), kg, LAST) * scale
            scores = jnp.where(causal, scores, -1e30)
            expo = jnp.exp(scores - jnp.max(scores, -1, keepdims=True))
            probs = expo / jnp.sum(expo, -1, keepdims=True)
            probs_s[t, g] = probs
            vg = v_s[t, :, g * HD : (g + 1) * HD].astype(f32)
            mixed_s[t, g] = lax.dot_general(
                probs, vg, PLAIN, precision=lax.Precision.HIGHEST, preferred_element_type=f32
            )
            turned_s[t, g] = probs.astype(bf16).T

    for t in range(TICKS):
        softmax(t)

    def pick_copy(ref, o):
        return remote(ref, ref, S_PICK, R_PICK, {"dp": (seq + o) % n_dp})

    def pick_spread(o):
        ref = picks.at[seq, 0]
        return remote(ref, ref, S_ROWS, R_SPREAD, {"section": o})

    def far_rows(h, o):
        return remote(
            rows_s.at[0, h], rows_r.at[0, h], S_ROWS, far_recv.at[h],
            {"section": o, "mp": across},
        )

    def own_rows_copy(h, o):
        return remote(
            rows_s.at[1, h], rows_r.at[1, h], S_ROWS, own_recv.at[h], {"section": o}
        )

    def sel_copy(i, h):
        return remote(
            sel_s.at[i, h], sel_r.at[i, h], S_CHOSEN, sel_recv.at[i, h], {"mp": partner}
        )

    gain_copy = remote(gain_s, gain_r, S_GAIN, R_GAIN, {"mp": across})

    def chosen(t):
        at = lax.broadcasted_iota(jnp.int32, (length, pos_s.shape[1]), 0)
        return (at == pos_s[pl.ds(t, 1), :]).astype(f32)

    def rs_copy(t, i, h, where):
        part = pl.ds(h, 1) if i == 1 else pl.ds(*groups[h])
        rsem = rs_recv.at[t, (h, len(groups) + h, len(groups) + chunks)[i]]
        return remote(
            send_s.at[t, i, part], recv_s.at[t, i, part], S_SUMS, rsem, {"mp": where}
        )

    def cross_copy(t, i, where):
        return remote(
            cross_s.at[t], cross_r.at[t, i], S_CROSS, cr_recv.at[t], {"mp": where}
        )

    def cross_start(t, total):
        cross_s[t] = row_lanes(total)
        for i, b in enumerate((across, diag, partner)):
            cross_copy(t, i, b).start()

    def cross_wait(t):
        cross = cross_s[t]
        landed(cross_r.at[t], cr_recv.at[t])
        for i in range(n_mp - 1):
            cross += cross_r[t, i]
        return cross

    def held_copy(c):
        return remote(
            out_s.at[0, c], g_s.at[1, me, c], S_HELD, held_recv.at[c],
            {"section": section - 1},
        )

    def held_far(c):
        return remote(
            out_s.at[0, c], g_s.at[1, me, c], S_FAR, across_recv.at[1, c],
            {"section": section - 1, "mp": across},
        )

    factor_copy = remote(
        factor_s, factor_r, S_FACTOR, R_FACTOR, {"section": section - 1}
    )

    def wo_part(t, b, c, n=1):
        rows = [g_s[t, b, c + i] for i in range(n)]
        lhs = rows[0] if n == 1 else jnp.concatenate(rows, axis=1)
        return mul(lhs, wo_s[b, :, c * cw : (c + n) * cw], LAST)

    def project():
        scaled_copy(across, 1, partner).wait_recv()
        scaled_copy(across, 2, partner).start()
        scaled_copy(partner, 0, partner).wait_recv()
        total = mul(scaled_s[me], w_s[me], PLAIN)
        for b in (partner, across):
            total += mul(scaled_s[b], w_s[b], PLAIN)
        scaled_copy(diag, 2, partner).wait_recv()
        proj_s[...] = total + mul(scaled_s[diag], w_s[diag], PLAIN)

    def uppers_forward():
        upper_copy(1).wait_recv()
        upper_near(across, 1).start()
        upper_copy(0).wait_recv()
        upper_near(me, 0).start()

    def uppers_wait():
        upper_near(partner, 0).wait_recv()
        upper_near(diag, 1).wait_recv()

    def stacked(b, c, n):
        lhs = jnp.concatenate([g_s[1, b, c + i] for i in range(n)], axis=1)
        at = slice(c * cw, (c + n) * cw)
        both = jnp.concatenate([lhs, upper_s[b, :, at]], axis=0)
        return mul(both, wo_s[b, :, at], LAST)

    def attention(t):
        for g in range(kv_local):
            lanes = slice(g * HD, (g + 1) * HD)
            kg, vg = k_s[t, :, lanes], v_s[t, :, lanes]
            qg = stack(q_s[t], g)
            ag = stack(attn_s[...], g)
            probs = probs_s[t, g]
            d_probs = mul(ag, vg, LAST)
            inner = jnp.sum(ag.astype(f32) * mixed_s[t, g], -1, keepdims=True)
            d_scores = (probs * (d_probs - inner) * scale).astype(bf16)
            d_query = mul(d_scores, kg, PLAIN).astype(bf16)
            for j in range(group):
                grad_s[:length, (g * group + j) * HD : (g * group + j + 1) * HD] = d_query[
                    j * length : (j + 1) * length
                ]
            low = width + g * HD
            grad_s[:length, low : low + HD] = mul(d_scores, qg, FIRST).astype(bf16)
            grad_s[:length, low + kw : low + kw + HD] = mul(
                turned_s[t, g], ag, PLAIN
            ).astype(bf16)

    def partial(b, low, count, rows):
        return mul(rows, w_s[b, low * cw : (low + count) * cw], LAST)

    def pieces(term, low, count):
        return [(low + j, term[:, j * cw : (j + 1) * cw]) for j in range(count)]

    def weights_wait(t, i, b):
        if t == 0:
            filled(w_s.at[b], w_sem.at[i])

    def lanes_of(h):
        low, count = groups[h]
        return slice(low * cw, (low + count) * cw)

    def scatter_first():
        rows = grad_s[:length]
        weights_wait(0, 0, diag)
        for h in range(len(groups)):
            for c, term in pieces(partial(diag, *groups[h], rows), *groups[h]):
                send_s[0, 0, c] = term.astype(bf16)
            rs_copy(0, 0, h, partner).start()
        weights_wait(0, 1, across)
        for h in range(len(groups)):
            terms = pieces(partial(across, *groups[h], rows), *groups[h])
            rs_copy(0, 0, h, partner).wait_recv()
            for c, term in terms:
                send_s[0, 1, c] = (term + recv_s[0, 0, c].astype(f32)).astype(bf16)
            for c, _ in terms:
                rs_copy(0, 1, c, across).start()
        weights_wait(0, 2, partner)
        for c, term in pieces(partial(partner, 0, chunks, rows), 0, chunks):
            send_s[0, 2, c] = term.astype(bf16)
        for h in range(len(groups)):
            rs_copy(0, 2, h, partner).start()
        weights_wait(0, 3, me)
        term_s[...] = partial(me, 0, chunks, rows)

    def scatter_last(handed):
        pick_of = chosen(1).astype(bf16)
        rstd = rstd_s[:, 0:1]

        def pass_on(i, h, term):
            for c, piece in pieces(term, *groups[h]):
                send_s[1, i, c] = piece.astype(bf16)
            rs_copy(1, i, h, partner).start()

        def pass_rows(i, h, rows):
            sel_s[i, h] = rows.astype(bf16)
            sel_copy(i, h).start()

        grad_s[length:] = mul(pick_of, grad_s[:length], FIRST).astype(bf16)
        every = grad_s[...]
        cross_start(1, lane_sum(grad_s[:length].astype(f32) * proj_s[...]))
        def far_part(h):
            term = partial(across, *groups[h], every)
            sel_copy(0, h).wait_recv()
            rows = term[length:] + sel_r[0, h].astype(f32)
            gain_far = gain_r[:, lanes_of(h)].astype(f32)
            rows_s[0, h] = (rstd * (gain_far * rows)).astype(bf16)

            @pl.when(section == 0)
            def _():
                for o in range(n_section - 1, -1, -1):
                    far_rows(h, o).start()

            rs_copy(1, 0, h, partner).wait_recv()
            for c, piece in pieces(term[:length], *groups[h]):
                send_s[1, 1, c] = (piece + recv_s[1, 0, c].astype(f32)).astype(bf16)

        def own_part(h, rows):
            at = lanes_of(h)
            sel_copy(1, h).wait_recv()
            rows = rstd * (gains[:, at] * (rows + sel_r[1, h].astype(f32)))
            rows_s[1, h] = (bases_s[:, at] + rows).astype(bf16)

            @pl.when(section == 0)
            def _():
                for o in range(1, n_section):
                    own_rows_copy(h, o).start()

        for h in range(len(groups)):
            term = partial(diag, *groups[h], every)
            pass_rows(0, h, term[length:])
            pass_on(0, h, term[:length])
        for h in range(len(groups)):
            far_part(h)
        for c in range(chunks):
            rs_copy(1, 1, c, across).start()
        term = partial(partner, *groups[0], every)
        pass_rows(1, 0, term[length:])
        pass_on(2, 0, term[:length])
        cross = cross_wait(1)
        inverse = rstd_lanes(1)
        terms = [partial(partner, *groups[h], every) for h in range(1, len(groups))]
        factor = as_column(inverse * inverse * inverse * (cross / depth))
        for c in range(chunks):
            at = slice(c * cw, (c + 1) * cw)
            below = g_s[1, me, c].astype(f32) - handed * upper_s[me, :, at].astype(f32)
            base_s[:, at] = below - x_s[1, :, at].astype(f32) * factor
        for h, term in enumerate(terms, 1):
            pass_rows(1, h, term[length:])
            pass_on(2, h, term[:length])
        for h in range(len(groups)):
            term = partial(me, *groups[h], every)
            if h == 0:
                bases_s[...] = mul(pick_of, base_s[...].astype(bf16), FIRST)
            term_s[:, lanes_of(h)] = term[:length]
            own_part(h, term[length:])

    def rstd_lanes(t):
        squares = square_s[t] + square_r[0, t] + square_r[1, t] + square_r[2, t]
        return lax.rsqrt(squares / depth + 1e-05)

    def d_normed(t, c):
        at = slice(c * cw, (c + 1) * cw)
        return term_s[:, at] + recv_s[t, 2, c].astype(f32) + recv_s[t, 1, c].astype(f32)

    def pick_first():
        rows = jnp.concatenate([out_s[0, c] for c in range(chunks)], axis=1)
        rows = mul(chosen(0).astype(bf16), rows, FIRST).astype(bf16)
        for h in range(len(groups)):
            picks[seq, 0, h] = rows[:, lanes_of(h)]
        for o in range(1, n_section):
            pick_spread(o).start()

    def picks_join(h, own):
        far_rows(h, 0).wait_recv()
        picks[seq, 1, h] = (own.astype(f32) + rows_r[0, h].astype(f32)).astype(bf16)
        for o in range(1, n_dp):
            pick_copy(picks.at[seq, 1, h], o).start()

    loads["wo0"].wait()
    d_attn = wo_part(0, me, 0, chunks)
    landed(g_s.at[0, partner], near_recv.at[0])
    loads["wo1"].wait()
    d_attn += wo_part(0, partner, 0, chunks)
    for c in range(chunks):
        forward(0, c)
        if c == 1:
            inputs_start()
        if c == 0:
            loads["wo2"].wait()
        d_attn += wo_part(0, across, c)
        if c > 0:
            landed(g_s.at[0, diag, c - 1], diag_recv.at[c - 1])
            if c == 1:
                loads["wo3"].wait()
            d_attn += wo_part(0, diag, c - 1)
    landed(g_s.at[0, diag, chunks - 1], diag_recv.at[chunks - 1])
    d_attn += wo_part(0, diag, chunks - 1)
    attn_s[...] = d_attn.astype(bf16)
    attention(0)
    scatter_first()
    loads["feat"].wait()
    for j in range(n_dp):
        for t in range(TICKS):
            cut_s[j, pl.ds(t * feat_s.shape[1], feat_s.shape[1]), :] = feat_s[
                t, :, j * own_rows : (j + 1) * own_rows
            ]
    feat_all[seq] = cut_s[seq]
    for o in range(1, n_dp):
        feat_copy(o).start()

    landed(square_r, R_SQUARE)
    loads["pos"].wait()
    rstd_s[...] = lax.dot_general(
        chosen(1), jnp.broadcast_to(as_column(rstd_lanes(1)), (length, LANES)), FIRST,
        precision=lax.Precision.HIGHEST, preferred_element_type=f32,
    )
    rstd = as_column(rstd_lanes(0))
    total = jnp.zeros((length, LANES), f32)
    landed(recv_s.at[0, 2], rs_recv.at[0, len(groups) + chunks])
    for c in range(chunks):
        rs_copy(0, 1, c, across).wait_recv()
        at = slice(c * cw, (c + 1) * cw)
        weighted = gains[:, at] * d_normed(0, c)
        passed = g_s[0, me, c].astype(f32) + rstd * weighted
        out_s[0, c] = passed.astype(bf16)

        @pl.when(section > 0)
        def _():
            if c in early:
                held_copy(c).start()
            else:
                held_far(c).start()
            if c == late[-1]:
                for b in late:
                    held_copy(b).start()

        term_s[:, at] = passed
        total += lane_sum(x_s[0, :, at].astype(f32) * weighted)

    cross_start(0, total)

    @pl.when(section == last)
    def _():
        filled(g_s.at[1, me], load_sem.at[3])
        for c in range(chunks):
            to_across(1, c).start()
            to_partner(1, c).start()
        project()

    def factor_make():
        rstd = rstd_lanes(0)
        factor_s[...] = rstd * rstd * rstd * (cross_wait(0) / depth)

    @pl.when(section > 0)
    def _():
        factor_make()
        factor_copy.start()

    def received(c):
        held_copy(c).wait_recv()
        if c not in direct:
            to_across(1, c).start()
        to_partner(1, c).start()

    @pl.when(section < last)
    def _():
        uppers_forward()
        project()
        uppers_wait()
        for c in early:
            received(c)

    pair = stacked(me, early[0], len(early))
    landed(g_s.at[1, partner, first_span], near_recv.at[1])
    pair += stacked(partner, early[0], len(early))

    for c in late:
        forward(1, c)
    pair += stacked(across, late[0], len(late))

    @pl.when(section == 0)
    def _():
        factor_make()
        factor = as_column(factor_s[...])
        for c in range(chunks):
            at = slice(c * cw, (c + 1) * cw)
            out_s[0, c] = (term_s[:, at] - x_s[0, :, at].astype(f32) * factor).astype(bf16)
        pick_first()

    landed(g_s.at[1, diag, later_span], diag_recv.at[chunks + 1])
    pair += stacked(diag, late[0], len(late))
    for c in late:

        @pl.when(section < last)
        def _():
            received(c)

    pair += stacked(me, late[0], len(late))
    for c in early:
        forward(1, c)
    pair += stacked(across, early[0], len(early))
    landed(g_s.at[1, partner, later_span], near_recv.at[2])
    pair += stacked(partner, late[0], len(late))

    @pl.when(section < last)
    def _():
        factor_copy.wait_recv()

    handed = as_column(factor_r[...])
    landed(g_s.at[1, diag, first_span], diag_recv.at[chunks])
    pair += stacked(diag, early[0], len(early))
    d_attn = pair[:length] - handed * pair[length:]
    attn_s[...] = d_attn.astype(bf16)

    @pl.when(section > 0)
    def _():
        pick_spread(0).wait_recv()

    for o in range(1, n_dp):
        pick_copy(picks.at[seq, 0], o).start()
    attention(1)
    gain_copy.wait_recv()
    scatter_last(handed)

    @pl.when(section == 0)
    def _():
        for h in range(len(groups)):
            picks_join(h, rows_s[1, h])

    @pl.when(section > 0)
    def _():
        for h in range(len(groups)):
            own_rows_copy(h, 0).wait_recv()
            picks_join(h, rows_r[1, h])

    landed(feat_all.at[pl.ds(0, n_dp - 1)], R_FEAT)
    feat_turned[...] = feat_all[...].reshape(-1, own_rows).T
    rstd = as_column(rstd_lanes(1))
    landed(recv_s.at[1, 2], rs_recv.at[1, len(groups) + chunks])
    for c in range(chunks):
        rs_copy(1, 1, c, across).wait_recv()
        at = slice(c * cw, (c + 1) * cw)
        out_s[1, c] = (base_s[:, at] + rstd * (gains[:, at] * d_normed(1, c))).astype(bf16)

    for c in range(chunks):
        pending[0, 0, :, c * cw : (c + 1) * cw] = out_s[1, c]

    drain(g_s.at[0, pl.ds(0, 3)], S_FIRST)
    drain(g_s.at[1, pl.ds(0, 2)], S_NEAR)
    drain(g_s.at[1, 0, first_span], S_EARLY)
    drain(scaled_s.at[pl.ds(0, 3)], S_SCALED)
    drain(send_s, S_SUMS)
    drain(cross_r, S_CROSS)
    drain(square_r, S_SQUARE)
    drain(gain_s, S_GAIN)
    drain(sel_s, S_CHOSEN)

    @pl.when(section == last)
    def _():
        drain(g_s.at[1, 0, later_span], S_LATE)

    @pl.when(section < last)
    def _():
        drain(upper_s.at[pl.ds(0, 2)], S_UPPER_NEAR)

    @pl.when(section > 0)
    def _():
        drain(out_s.at[0], S_HELD)
        drain(g_s.at[1, 0, later_span], S_FAR)
        drain(upper_s.at[pl.ds(0, 2)], S_UPPER)
        drain(factor_s, S_FACTOR)

    @pl.when(section == 0)
    def _():
        sent = 3 * n_section - 2
        drain(picks.at[pl.ds(0, sent // 2)], S_ROWS)
        if sent % 2:
            drain(picks.at[0, 0], S_ROWS)

    others = pl.ds(0, n_dp - 1)
    drain(feat_all.at[others], S_FEAT)
    drain(picks.at[others], S_PICK)
    landed(picks.at[others], R_PICK)


def project_kernel(bands, feat, picked, pending, out, pending_out, out_s, out_sem, pending_sem):
    handed = pltpu.make_async_copy(pending, pending_out, pending_sem)
    handed.start()
    band = out.shape[0] // bands
    rhs = jnp.concatenate(
        [picked[:, h].reshape(-1, picked.shape[3]) for h in range(picked.shape[1])], axis=1
    )
    copies = []
    for i in range(bands):
        rows = pl.ds(i * band, band)
        out_s[rows, :] = mul(feat[rows, :], rhs, PLAIN).astype(out_s.dtype)
        copies.append(pltpu.make_async_copy(out_s.at[rows], out.at[rows], out_sem.at[i]))
        copies[-1].start()
    for copy in copies:
        copy.wait()
    handed.wait()


def shards(
    w_query, w_key, w_value, w_out, norm_gain, saved_input, saved_query, saved_key,
    saved_value, grad_in, fresh_grad, features, image_pos, chunks=4, direct=(2, 3), groups=((0, 2), (2, 2)), bands=5,
):
    n_section, n_dp, n_mp = (lax.axis_size(a) for a in ("section", "dp", "mp"))
    assert n_mp == 4
    length, width = grad_in.shape[2:]
    kw = saved_key.shape[4]
    kv_local = kw // HD
    group = width // kw
    images = features.shape[2]
    own_rows = features.shape[3] // n_dp
    halves = len(groups)
    f32, bf16 = jnp.float32, jnp.bfloat16
    vmem, dma = pltpu.VMEM, pltpu.SemaphoreType.DMA
    feat_all, picks, pending = pl.pallas_call(
        functools.partial(kernel, n_section, n_dp, n_mp, chunks, direct, groups),
        out_shape=(
            jax.ShapeDtypeStruct((own_rows, n_dp * TICKS * images), bf16),
            jax.ShapeDtypeStruct((n_dp, TICKS, halves, images, width // halves), bf16),
            jax.ShapeDtypeStruct((1, 1, length, width), bf16),
        ),
        in_specs=[pl.BlockSpec(memory_space=pltpu.HBM)] * 13,
        out_specs=(pl.BlockSpec(memory_space=pltpu.VMEM),) * 3,
        scratch_shapes=[
            vmem((n_mp, width, width + 2 * kw), bf16),
            vmem((n_mp, width, width), bf16),
            vmem((1, width), bf16),
            vmem((TICKS, length, width), bf16),
            vmem((TICKS, length, width), bf16),
            vmem((TICKS, length, kw), bf16),
            vmem((TICKS, length, kw), bf16),
            vmem((TICKS, n_mp, chunks, length, width // chunks), bf16),
            vmem((TICKS, images, features.shape[3]), bf16),
            vmem((n_dp, TICKS * images, own_rows), bf16),
            vmem((TICKS, images), jnp.int32),
            vmem((TICKS, kv_local, group * length, length), f32),
            vmem((TICKS, kv_local, group * length, HD), f32),
            vmem((TICKS, kv_local, length, group * length), bf16),
            vmem((length, width), bf16),
            vmem((length + images, width + 2 * kw), bf16),
            vmem((TICKS, chunks, length, width // chunks), bf16),
            vmem((TICKS, 3, chunks, length, width // chunks), bf16),
            vmem((TICKS, 3, chunks, length, width // chunks), bf16),
            vmem((length, width), f32),
            vmem((n_mp, length, width), bf16),
            vmem((n_mp, length, width), bf16),
            vmem((length, width + 2 * kw), f32),
            vmem((TICKS, 8, LANES), f32),
            vmem((TICKS, 3, 8, LANES), f32),
            vmem((TICKS, 8, LANES), f32),
            vmem((3, TICKS, 8, LANES), f32),
            vmem((8, LANES), f32),
            vmem((8, LANES), f32),
            vmem((1, width), bf16),
            vmem((n_dp, TICKS * images, own_rows), bf16),
            vmem((2, halves, images, width // halves), bf16),
            vmem((2, halves, images, width // halves), bf16),
            vmem((length, width), f32),
            vmem((2, halves, images, width // halves), bf16),
            vmem((2, halves, images, width // halves), bf16),
            vmem((images, LANES), f32),
            vmem((images, width), f32),
            dma((9,)), dma((n_mp,)), dma((n_mp,)), dma((18,)),
            dma((TICKS, chunks)), dma((3,)), dma((chunks + 2,)),
            dma((3,)), dma((4,)), dma((TICKS, len(groups) + chunks + 1)), dma((TICKS,)),
            dma((6,)), dma((chunks,)), dma((2, halves)), dma((halves,)), dma((halves,)),
        ],
        compiler_params=pltpu.CompilerParams(
            collective_id=0, has_side_effects=True, vmem_limit_bytes=48 * 2**20
        ),
    )(
        *[
            pltpu.with_memory_space_constraint(a, pltpu.HBM)
            for a in (
                w_query, w_key, w_value, w_out, norm_gain, saved_input, saved_query, saved_key,
                saved_value, grad_in, fresh_grad, features, image_pos,
            )
        ]
    )
    return pl.pallas_call(
        functools.partial(project_kernel, bands),
        out_shape=(
            jax.ShapeDtypeStruct((own_rows, width), bf16),
            jax.ShapeDtypeStruct(pending.shape, bf16),
        ),
        in_specs=[pl.BlockSpec(memory_space=pltpu.VMEM)] * 3,
        out_specs=(pl.BlockSpec(memory_space=pltpu.HBM),) * 2,
        scratch_shapes=[
            vmem((own_rows, width), bf16), dma((bands,)), dma(()),
        ],
        compiler_params=pltpu.CompilerParams(vmem_limit_bytes=8 * 2**20),
    )(feat_all, picks.reshape((-1,) + picks.shape[2:]), pending)


def solution(mesh):
    in_specs = (
        P("section", None, "mp"),
        P("section", None, "mp"),
        P("section", None, "mp"),
        P("section", "mp", None),
        P("section", "mp"),
        P("section", None, "dp", None, "mp"),
        P("section", None, "dp", None, "mp"),
        P("section", None, "dp", None, "mp"),
        P("section", None, "dp", None, "mp"),
        P("section", "dp", None, "mp"),
        P(None, "dp", None, "mp"),
        P(None, "dp", None, "section"),
        P(None, "dp", None),
    )
    out_specs = (P(("section", "dp"), "mp"), P("section", "dp", None, "mp"))
    return jax.shard_map(shards, mesh=mesh, in_specs=in_specs, out_specs=out_specs, check_vma=False)
```
